32 devices in a mesh: dp: 16 (over z, y, x), tensor: 2 (over core).
Axes of the slice: x: 2, y: 2, z: 4, core: 2. Of those that a mesh axis runs over, the one named last changes fastest.
Arguments:
- tokens: bfloat16 [32, 512, 768], P('dp', 'tensor'), may hold values from -6 to 6
- lengths: int32 [32], P('dp'), may hold values from 1 to 512, 10240 in all
- key_mask: int32 [32, 512], P('dp'), may hold values 0 or 1
- order: int32 [16, 2], P('dp'), may hold values from 0 to 1, each once within a row
- query_key_value_weight: bfloat16 [3, 768, 768], P(None, 'dp', 'tensor'), may hold values from -0.21875 to 0.21875
- output_projection_weight: bfloat16 [768, 768], P('tensor', 'dp'), may hold values from -1.25 to 1.25
- up_projection_weight: bfloat16 [768, 3072], P('dp', 'tensor'), may hold values from -0.21875 to 0.21875
- down_projection_weight: bfloat16 [3072, 768], P('tensor', 'dp'), may hold values from -0.109375 to 0.109375
- embedding_projection_weight: bfloat16 [768, 128], P(('dp', 'tensor')), may hold values from -0.21875 to 0.21875
- gains: float32 [2, 768], P(None, ('dp', 'tensor')), may hold values from 0.5 to 1.5
- biases: float32 [6, 768], P(None, ('dp', 'tensor')), may hold values from -3 to 3
- up_bias_vector: float32 [3072], P(('dp', 'tensor')), may hold values from -3 to 3
- cotangent: float32 [32, 512, 128], P('dp', 'tensor'), may hold values from -6 to 6
Outputs:
- embeddings: float32 [32, 512, 128], P('dp', 'tensor')
- grad_tokens: float32 [32, 512, 768], P('dp', 'tensor')
- query_key_value_gradient: float32 [3, 768, 768], P(None, 'dp', 'tensor')
- output_gradient: float32 [768, 768], P('tensor', 'dp')
- up_gradient: float32 [768, 3072], P('dp', 'tensor')
- down_gradient: float32 [3072, 768], P('tensor', 'dp')
- grad_proj: float32 [768, 128], P(('dp', 'tensor'))
- grad_gains: float32 [2, 768], P(None, ('dp', 'tensor'))
- grad_biases: float32 [6, 768], P(None, ('dp', 'tensor'))
- grad_up_bias: float32 [3072], P(('dp', 'tensor'))
The draws below stay inside these ranges and needn't reach their ends.
Inputs may be any that keep to these rules, and one draw needn't show every extreme that they name: `lengths`: each sequence has 1 to 512 real tokens, and some sequence has exactly 512. `order`: each row is a permutation of 0 to 1.
All inputs are finite; a program needn't handle non-finite values. No bound on the sum of `lengths` or of `key_mask` on one device may be relied on, other than what follows from the above.
Results may differ from the reference program's by a relative error of at most 0.018.
Values may be sent and summed in bfloat16 or wider, within the bound.
No kernel may reach another device: no remote copies, remote signals or barrier semaphores. Data moves between devices by JAX's collectives and lax.ppermute only.
A program may use at most 192 MiB of HBM per device.

```python
import math
import jax
import jax.numpy as jnp
import numpy as np
from jax import lax

D = 768
HD = 64
FF = 3072
DE = 128
L = 512
SEQ_LOC = 2
NSEQ = 32


def plant(entries, key, low, largest):
    longest = entries.shape.index(max(entries.shape))
    spots = []
    for shift in (0, 1):
        where = [jax.random.randint(jax.random.fold_in(key, axis), (), 0, length) for axis, length in enumerate(entries.shape)]
        where[longest] = (where[longest] + shift) % entries.shape[longest]
        spots.append(tuple(where))
    return entries.at[spots[0]].set(low).at[spots[1]].set(largest)


def block_scale(key, dims, cuts, smallest, largest):
    loudness, own = 1.0, jax.random.fold_in(key, 6)
    for dim, shards_of in cuts:
        steps = jnp.exp(jax.random.uniform(jax.random.fold_in(own, dim), (shards_of,), jnp.float32, smallest / len(cuts), largest / len(cuts)))
        loudness = loudness * jnp.repeat(steps, dims[dim] // shards_of).reshape([-1 if axis == dim else 1 for axis in range(len(dims))])
    return loudness


def split_up(count, total, limit, slope):
    loads = [(1 << 20) // math.isqrt(rank ** slope) + 1 for rank in range(2, count + 1)]
    rest, counts = total - limit - (count - 1), [1] * (count - 1)
    while rest > 0:
        candidates = [i for i in range(count - 1) if counts[i] < limit]
        mass, budget = sum([loads[i] for i in candidates]), rest
        for i in candidates:
            more = min(limit - counts[i], max(1, budget * loads[i] // mass), rest)
            counts[i] = counts[i] + more
            rest = rest - more
    return np.array([limit] + counts)


def ragged_sizes(own_key, number_of, total, most, skew):
    if number_of == 2:
        one = jax.random.randint(own_key, (), max(1, total - most), min(most, total - 1) + 1)
        return jnp.stack([one, total - one])
    tallies = jnp.asarray(split_up(number_of, total, most, skew), jnp.int32)
    pairs = (number_of - 1) // 2
    source_of, sink = tallies[1:1 + 2 * pairs:2], tallies[2:2 + 2 * pairs:2]
    margin = jnp.minimum(source_of - 1, most - sink)
    moved = jax.random.randint(jax.random.fold_in(own_key, 1), (pairs,), 0, 1 << 20) % (margin + 1)
    tallies = tallies.at[1:1 + 2 * pairs:2].set(source_of - moved).at[2:2 + 2 * pairs:2].set(sink + moved)
    return tallies[jax.random.permutation(jax.random.fold_in(own_key, 2), number_of)]


def normal_values(own_key, shape, scale, limit, cuts=(), held_as=jnp.bfloat16):
    level = block_scale(own_key, shape, cuts, -0.22, 0.18) if cuts else 1.0
    values = jax.random.normal(own_key, shape, jnp.float32) * scale * level
    return jnp.minimum(jnp.maximum(values, -limit), limit).astype(held_as)


def setup_inputs(seed: int = 0) -> dict:
    key_list = jax.random.split(jax.random.key(seed), 14)
    tokens = normal_values(key_list[0], (NSEQ, L, D), 1.0, 6.0, ((0, 16), (1, 2)))
    lengths = ragged_sizes(key_list[1], NSEQ, NSEQ * L * 5 // 8, L, 1).astype(jnp.int32)
    key_mask = plant((jax.random.randint(key_list[2], (NSEQ, L), 0, 8) < 7).astype(jnp.int32), jax.random.fold_in(key_list[2], 1), 0, 1)
    order = jax.vmap(lambda own: jax.random.permutation(own, SEQ_LOC))(jax.random.split(key_list[3], (NSEQ // SEQ_LOC))).reshape((NSEQ // SEQ_LOC, SEQ_LOC)).astype(jnp.int32)
    query_key_value_weight = normal_values(key_list[4], (3, D, D), D ** -0.5, 0.21875, ((1, 16), (2, 2)))
    output_projection_weight = normal_values(key_list[5], (D, D), (D // 32) ** -0.5, 1.25, ((0, 2), (1, 16)))
    up_projection_weight = normal_values(key_list[6], (D, FF), D ** -0.5, 0.21875, ((0, 16), (1, 2)))
    down_projection_weight = normal_values(key_list[7], (FF, D), FF ** -0.5, 0.109375, ((0, 2), (1, 16)))
    embedding_projection_weight = normal_values(key_list[8], (D, DE), D ** -0.5, 0.21875, ((0, 32),))
    gains = jnp.clip(1.0 + 0.1 * jax.random.normal(key_list[9], (2, D), jnp.float32), 0.5, 1.5)
    biases = normal_values(key_list[10], (6, D), 0.5, 3.0, ((1, 32),), jnp.float32)
    up_bias_vector = normal_values(key_list[11], (FF,), 0.5, 3.0, ((0, 32),), jnp.float32)
    cotangent = normal_values(key_list[12], (NSEQ, L, DE), 1.0, 6.0, ((0, 16), (1, 2)), jnp.float32)
    return {"tokens": tokens, "lengths": lengths, "key_mask": key_mask, "order": order, "query_key_value_weight": query_key_value_weight, "output_projection_weight": output_projection_weight, "up_projection_weight": up_projection_weight, "down_projection_weight": down_projection_weight, "embedding_projection_weight": embedding_projection_weight, "gains": gains, "biases": biases, "up_bias_vector": up_bias_vector, "cotangent": cotangent}


@jax.custom_vjp
def reduced_precision(v):
    return lax.optimization_barrier(v.astype(jnp.bfloat16)).astype(jnp.float32)

@jax.custom_vjp
def reduced_backward(v):
    return v

def low_keep(v):
    return (reduced_precision(v), None)

def low_pass(kept, grad):
    return (grad,)

def back_keep(v):
    return (v, None)

def back_low(kept, grad):
    return (reduced_precision(grad),)
reduced_precision.defvjp(low_keep, low_pass)
reduced_backward.defvjp(back_keep, back_low)
highest = lax.Precision.HIGHEST

def matrix_multiply(left, right, form):
    return jnp.einsum(form, left, right, precision=highest)

def layer_norm(value, gain, shift):
    average = lax.optimization_barrier(jnp.mean(value, axis=-1, keepdims=True))
    centred = value - average
    spread = lax.optimization_barrier(jnp.mean(centred * centred, axis=-1, keepdims=True))
    return centred * lax.rsqrt(spread + 1e-12) * gain + shift

def forward(weights_all, token_row_block, seq_lens, key_marks):
    query_key_value_weight, output_projection_weight, up_projection_weight, down_projection_weight, embedding_projection_weight, gains, biases, up_bias_vector = weights_all
    count, length, width = token_row_block.shape
    places = jnp.arange(length, dtype=jnp.int32)
    key_ok = (places[None, :] < seq_lens[:, None]) & ((key_marks == 1) | (places[None, :] == 0))
    row_ok = (places[None, :] < seq_lens[:, None]).astype(jnp.float32)
    query_rows = reduced_backward(reduced_precision(matrix_multiply(token_row_block, query_key_value_weight[0], 'yig,gz->yiz') + biases[0]))
    key_head_rows = reduced_backward(reduced_precision(matrix_multiply(token_row_block, query_key_value_weight[1], 'yig,gz->yiz')))
    value_rows = reduced_backward(reduced_precision(matrix_multiply(token_row_block, query_key_value_weight[2], 'yig,gz->yiz') + biases[1]))
    head_shape = (count, length, width // HD, HD)
    scores = matrix_multiply(query_rows.reshape(head_shape), key_head_rows.reshape(head_shape), 'sqhd,skhd->shqk') * HD ** (-0.5)
    scores = reduced_backward(jnp.where(key_ok[:, None, None, :], scores, -1e+30))
    shifted = jnp.exp(scores - lax.optimization_barrier(jnp.max(scores, axis=-1, keepdims=True)))
    attn_probs = reduced_precision(shifted / lax.optimization_barrier(jnp.sum(shifted, axis=-1, keepdims=True)))
    attended_rows = matrix_multiply(attn_probs, value_rows.reshape(head_shape), 'shqk,skhd->sqhd').reshape(count, length, width)
    attended_rows = reduced_backward(reduced_precision(attended_rows))
    branch_output = reduced_backward(matrix_multiply(attended_rows, output_projection_weight, 'yig,gz->yiz') + biases[2])
    first_output = layer_norm(token_row_block + branch_output, gains[0], biases[3])
    hidden_input = reduced_backward(matrix_multiply(reduced_precision(first_output), up_projection_weight, 'pjb,bt->pjt') + up_bias_vector)
    hidden_activation = reduced_precision(jax.nn.gelu(hidden_input, approximate=False))
    feedforward_output = reduced_backward(matrix_multiply(hidden_activation, down_projection_weight, 'tpv,vn->tpn') + biases[4])
    second_output = layer_norm(first_output + feedforward_output, gains[1], biases[5])
    projected_rows = reduced_backward(matrix_multiply(reduced_precision(second_output), embedding_projection_weight, 'yig,gz->yiz'))
    unit_rows = projected_rows * lax.rsqrt(lax.optimization_barrier(jnp.sum(projected_rows * projected_rows, axis=-1, keepdims=True)) + 1e-06)
    return unit_rows * row_ok[:, :, None]

def reference(tokens, lengths, key_mask, order, query_key_value_weight, output_projection_weight, up_projection_weight, down_projection_weight, embedding_projection_weight, gains, biases, up_bias_vector, cotangent):
    weights_all = (query_key_value_weight.astype(jnp.float32), output_projection_weight.astype(jnp.float32), up_projection_weight.astype(jnp.float32), down_projection_weight.astype(jnp.float32), embedding_projection_weight.astype(jnp.float32), gains.astype(jnp.float32), biases.astype(jnp.float32), up_bias_vector.astype(jnp.float32))
    slots = jnp.arange(NSEQ, dtype=jnp.int32) // SEQ_LOC * SEQ_LOC + order.reshape(-1).astype(jnp.int32)
    back_cot = jnp.zeros(cotangent.shape, jnp.float32).at[slots].set(cotangent.astype(jnp.float32))
    group = math.gcd(NSEQ, max(1, 4096 // L))

    def grouped(array):
        return array.reshape((NSEQ // group, group) + array.shape[1:])

    def one_group(totals, pieces):
        token_row_block, seq_lens, key_marks, cot_rows = pieces

        def apply(weights_now, rows_now):
            return forward(weights_now, rows_now, seq_lens, key_marks)
        embedded, pull = jax.vjp(apply, weights_all, token_row_block.astype(jnp.float32))
        grads_now, grad_rows = pull(cot_rows)
        return (jax.tree.map(jnp.add, totals, grads_now), (embedded, grad_rows))
    zeros_all = jax.tree.map(jnp.zeros_like, weights_all)
    totals, outputs = lax.scan(one_group, zeros_all, (grouped(tokens), grouped(lengths), grouped(key_mask), grouped(back_cot)))
    embedded = outputs[0].reshape(NSEQ, L, DE)[slots]
    grad_tokens = outputs[1].reshape(NSEQ, L, D)
    return (embedded, grad_tokens, totals[0], totals[1], totals[2], totals[3], totals[4], totals[5], totals[6], totals[7])
```

```python
import jax
import jax.numpy as jnp
from jax import lax
from jax.sharding import PartitionSpec as P

HD = 64
F32 = jnp.float32
BF16 = jnp.bfloat16


def norm_rows(value, gain, shift):
    average = jnp.mean(value, axis=-1, keepdims=True)
    centred = value - average
    inverse = lax.rsqrt(jnp.mean(centred * centred, axis=-1, keepdims=True) + 1e-12)
    normed = centred * inverse
    return (normed * gain + shift, normed, inverse)


def norm_back(grad_rows, normed, inverse, gain):
    scaled = grad_rows * gain
    inside = (
        scaled
        - jnp.mean(scaled, axis=-1, keepdims=True)
        - normed * jnp.mean(scaled * normed, axis=-1, keepdims=True)
    )
    return (
        inside * inverse,
        jnp.sum(grad_rows * normed, axis=0),
        jnp.sum(grad_rows, axis=0),
    )


def exact_gelu(value):
    return jax.nn.gelu(value, approximate=False)


def dot(form, left, right):
    return jnp.einsum(form, left, right, preferred_element_type=F32)


def swap_cores(value):
    return lax.ppermute(value, "tensor", [(0, 1), (1, 0)])


class Exchange:
    def __init__(self, dp_size):
        self.size = dp_size
        self.outer = [bit for bit in range(dp_size.bit_length() - 2, 1, -1)]
        self.rank = lax.axis_index("dp")
        self.core = lax.axis_index("tensor")
        self.low = self.rank & 1
        self.high = (self.rank >> 1) & 1

    def flip(self, value, bit):
        pairs = [(i, i ^ (1 << bit)) for i in range(self.size)]
        return lax.ppermute(value, "dp", pairs)

    def flip_colored(self, value, first):
        pairs = []
        for i in range(self.size):
            for core in range(2):
                bit = 1 if (core == 0) == first else 0
                pairs.append((i * 2 + core, (i ^ (1 << bit)) * 2 + core))
        return lax.ppermute(value, ("dp", "tensor"), pairs)

    def spots(self):
        zero = self.core == 0
        high, low = self.high, self.low
        return (
            (high, low),
            (jnp.where(zero, 1 - high, high), jnp.where(zero, low, 1 - low)),
            (jnp.where(zero, high, 1 - high), jnp.where(zero, 1 - low, low)),
            (1 - high, 1 - low),
        )

    def gather(self, block):
        held = block[None]
        for bit in self.outer:
            came = self.flip(held, bit)
            mine = ((self.rank >> bit) & 1) == 0
            pair = jnp.where(
                mine, jnp.stack([held, came], axis=1), jnp.stack([came, held], axis=1)
            )
            held = pair.reshape((-1,) + block.shape)
        came = self.flip_colored(held, True)
        both = jnp.stack([held, came])
        more = self.flip_colored(both, False)
        whole = jnp.zeros((held.shape[0], 2, 2) + block.shape, block.dtype)
        for piece, (high, low) in zip((held, came, more[0], more[1]), self.spots()):
            whole = lax.dynamic_update_slice(whole, piece[:, None, None], (0, high, low, 0, 0))
        return whole.reshape((-1, block.shape[1]))

    def scatter(self, own, other):
        total = own + swap_cores(other.astype(BF16)).astype(F32)
        rows = own.shape[0] // self.size
        blocks = total.reshape((self.size // 4, 2, 2, rows, own.shape[1]))
        parts = []
        for high, low in self.spots():
            piece = lax.dynamic_slice(
                blocks, (0, high, low, 0, 0), (blocks.shape[0], 1, 1) + blocks.shape[3:]
            )
            parts.append(piece[:, 0, 0])
        sent = jnp.stack([parts[2], parts[3]]).astype(BF16)
        came = self.flip_colored(sent, False).astype(F32)
        held, sent = parts[0] + came[0], parts[1] + came[1]
        held = held + self.flip_colored(sent.astype(BF16), True).astype(F32)
        for bit in reversed(self.outer):
            pair = held.reshape((-1, 2) + held.shape[1:])
            mine = (self.rank >> bit) & 1
            sent = lax.dynamic_index_in_dim(pair, 1 - mine, 1, keepdims=False)
            kept = lax.dynamic_index_in_dim(pair, mine, 1, keepdims=False)
            held = kept + self.flip(sent.astype(BF16), bit).astype(F32)
        return held[0]


def three_parts(value):
    high = lax.reduce_precision(value, 8, 7)
    rest = value - high
    middle = lax.reduce_precision(rest, 8, 7)
    return (high.astype(BF16), middle.astype(BF16), (rest - middle).astype(BF16))


def body(
    tokens,
    lengths,
    key_mask,
    order,
    query_key_value_weight,
    output_projection_weight,
    up_projection_weight,
    down_projection_weight,
    embedding_projection_weight,
    gains,
    biases,
    up_bias_vector,
    cotangent,
):
    dp_size = lax.axis_size("dp")
    core = lax.axis_index("tensor")
    ways = Exchange(dp_size)
    half_len = tokens.shape[1]
    full_len = key_mask.shape[1]
    width = tokens.shape[2]
    cols = output_projection_weight.shape[0]
    rows = output_projection_weight.shape[1]
    ff_local = up_projection_weight.shape[1]
    heads = cols // HD
    scale_factor = HD ** (-0.5)

    chunk = gains.shape[1]
    emb_size = embedding_projection_weight.size
    vector = jnp.concatenate([gains.reshape(-1), biases.reshape(-1), up_bias_vector])
    pad_to = -(-vector.size // 128) * 128
    vector_size = vector.size
    vector = jnp.pad(vector, (0, pad_to - vector_size))
    flat = jnp.concatenate([embedding_projection_weight.reshape(-1), *three_parts(vector)])
    extra = -(-flat.size // (rows * 128)) * 128
    flat = jnp.pad(flat, (0, rows * extra - flat.size)).reshape(rows, extra)

    first_group = jnp.concatenate(
        [
            query_key_value_weight[0],
            query_key_value_weight[1],
            query_key_value_weight[2],
            output_projection_weight.T,
            flat,
        ],
        axis=1,
    )
    group_one = ways.gather(first_group)
    one = (group_one, swap_cores(group_one))
    group_two = ways.gather(up_projection_weight)
    up = (group_two, swap_cores(group_two))
    group_three = ways.gather(down_projection_weight.T)
    down = (group_three, swap_cores(group_three))

    mine = order[0, core]
    theirs = order[0, 1 - core]
    my_half = lax.dynamic_index_in_dim(tokens, mine, 0, keepdims=False)
    their_half = lax.dynamic_index_in_dim(tokens, theirs, 0, keepdims=False)
    came = swap_cores(their_half)

    def in_order(own, other):
        return jnp.where(
            core == 0, jnp.concatenate([own, other]), jnp.concatenate([other, own])
        )

    def half_of(value, which):
        return lax.dynamic_slice_in_dim(value, which * half_len, half_len)

    here = in_order(my_half, came)
    seq_len = lengths[mine]
    marks = lax.dynamic_index_in_dim(key_mask, mine, 0, keepdims=False)
    places = jnp.arange(full_len, dtype=jnp.int32)
    key_ok = (places < seq_len) & ((marks == 1) | (places == 0))
    row_ok = (places < seq_len).astype(F32)[:, None]

    wide = 3 * cols + cols
    small = [part[:, wide:].reshape(dp_size, rows * extra) for part in one]
    small = jnp.where(core == 0, jnp.stack(small, 1), jnp.stack(small[::-1], 1))
    small = small.reshape(dp_size * 2, rows * extra)
    projection_matrix = small[:, :emb_size].reshape(width, -1)
    thirds = small[:, emb_size : emb_size + 3 * pad_to].astype(F32)
    thirds = thirds.reshape(dp_size * 2, 3, pad_to)
    vectors = thirds[:, 0] + (thirds[:, 1] + thirds[:, 2])
    gain_full = jnp.moveaxis(vectors[:, : 2 * chunk].reshape(-1, 2, chunk), 1, 0).reshape(2, width)
    bias_full = jnp.moveaxis(
        vectors[:, 2 * chunk : 8 * chunk].reshape(-1, 6, chunk), 1, 0
    ).reshape(6, width)
    up_bias = vectors[:, 8 * chunk : vector_size].reshape(-1)

    sides = (core, 1 - core)
    qkv_w = [part[:, : 3 * cols] for part in one]
    out_w = [part[:, 3 * cols : wide] for part in one]

    qkv = []
    for side, weight in zip(sides, qkv_w):
        query_bias = lax.dynamic_slice_in_dim(bias_full[0], side * cols, cols)
        value_bias = lax.dynamic_slice_in_dim(bias_full[1], side * cols, cols)
        bias = jnp.concatenate([query_bias, jnp.zeros_like(query_bias), value_bias])
        qkv.append((dot("qm,mb->qb", here, weight) + bias).astype(BF16))

    def heads_of(index):
        return jnp.concatenate(
            [
                part[:, index * cols : (index + 1) * cols].reshape(full_len, heads, HD)
                for part in qkv
            ],
            axis=1,
        )

    query_rows, key_rows, value_rows = heads_of(0), heads_of(1), heads_of(2)

    def scores_of():
        raw = dot("qhd,khd->hqk", query_rows, key_rows) * scale_factor
        return jnp.where(key_ok[None, None, :], raw, -1e30)

    scores = scores_of()
    row_max = jnp.max(scores, axis=-1, keepdims=True)
    shifted = jnp.exp(scores - row_max)
    row_sum = jnp.sum(shifted, axis=-1, keepdims=True)
    log_total = row_max + jnp.log(row_sum)
    probs_low = (shifted / row_sum).astype(BF16)
    attended = dot("hqk,khd->qhd", probs_low, value_rows).astype(BF16)
    attended = attended.reshape(full_len, 2 * cols)
    halves = (attended[:, :cols], attended[:, cols:])
    branch = (
        dot("qc,oc->qo", halves[0], out_w[0])
        + dot("qc,oc->qo", halves[1], out_w[1])
        + bias_full[2]
    )
    first, normed_one, inverse_one = norm_rows(
        here.astype(F32) + branch, gain_full[0], bias_full[3]
    )
    first_low = first.astype(BF16)
    hidden, pulls = [], []
    for side, weight in zip(sides, up):
        bias = lax.dynamic_slice_in_dim(up_bias, side * ff_local, ff_local)
        active, pull = jax.vjp(exact_gelu, dot("qm,mf->qf", first_low, weight) + bias)
        hidden.append(active.astype(BF16))
        pulls.append(pull)
    ffn = (
        dot("qf,of->qo", hidden[0], down[0]) + dot("qf,of->qo", hidden[1], down[1]) + bias_full[4]
    )
    second, normed_two, inverse_two = norm_rows(first + ffn, gain_full[1], bias_full[5])
    second_low = second.astype(BF16)
    projected = dot("qm,me->qe", second_low, projection_matrix)
    row_scale = lax.rsqrt(jnp.sum(projected * projected, axis=-1, keepdims=True) + 1e-06)
    unit = projected * row_scale
    emb = unit * row_ok

    cot_mine = lax.dynamic_index_in_dim(cotangent, core, 0, keepdims=False)
    cot_other = lax.dynamic_index_in_dim(cotangent, 1 - core, 0, keepdims=False)
    cot = in_order(cot_mine, swap_cores(cot_other)) * row_ok
    g_proj = row_scale * (cot - unit * jnp.sum(unit * cot, axis=-1, keepdims=True))
    g_proj = g_proj.astype(BF16)
    proj_grad = dot("qm,qe->me", second_low, g_proj)
    g_second = dot("qe,me->qm", g_proj, projection_matrix)
    g_res_two, gain_two, shift_two = norm_back(g_second, normed_two, inverse_two, gain_full[1])
    g_ffn = g_res_two.astype(BF16)
    ffn_bias_grad = jnp.sum(g_ffn.astype(F32), axis=0)
    down_grads = [dot("qo,qf->of", g_ffn, part) for part in hidden]
    down_shard = ways.scatter(*down_grads)
    g_in = []
    for weight, pull in zip(down, pulls):
        g_in.append(pull(dot("qo,of->qf", g_ffn, weight))[0].astype(BF16))
    up_bias_grads = [jnp.sum(part.astype(F32), axis=0) for part in g_in]
    up_grads = [dot("qm,qf->mf", first_low, part) for part in g_in]
    up_shard = ways.scatter(*up_grads)
    g_first = (
        g_res_two + dot("qf,mf->qm", g_in[0], up[0]) + dot("qf,mf->qm", g_in[1], up[1])
    )
    g_res_one, gain_one, shift_one = norm_back(g_first, normed_one, inverse_one, gain_full[0])
    g_branch = g_res_one.astype(BF16)
    out_bias_grad = jnp.sum(g_branch.astype(F32), axis=0)
    out_grads = [dot("qo,qc->oc", g_branch, part) for part in halves]
    g_att = jnp.concatenate([dot("qo,oc->qc", g_branch, part) for part in out_w], axis=1)
    g_att = g_att.astype(BF16).reshape(full_len, 2 * heads, HD)
    attn_probs = jnp.exp(scores_of() - log_total)
    probs_low = attn_probs.astype(BF16)
    g_probs = dot("qhd,khd->hqk", g_att, value_rows)
    row_delta = jnp.sum(attn_probs * g_probs, axis=-1, keepdims=True)
    g_scores = (attn_probs * (g_probs - row_delta)).astype(BF16)
    g_query = (dot("hqk,khd->qhd", g_scores, key_rows) * scale_factor).astype(BF16)
    g_key = (dot("hqk,qhd->khd", g_scores, query_rows) * scale_factor).astype(BF16)
    g_value = dot("hqk,qhd->khd", probs_low, g_att).astype(BF16)
    flats = [part.reshape(full_len, 2 * cols) for part in (g_query, g_key, g_value)]
    g_qkv = [
        jnp.concatenate([part[:, h * cols : (h + 1) * cols] for part in flats], axis=1)
        for h in range(2)
    ]
    qkv_bias_grads = [jnp.sum(part.astype(F32), axis=0) for part in g_qkv]
    qkv_grads = [dot("qm,qb->mb", here, part) for part in g_qkv]
    g_here = (
        g_res_one + dot("qb,mb->qm", g_qkv[0], qkv_w[0]) + dot("qb,mb->qm", g_qkv[1], qkv_w[1])
    )

    def absolute(own, other):
        return jnp.where(
            core == 0, jnp.concatenate([own, other]), jnp.concatenate([other, own])
        )

    query_bias_grad = absolute(qkv_bias_grads[0][:cols], qkv_bias_grads[1][:cols])
    value_bias_grad = absolute(qkv_bias_grads[0][2 * cols :], qkv_bias_grads[1][2 * cols :])
    gain_grads = jnp.stack([gain_one, gain_two])
    bias_grads = jnp.stack(
        [query_bias_grad, value_bias_grad, out_bias_grad, shift_one, ffn_bias_grad, shift_two]
    )
    up_bias_grad = absolute(*up_bias_grads)
    small_grads = jnp.concatenate(
        [
            proj_grad.reshape(dp_size * 2, emb_size),
            jnp.moveaxis(gain_grads.reshape(2, -1, chunk), 0, 1).reshape(dp_size * 2, -1),
            jnp.moveaxis(bias_grads.reshape(6, -1, chunk), 0, 1).reshape(dp_size * 2, -1),
            up_bias_grad.reshape(dp_size * 2, -1),
        ],
        axis=1,
    )
    small_grads = jnp.pad(small_grads, ((0, 0), (0, rows * extra - small_grads.shape[1])))
    small_grads = small_grads.reshape(dp_size, 2, rows, extra)
    last = []
    for h, side in enumerate(sides):
        part = lax.dynamic_index_in_dim(small_grads, side, 1, keepdims=False)
        part = part.reshape(dp_size * rows, extra)
        last.append(jnp.concatenate([qkv_grads[h], out_grads[h], part], axis=1))
    one_shard = ways.scatter(*last)

    qkv_shard = jnp.stack([one_shard[:, i * cols : (i + 1) * cols] for i in range(3)])
    out_shard = one_shard[:, 3 * cols : wide].T
    tail = one_shard[:, wide:].reshape(-1)
    emb_shard = tail[:emb_size].reshape(embedding_projection_weight.shape)
    tail = tail[emb_size:]
    gain_shard = tail[: 2 * chunk].reshape(2, chunk)
    bias_shard = tail[2 * chunk : 8 * chunk].reshape(6, chunk)
    up_bias_shard = tail[8 * chunk : vector_size]

    def give_back(value, places_of):
        own = half_of(value, core)
        other = swap_cores(half_of(value, 1 - core))
        blank = jnp.zeros((2,) + own.shape, value.dtype)
        blank = lax.dynamic_update_slice(blank, own[None], (places_of[0], 0, 0))
        return lax.dynamic_update_slice(blank, other[None], (places_of[1], 0, 0))

    embeddings = give_back(emb, (core, 1 - core))
    grad_tokens = give_back(g_here, (mine, theirs))
    return (
        embeddings,
        grad_tokens,
        qkv_shard,
        out_shard,
        up_shard,
        down_shard.T,
        emb_shard,
        gain_shard,
        bias_shard,
        up_bias_shard,
    )


def solution(mesh):
    return jax.shard_map(
        body,
        mesh=mesh,
        in_specs=(
            P("dp", "tensor", None),
            P("dp"),
            P("dp", None),
            P("dp", None),
            P(None, "dp", "tensor"),
            P("tensor", "dp"),
            P("dp", "tensor"),
            P("tensor", "dp"),
            P(("dp", "tensor"), None),
            P(None, ("dp", "tensor")),
            P(None, ("dp", "tensor")),
            P(("dp", "tensor")),
            P("dp", "tensor", None),
        ),
        out_specs=(
            P("dp", "tensor", None),
            P("dp", "tensor", None),
            P(None, "dp", "tensor"),
            P("tensor", "dp"),
            P("dp", "tensor"),
            P("tensor", "dp"),
            P(("dp", "tensor"), None),
            P(None, ("dp", "tensor")),
            P(None, ("dp", "tensor")),
            P(("dp", "tensor")),
        ),
        check_vma=False,
    )
```

```python
import jax
import jax.numpy as jnp
import numpy as np
from jax import lax
from jax.experimental import pallas as pl
from jax.experimental.pallas import tpu as pltpu
from jax.sharding import PartitionSpec as P

HD = 64
LANES = 128
STRIP = 128
F32 = jnp.float32
BF16 = jnp.bfloat16
VMEM_LIMIT = 60 * 1024 * 1024


def nn(left, right):
    return lax.dot_general(left, right, (((1,), (0,)), ((), ())), preferred_element_type=F32)


def nt(left, right):
    return lax.dot_general(left, right, (((1,), (1,)), ((), ())), preferred_element_type=F32)


def swap_cores(value):
    return lax.ppermute(value, "tensor", [(0, 1), (1, 0)])


def after(value, *others):
    return lax.optimization_barrier((value, others))[0]


def together(*values):
    return lax.optimization_barrier(values)


def strips(count, size, step):
    def run(i, carry):
        step(pl.ds(pl.multiple_of(i * size, size), size))
        return carry

    lax.fori_loop(0, count // size, run, 0)


def call(body, outs, args, grid=None, in_specs=None, out_specs=None, scratch=(), flops=0):
    whole = pl.BlockSpec(memory_space=pltpu.VMEM)
    return pl.pallas_call(
        body,
        out_shape=outs,
        grid=grid or (),
        in_specs=in_specs or [whole] * len(args),
        out_specs=out_specs or jax.tree.map(lambda _: whole, outs),
        scratch_shapes=scratch,
        compiler_params=pltpu.CompilerParams(vmem_limit_bytes=VMEM_LIMIT),
        cost_estimate=pl.CostEstimate(flops=flops, bytes_accessed=1 << 20, transcendentals=0),
    )(*args)


def shaped(shape, dtype):
    return jax.ShapeDtypeStruct(shape, dtype)


ANY = pl.BlockSpec(memory_space=pl.ANY)
WHOLE = pl.BlockSpec(memory_space=pltpu.VMEM)


def load_weights(pieces, target, sems, first=0, last=None):
    quarter = target.shape[1] // 4
    columns = slice(first, last)
    copies = []
    for side in range(2):
        for place in range(4):
            source = place if side == 0 else (0, 2, 1, 3)[place]
            ref = pieces[2 * side + source // 2]
            copies.append(
                pltpu.make_async_copy(
                    ref.at[pl.ds((source % 2) * quarter, quarter), columns],
                    target.at[side, pl.ds(place * quarter, quarter)],
                    sems.at[side, place],
                )
            )
    for copy in copies:
        copy.start()
    return copies


def attention_kernel(
    x_ref, perm_ref, bias_ref, mask_ref, vec_ref, b0_ref, m0_ref, b1_ref, m1_ref, qkv_ref,
    lse_ref, att_ref, res_ref, first_ref, low_ref, lowt_ref, xt_ref, col_ref, rel_ref, w_ref, sems,
):
    cols = qkv_ref.shape[2] // 3
    tokens = x_ref.shape[0]
    copies = load_weights((b0_ref, m0_ref, b1_ref, m1_ref), w_ref, sems, 0, 4 * cols)
    rel_ref[...] = nn(x_ref[...], perm_ref[...]).astype(BF16)
    xt_ref[...] = rel_ref[...].T
    col_ref[...] = jnp.broadcast_to(mask_ref[...], (LANES, tokens)).T
    for copy in copies:
        copy.wait()
    for half in range(2):
        for part in range(3):
            span = slice(part * cols, (part + 1) * cols)
            made = nn(rel_ref[...], w_ref[half, :, span]) + bias_ref[half : half + 1, span]
            qkv_ref[half, :, span] = made.astype(BF16)
    lane = lax.broadcasted_iota(jnp.int32, (tokens, LANES), 1) < HD
    pairs = cols // LANES

    for half in range(2):

        def pair(i, carry, half=half):
            off = pl.multiple_of(i * LANES, LANES)
            query = qkv_ref[half, :, pl.ds(off, LANES)] * BF16(HD ** (-0.5))
            key = qkv_ref[half, :, pl.ds(pl.multiple_of(cols + off, LANES), LANES)]
            value = qkv_ref[half, :, pl.ds(pl.multiple_of(2 * cols + off, LANES), LANES)]
            value_t = value.T
            outs = []
            for head in range(2):
                kept = jnp.where(lane == (head == 0), key, jnp.zeros_like(key))
                scores = nt(kept, query)
                scores = scores + jnp.concatenate([col_ref[...]] * (tokens // LANES), axis=1)
                top = jnp.max(scores, axis=0, keepdims=True)
                shifted = jnp.exp(scores - top)
                total = jnp.sum(shifted, axis=0, keepdims=True)
                out = nn(value_t[head * HD : (head + 1) * HD], shifted.astype(BF16))
                outs.append(out / total)
                lse_ref[half, pl.ds(i * 2 + head, 1), :] = top + jnp.log(total)
            both = jnp.concatenate(outs, axis=0).T
            att_ref[half, :, pl.ds(off, LANES)] = both.astype(BF16)
            return carry

        lax.fori_loop(0, pairs, pair, 0)
    span = slice(3 * cols, 4 * cols)
    res_ref[...] = nt(att_ref[0], w_ref[0, :, span]) + nt(att_ref[1], w_ref[1, :, span])

    def norm(rows):
        value = res_ref[rows, :] + vec_ref[4:5, :] + rel_ref[rows, :].astype(F32)
        res_ref[rows, :] = value
        average = jnp.mean(value, axis=-1, keepdims=True)
        centred = value - average
        inverse = lax.rsqrt(jnp.mean(centred * centred, axis=-1, keepdims=True) + 1e-12)
        first = centred * inverse * vec_ref[0:1, :] + vec_ref[5:6, :]
        first_ref[rows, :] = first
        low_ref[rows, :] = first.astype(BF16)

    strips(tokens, STRIP, norm)
    lowt_ref[...] = low_ref[...].T


def attention_forward(x, perm, head_bias, mask, vec, pieces, cols):
    tokens, width = x.shape
    heads = cols // HD
    outs = (
        shaped((2, tokens, 3 * cols), BF16),
        shaped((2, heads, tokens), F32),
        shaped((2, tokens, cols), BF16),
        shaped((tokens, width), F32),
        shaped((tokens, width), F32),
        shaped((tokens, width), BF16),
        shaped((width, tokens), BF16),
        shaped((width, tokens), BF16),
    )
    return call(
        attention_kernel,
        outs,
        (x, perm, head_bias, mask, vec, *pieces),
        in_specs=[WHOLE] * 5 + [ANY] * 4,
        scratch=[
            pltpu.VMEM((tokens, LANES), F32),
            pltpu.VMEM((tokens, width), BF16),
            pltpu.VMEM((2, width, 4 * cols), BF16),
            pltpu.SemaphoreType.DMA((2, 4)),
        ],
        flops=8 * tokens * width * width,
    )


ERF = (0.254829592, -0.284496736, 1.421413741, -1.453152027, 1.061405429)


def gelu_pair(value):
    size = jnp.abs(value)
    bell = jnp.exp(-0.5 * value * value)
    t = 1.0 / (1.0 + (0.3275911 * 0.5**0.5) * size)
    poly = ERF[4]
    for term in ERF[3::-1]:
        poly = poly * t + term
    tail = 0.5 * poly * t * bell
    phi = jnp.where(value >= 0, 1.0 - tail, tail)
    return value * phi, phi + value * bell * 0.3989422804014327


def join_rows(both_ref, more_ref, target, swapped):
    quarter = target.shape[0] // 4
    for place in range(4):
        source = (0, 2, 1, 3)[place] if swapped else place
        ref = (both_ref, more_ref)[source // 2]
        rows = slice((source % 2) * quarter, (source % 2 + 1) * quarter)
        target[place * quarter : (place + 1) * quarter, :] = ref[rows, :]


def split_rows(value, keep_ref, send_ref, swapped):
    quarter = value.shape[0] // 4
    for place in range(4):
        source = (0, 2, 1, 3)[place] if swapped else place
        ref = (keep_ref, send_ref)[place // 2]
        rows = slice((place % 2) * quarter, (place % 2 + 1) * quarter)
        ref[rows, :] = value[source * quarter : (source + 1) * quarter, :]


def column_block(hidden):
    return 512 if hidden % 512 == 0 else hidden


def up_forward(low, pieces, bias, swapped):
    tokens, width = low.shape
    hidden = pieces[0].shape[1]
    block = column_block(hidden)

    def kernel(low_ref, both_ref, more_ref, bias_ref, hid_ref, slope_ref, acc_ref, w_ref):
        join_rows(both_ref, more_ref, w_ref, swapped)
        acc_ref[...] = nn(low_ref[...], w_ref[...])

        def act(rows):
            active, slope = gelu_pair(acc_ref[rows, :] + bias_ref[...])
            hid_ref[rows, :] = active.astype(BF16)
            slope_ref[rows, :] = slope.astype(BF16)

        strips(tokens, STRIP, act)

    outs = (shaped((tokens, hidden), BF16), shaped((tokens, hidden), BF16))
    chunk = pl.BlockSpec((tokens, block), lambda i: (0, i))
    piece = pl.BlockSpec((width // 2, block), lambda i: (0, i))
    return call(
        kernel,
        outs,
        (low, *pieces, bias),
        grid=(hidden // block,),
        in_specs=[
            pl.BlockSpec((tokens, width), lambda i: (0, 0)),
            piece,
            piece,
            pl.BlockSpec((1, block), lambda i: (0, i)),
        ],
        out_specs=(chunk, chunk),
        scratch=[pltpu.VMEM((tokens, block), F32), pltpu.VMEM((width, block), BF16)],
        flops=2 * tokens * width * hidden,
    )


def down_kernel(
    len_ref, h0_ref, h1_ref, first_ref, vec_ref, proj_ref, cot_ref, b0_ref, m0_ref, b1_ref, m1_ref, emb_ref,
    low_ref, lowt_ref, res_ref, pgrad_ref, sums_ref, ffn_ref, norm_ref, sec_ref, gp_ref,
    gs_ref, inv_ref, prj_ref, w_ref, sems,
):
    copies = load_weights((b0_ref, m0_ref, b1_ref, m1_ref), w_ref, sems)
    tokens = first_ref.shape[0]
    length = len_ref[0]
    for copy in copies:
        copy.wait()
    ffn_ref[...] = nt(h0_ref[...], w_ref[0]) + nt(h1_ref[...], w_ref[1])

    def norm(rows):
        value = first_ref[rows, :] + ffn_ref[rows, :] + vec_ref[6:7, :]
        average = jnp.mean(value, axis=-1, keepdims=True)
        centred = value - average
        inverse = lax.rsqrt(jnp.mean(centred * centred, axis=-1, keepdims=True) + 1e-12)
        normed = centred * inverse
        norm_ref[rows, :] = normed
        inv_ref[rows, :] = jnp.broadcast_to(inverse, (STRIP, LANES))
        sec_ref[rows, :] = (normed * vec_ref[1:2, :] + vec_ref[7:8, :]).astype(BF16)

    strips(tokens, STRIP, norm)
    prj_ref[...] = nn(sec_ref[...], proj_ref[...])

    def embed(rows):
        projected = prj_ref[rows, :]
        valid = rows.start + lax.broadcasted_iota(jnp.int32, projected.shape, 0) < length
        valid = valid.astype(F32)
        scale = lax.rsqrt(jnp.sum(projected * projected, axis=-1, keepdims=True) + 1e-06)
        unit = projected * scale
        emb_ref[rows, :] = unit * valid
        cot = cot_ref[rows, :] * valid
        back = scale * (cot - unit * jnp.sum(unit * cot, axis=-1, keepdims=True))
        gp_ref[rows, :] = back.astype(BF16)

    strips(tokens, STRIP, embed)
    pgrad_ref[...] = nn(sec_ref[...].T, gp_ref[...])
    gs_ref[...] = nt(gp_ref[...], proj_ref[...])
    sums_ref[...] = jnp.zeros_like(sums_ref)

    def back(rows):
        grad = gs_ref[rows, :]
        normed = norm_ref[rows, :]
        scaled = grad * vec_ref[1:2, :]
        inside = (
            scaled
            - jnp.mean(scaled, axis=-1, keepdims=True)
            - normed * jnp.mean(scaled * normed, axis=-1, keepdims=True)
        )
        value = inside * inv_ref[rows, 0:1]
        low = value.astype(BF16)
        res_ref[rows, :] = value
        low_ref[rows, :] = low
        fold = lambda v: jnp.sum(v.reshape(STRIP // 8, 8, v.shape[1]), axis=0)
        sums_ref[0:8, :] += fold(grad * normed)
        sums_ref[8:16, :] += fold(grad)
        sums_ref[16:24, :] += fold(low.astype(F32))

    strips(tokens, STRIP, back)
    lowt_ref[...] = low_ref[...].T


def down_both(length, hidden, pieces, first, vec, proj, cot):
    tokens, width = first.shape
    embed = proj.shape[1]
    outs = (
        shaped((tokens, embed), F32),
        shaped((tokens, width), BF16),
        shaped((width, tokens), BF16),
        shaped((tokens, width), F32),
        shaped((width, embed), F32),
        shaped((24, width), F32),
    )
    args = (length, *hidden, first, vec, proj, cot, *pieces)
    return call(
        down_kernel,
        outs,
        args,
        in_specs=[pl.BlockSpec(memory_space=pltpu.SMEM)] + [WHOLE] * 6 + [ANY] * 4,
        scratch=[
            pltpu.VMEM((tokens, width), F32),
            pltpu.VMEM((tokens, width), F32),
            pltpu.VMEM((tokens, width), BF16),
            pltpu.VMEM((tokens, embed), BF16),
            pltpu.VMEM((tokens, width), F32),
            pltpu.VMEM((tokens, LANES), F32),
            pltpu.VMEM((tokens, embed), F32),
            pltpu.VMEM((2, width, hidden[0].shape[1]), BF16),
            pltpu.SemaphoreType.DMA((2, 4)),
        ],
        flops=2 * tokens * width * hidden[0].shape[1] * 2,
    )


def down_grad(g_low_t, hid, swapped):
    width, tokens = g_low_t.shape
    hidden = hid.shape[1]
    block = column_block(hidden)

    def kernel(gt_ref, hid_ref, keep_ref, send_ref):
        split_rows(nn(gt_ref[...], hid_ref[...]).astype(BF16), keep_ref, send_ref, swapped)

    piece = pl.BlockSpec((width // 2, block), lambda i: (0, i))
    out = shaped((width // 2, hidden), BF16)
    return call(
        kernel,
        (out, out),
        (g_low_t, hid),
        grid=(hidden // block,),
        in_specs=[
            pl.BlockSpec((width, tokens), lambda i: (0, 0)),
            pl.BlockSpec((tokens, block), lambda i: (0, i)),
        ],
        out_specs=(piece, piece),
        flops=2 * tokens * width * hidden,
    )


def up_grad(g_low, low_t, slope, down, up, start, swapped):
    tokens, width = g_low.shape
    hidden = slope.shape[1]
    block = column_block(hidden)

    def kernel(
        g_ref, lowt_ref, slope_ref, db_ref, dm_ref, ub_ref, um_ref, start_ref, keep_ref, send_ref,
        bias_ref, first_ref, gh_ref, gin_ref, wd_ref, wu_ref,
    ):
        join_rows(db_ref, dm_ref, wd_ref, swapped)
        join_rows(ub_ref, um_ref, wu_ref, swapped)
        gh_ref[...] = nn(g_ref[...], wd_ref[...])
        bias_ref[...] = jnp.zeros_like(bias_ref)

        def act(rows):
            grad = (gh_ref[rows, :] * slope_ref[rows, :].astype(F32)).astype(BF16)
            gin_ref[rows, :] = grad
            wide = grad.astype(F32)
            bias_ref[...] += jnp.sum(wide.reshape(STRIP // 8, 8, wide.shape[1]), axis=0)

        strips(tokens, STRIP, act)
        split_rows(nn(lowt_ref[...], gin_ref[...]).astype(BF16), keep_ref, send_ref, swapped)
        part = nt(gin_ref[...], wu_ref[...])

        @pl.when(pl.program_id(0) == 0)
        def _():
            first_ref[...] = start_ref[...] + part

        @pl.when(pl.program_id(0) > 0)
        def _():
            first_ref[...] += part

    row = pl.BlockSpec((tokens, width), lambda i: (0, 0))
    turned = pl.BlockSpec((width, tokens), lambda i: (0, 0))
    act = pl.BlockSpec((tokens, block), lambda i: (0, i))
    piece = pl.BlockSpec((width // 2, block), lambda i: (0, i))
    out = shaped((width // 2, hidden), BF16)
    return call(
        kernel,
        (out, out, shaped((8, hidden), F32), shaped((tokens, width), F32)),
        (g_low, low_t, slope, *down, *up, start),
        grid=(hidden // block,),
        in_specs=[row, turned, act, piece, piece, piece, piece, row],
        out_specs=(piece, piece, pl.BlockSpec((8, block), lambda i: (0, i)), row),
        scratch=[
            pltpu.VMEM((tokens, block), F32),
            pltpu.VMEM((tokens, block), BF16),
            pltpu.VMEM((width, block), BF16),
            pltpu.VMEM((width, block), BF16),
        ],
        flops=6 * tokens * width * hidden,
    )


def branch_kernel(
    gf_ref, res_ref, vec_ref, att_ref, qkv_ref, lse_ref, mask_ref, b0_ref, m0_ref, b1_ref, m1_ref,
    gres_ref, gqkv_ref, sums_ref, low_ref, gatt_ref, col_ref, w_ref, sems,
):
    copies = load_weights(
        (b0_ref, m0_ref, b1_ref, m1_ref), w_ref, sems, 3 * att_ref.shape[2], 4 * att_ref.shape[2]
    )
    tokens = gf_ref.shape[0]
    cols = att_ref.shape[2]
    sums_ref[...] = jnp.zeros_like(sums_ref)

    def back(rows):
        value = res_ref[rows, :]
        average = jnp.mean(value, axis=-1, keepdims=True)
        centred = value - average
        inverse = lax.rsqrt(jnp.mean(centred * centred, axis=-1, keepdims=True) + 1e-12)
        normed = centred * inverse
        grad = gf_ref[rows, :]
        scaled = grad * vec_ref[0:1, :]
        inside = (
            scaled
            - jnp.mean(scaled, axis=-1, keepdims=True)
            - normed * jnp.mean(scaled * normed, axis=-1, keepdims=True)
        )
        out = inside * inverse
        low = out.astype(BF16)
        gres_ref[rows, :] = out
        low_ref[rows, :] = low
        fold = lambda v: jnp.sum(v.reshape(STRIP // 8, 8, v.shape[1]), axis=0)
        sums_ref[0:8, :] += fold(grad * normed)
        sums_ref[8:16, :] += fold(grad)
        sums_ref[16:24, :] += fold(low.astype(F32))

    strips(tokens, STRIP, back)
    for copy in copies:
        copy.wait()
    for half in range(2):
        gatt_ref[half] = nn(low_ref[...], w_ref[half]).astype(BF16)

    col_ref[...] = jnp.broadcast_to(mask_ref[...], (LANES, tokens)).T
    lane = lax.broadcasted_iota(jnp.int32, (tokens, LANES), 1) < HD
    pairs = cols // LANES
    scale = BF16(HD ** (-0.5))
    for half in range(2):

        def pair(i, carry, half=half):
            off = pl.multiple_of(i * LANES, LANES)
            off_k = pl.multiple_of(cols + off, LANES)
            off_v = pl.multiple_of(2 * cols + off, LANES)
            query = qkv_ref[half, :, pl.ds(off, LANES)] * scale
            key = qkv_ref[half, :, pl.ds(off_k, LANES)]
            value = qkv_ref[half, :, pl.ds(off_v, LANES)]
            grad = gatt_ref[half, :, pl.ds(off, LANES)]
            att = att_ref[half, :, pl.ds(off, LANES)]
            key_t = (key * scale).T
            delta = (grad.astype(F32) * att.astype(F32)).T
            g_query, g_key, g_value = [], [], []
            for head in range(2):
                pick = lane == (head == 0)
                span = slice(head * HD, (head + 1) * HD)
                zero = jnp.zeros_like(key)
                scores = nt(jnp.where(pick, key, zero), query)
                scores = scores + jnp.concatenate([col_ref[...]] * (tokens // LANES), axis=1)
                probs = jnp.exp(scores - lse_ref[half, pl.ds(i * 2 + head, 1), :])
                g_probs = nt(jnp.where(pick, value, zero), grad)
                row_delta = jnp.sum(delta[span], axis=0, keepdims=True)
                g_scores = (probs * (g_probs - row_delta)).astype(BF16)
                g_value.append(nn(probs.astype(BF16), grad))
                g_key.append(nn(g_scores, query))
                g_query.append(nn(key_t[span], g_scores))
            g_q = jnp.concatenate(g_query, axis=0).T
            gqkv_ref[half, :, pl.ds(off, LANES)] = g_q.astype(BF16)
            gqkv_ref[half, :, pl.ds(off_k, LANES)] = jnp.where(lane, *g_key).astype(BF16)
            gqkv_ref[half, :, pl.ds(off_v, LANES)] = jnp.where(lane, *g_value).astype(BF16)
            return carry

        lax.fori_loop(0, pairs, pair, 0)


def branch_back(g_first, res, vec, att, qkv, lse, mask, pieces):
    tokens, width = g_first.shape
    cols = att.shape[2]
    outs = (
        shaped((tokens, width), F32),
        shaped((2, tokens, 3 * cols), BF16),
        shaped((24, width), F32),
        shaped((tokens, width), BF16),
    )
    return call(
        branch_kernel,
        outs,
        (g_first, res, vec, att, qkv, lse, mask, *pieces),
        in_specs=[WHOLE] * 7 + [ANY] * 4,
        scratch=[
            pltpu.VMEM((2, tokens, cols), BF16),
            pltpu.VMEM((tokens, LANES), F32),
            pltpu.VMEM((2, width, cols), BF16),
            pltpu.SemaphoreType.DMA((2, 4)),
        ],
        flops=8 * tokens * width * width,
    )


def project_back(x_t, g_qkv, g_branch, att, extra):
    width, tokens = x_t.shape
    cols = att.shape[2]
    small = [] if extra is None else [extra]
    columns = 4 * cols + (extra.shape[2] if small else 0)

    def kernel(xt_ref, g_ref, gb_ref, att_ref, *refs):
        outs = refs[len(small) :]
        turned = gb_ref[...].T
        for half in range(2):
            keep, send = outs[2 * half], outs[2 * half + 1]
            span = slice(0, 3 * cols)
            made = nn(xt_ref[...], g_ref[half]).astype(BF16)
            split_rows(made, keep.at[:, span], send.at[:, span], half == 1)
            span = slice(3 * cols, 4 * cols)
            made = nn(turned, att_ref[half]).astype(BF16)
            split_rows(made, keep.at[:, span], send.at[:, span], half == 1)
            if small:
                span = slice(4 * cols, columns)
                made = refs[0][half]
                split_rows(made, keep.at[:, span], send.at[:, span], half == 1)

    out = shaped((width // 2, columns), BF16)
    return call(
        kernel,
        (out, out, out, out),
        (x_t, g_qkv, g_branch, att, *small),
        flops=8 * tokens * width * cols * 2,
    )


def token_back(g_qkv, start, perm, pieces):
    tokens, width = start.shape
    cols = g_qkv.shape[2]

    def kernel(g_ref, start_ref, perm_ref, b0_ref, m0_ref, b1_ref, m1_ref, out_ref, w_ref, sems):
        copies = load_weights((b0_ref, m0_ref, b1_ref, m1_ref), w_ref, sems, 0, cols)
        for copy in copies:
            copy.wait()
        out_ref[...] = start_ref[...] + nt(g_ref[0], w_ref[0]) + nt(g_ref[1], w_ref[1])
        high = out_ref[...].astype(BF16)
        rest = (out_ref[...] - high.astype(F32)).astype(BF16)
        out_ref[...] = nt(high, perm_ref[...]) + nt(rest, perm_ref[...])

    return call(
        kernel,
        shaped((tokens, width), F32),
        (g_qkv, start, perm, *pieces),
        in_specs=[WHOLE] * 3 + [ANY] * 4,
        scratch=[pltpu.VMEM((2, width, cols), BF16), pltpu.SemaphoreType.DMA((2, 4))],
        flops=4 * tokens * width * cols,
    )


class Exchange:
    def __init__(self, size):
        self.size = size
        self.depth = size.bit_length() - 1
        self.rank = lax.axis_index("dp")
        self.core = lax.axis_index("tensor")
        outer = list(range(self.depth - 1, 1, -1))
        self.bits = (outer + [1, 0], outer + [0, 1])

    def flip(self, value, step):
        pairs = []
        for i in range(self.size):
            for core in range(2):
                pairs.append((i * 2 + core, (i ^ (1 << self.bits[core][step])) * 2 + core))
        return lax.ppermute(value, ("dp", "tensor"), pairs)

    def blocks(self):
        tables = []
        for bits in self.bits:
            tables.append(
                [
                    sum(((j >> step) & 1) << bit for step, bit in enumerate(bits))
                    for j in range(self.size)
                ]
            )
        table = np.array(tables, np.int32)
        return jnp.where(self.core == 0, table[0], table[1]) ^ self.rank


def join(held, came):
    return jnp.concatenate([held, came], axis=0)


def added(*values):
    total = values[0].astype(F32)
    for value in values[1:]:
        total = total + value.astype(F32)
    return total


def halves(value):
    middle = value.shape[0] // 2
    return value[:middle], value[middle:]


def three_parts(value):
    high = lax.reduce_precision(value, 8, 7)
    rest = value - high
    middle = lax.reduce_precision(rest, 8, 7)
    return (high.astype(BF16), middle.astype(BF16), (rest - middle).astype(BF16))


def body(
    tokens,
    lengths,
    key_mask,
    order,
    query_key_value_weight,
    output_projection_weight,
    up_projection_weight,
    down_projection_weight,
    embedding_projection_weight,
    gains,
    biases,
    up_bias_vector,
    cotangent,
):
    size = lax.axis_size("dp")
    core = lax.axis_index("tensor")
    ways = Exchange(size)
    depth = ways.depth
    half_len = tokens.shape[1]
    full_len = key_mask.shape[1]
    width = tokens.shape[2]
    cols = output_projection_weight.shape[0]
    rows = output_projection_weight.shape[1]
    ff_local = up_projection_weight.shape[1]
    chunk = gains.shape[1]
    emb_size = embedding_projection_weight.size
    sides = (core, 1 - core)

    vector = jnp.concatenate([gains.reshape(-1), biases.reshape(-1), up_bias_vector])
    pad_to = -(-vector.size // 128) * 128
    vector_size = vector.size
    vector = jnp.pad(vector, (0, pad_to - vector_size))
    flat = jnp.concatenate([embedding_projection_weight.reshape(-1), *three_parts(vector)])
    extra = -(-flat.size // (rows * 128)) * 128
    flat = jnp.pad(flat, (0, rows * extra - flat.size)).reshape(rows, extra)
    one = jnp.concatenate(
        [
            query_key_value_weight[0],
            query_key_value_weight[1],
            query_key_value_weight[2],
            output_projection_weight.T,
            flat,
        ],
        axis=1,
    )
    two = up_projection_weight
    three = down_projection_weight.T

    mine = order[0, core]
    theirs = order[0, 1 - core]
    my_half = lax.dynamic_index_in_dim(tokens, mine, 0, keepdims=False)
    their_half = lax.dynamic_index_in_dim(tokens, theirs, 0, keepdims=False)
    for step in range(depth - 2):
        if step == 0:
            one_came, half_came = together(ways.flip(one, step), swap_cores(their_half))
        else:
            one_came = ways.flip(one, step)
        one = join(one, one_came)
    for step in range(depth - 3):
        two = join(two, ways.flip(two, step))
    one_came, two_came = together(ways.flip(one, depth - 2), ways.flip(two, depth - 3))
    one_both = join(one, one_came)
    two = join(two, two_came)
    for step in range(depth - 3):
        three = join(three, ways.flip(three, step))
    one_more, three_came = together(ways.flip(one_both, depth - 1), ways.flip(three, depth - 3))
    three = join(three, three_came)
    one_both_other, one_more_other, two_came = together(
        swap_cores(one_both), swap_cores(one_more), ways.flip(two, depth - 2)
    )
    two_both = join(two, two_came)
    one_pieces = (one_both, one_more, one_both_other, one_more_other)

    def in_order(own, other):
        return jnp.where(
            core == 0, jnp.concatenate([own, other]), jnp.concatenate([other, own])
        )

    def half_of(value, which):
        return lax.dynamic_slice_in_dim(value, which * half_len, half_len)

    here = in_order(my_half, half_came)
    seq_len = lengths[mine]
    marks = lax.dynamic_index_in_dim(key_mask, mine, 0, keepdims=False)
    places = jnp.arange(full_len, dtype=jnp.int32)
    key_ok = (places < seq_len) & ((marks == 1) | (places == 0))
    mask = jnp.where(key_ok, 0.0, -1e30).astype(F32)[None, :]
    blocks = ways.blocks()
    where = (blocks[:, None] * rows + jnp.arange(rows, dtype=jnp.int32)[None]).reshape(-1)
    perm = (jnp.arange(width, dtype=jnp.int32)[:, None] == where[None]).astype(BF16)

    wide = 4 * cols
    quarter = width // 4
    small_own = jnp.concatenate([one_both[:, wide:], one_more[:, wide:]])
    small_other = jnp.concatenate(
        [
            one_both_other[:quarter, wide:],
            one_more_other[:quarter, wide:],
            one_both_other[quarter:, wide:],
            one_more_other[quarter:, wide:],
        ]
    )
    small = [part.reshape(size, rows * extra) for part in (small_own, small_other)]
    small = jnp.where(core == 0, jnp.stack(small, 1), jnp.stack(small[::-1], 1))
    proj = small[:, :, :emb_size].reshape(width, -1)
    thirds = small[:, :, emb_size : emb_size + 3 * pad_to].astype(F32)
    thirds = thirds.reshape(size, 2, 3, pad_to)
    vectors = thirds[:, :, 0] + (thirds[:, :, 1] + thirds[:, :, 2])
    places_of = jnp.argsort(blocks)
    plain = vectors[places_of].reshape(size * 2, pad_to)
    vectors = vectors.reshape(size * 2, pad_to)
    vec = jnp.moveaxis(vectors[:, : 8 * chunk].reshape(-1, 8, chunk), 1, 0).reshape(8, width)
    query_bias = plain[:, 2 * chunk : 3 * chunk].reshape(-1)
    value_bias = plain[:, 3 * chunk : 4 * chunk].reshape(-1)
    up_bias = plain[:, 8 * chunk : vector_size].reshape(-1)
    head_bias, side_bias = [], []
    for side in sides:
        query_part = lax.dynamic_slice_in_dim(query_bias, side * cols, cols)
        value_part = lax.dynamic_slice_in_dim(value_bias, side * cols, cols)
        head_bias.append(jnp.concatenate([query_part, jnp.zeros_like(query_part), value_part]))
        side_bias.append(lax.dynamic_slice_in_dim(up_bias, side * ff_local, ff_local)[None])
    head_bias = jnp.stack(head_bias)

    two_more, three_came = ways.flip(two_both, depth - 1), ways.flip(three, depth - 2)
    qkv, lse, att, res_one, first, first_low, first_low_t, here_t = attention_forward(
        after(here, two_both, three), perm, head_bias, mask, vec, one_pieces, cols
    )
    two_more, three_came = after((two_more, three_came), first_low)
    three_both = join(three, three_came)
    three_more = ways.flip(three_both, depth - 1)
    two_both_other, two_more_other = swap_cores(two_both), swap_cores(two_more)
    hid_own, slope_own = up_forward(
        after(first_low, three_both, two_more), (two_both, two_more), side_bias[0], False
    )
    two_both_other, two_more_other = after((two_both_other, two_more_other), hid_own)
    hid_other, slope_other = up_forward(
        first_low, (two_both_other, two_more_other), side_bias[1], True
    )
    three_more = after(three_more, hid_other)
    cot_mine = lax.dynamic_index_in_dim(cotangent, core, 0, keepdims=False)
    cot_other = lax.dynamic_index_in_dim(cotangent, 1 - core, 0, keepdims=False)
    three_both_other, three_more_other, cot_came = together(
        swap_cores(three_both), swap_cores(three_more), swap_cores(cot_other)
    )
    cot = in_order(cot_mine, cot_came)
    emb, g_ffn, g_ffn_t, g_res_two, proj_grad, sums_two = down_both(
        seq_len[None],
        (hid_own, hid_other),
        (three_both, three_more, three_both_other, three_more_other),
        first,
        vec,
        proj,
        cot,
    )

    def low(*values):
        return added(*values).astype(BF16)

    dk_other, ds_other = down_grad(g_ffn_t, hid_other, True)
    ds_came, dk_came = swap_cores(ds_other), swap_cores(dk_other)
    dk, ds = down_grad(g_ffn_t, after(hid_own, ds_other), False)
    ds_came, dk_came = after((ds_came, dk_came), ds)
    d_sent = low(ds, ds_came)
    d_came = ways.flip(d_sent, depth - 1)
    uk_other, us_other, up_bias_other, part = up_grad(
        after(g_ffn, d_sent),
        first_low_t,
        slope_other,
        (three_both_other, three_more_other),
        (two_both_other, two_more_other),
        g_res_two,
        True,
    )
    us_came, uk_came = swap_cores(us_other), swap_cores(uk_other)
    uk, us, up_bias_own, g_first = up_grad(
        after(g_ffn, us_other),
        first_low_t,
        slope_own,
        (three_both, three_more),
        (two_both, two_more),
        part,
        False,
    )
    d_came, us_came, uk_came = after((d_came, us_came, uk_came), us)
    u_sent = low(us, us_came)
    d_kept, d_sent = halves(dk), low(halves(dk)[1], halves(dk_came)[1], halves(d_came)[1])
    u_came = ways.flip(u_sent, depth - 1)
    d_held = added(halves(dk)[0], halves(dk_came)[0], halves(d_came)[0])
    d_came = ways.flip(d_sent, depth - 2)
    g_res_one, g_qkv, sums_one, g_branch = branch_back(
        after(g_first, u_sent, d_sent), res_one, vec, att, qkv, lse, mask, one_pieces
    )
    d_came, u_came = after((d_came, u_came), g_qkv)
    u_sent = low(halves(uk)[1], halves(uk_came)[1], halves(u_came)[1])
    u_held = added(halves(uk)[0], halves(uk_came)[0], halves(u_came)[0])
    u_came = ways.flip(u_sent, depth - 2)
    d_held = d_held + d_came.astype(F32)
    held, sent = halves(d_held)
    d_sent = sent.astype(BF16)
    d_came = ways.flip(d_sent, depth - 3)

    def fold(value):
        return jnp.sum(value.reshape(-1, 8, value.shape[-1]), axis=1)

    def absolute(own, other):
        return jnp.where(
            core == 0, jnp.concatenate([own, other]), jnp.concatenate([other, own])
        )

    gain_two, shift_two, ffn_bias_grad = fold(sums_two)
    gain_one, shift_one, out_bias_grad = fold(sums_one)
    up_bias_grad = absolute(fold(up_bias_own)[0], fold(up_bias_other)[0])
    qkv_bias_grads = jnp.sum(g_qkv.astype(F32), axis=1)
    query_bias_grad = absolute(qkv_bias_grads[0][:cols], qkv_bias_grads[1][:cols])
    value_bias_grad = absolute(qkv_bias_grads[0][2 * cols :], qkv_bias_grads[1][2 * cols :])

    def relative(value):
        return value.reshape(size, 2, -1)[blocks]

    small_grads = jnp.concatenate(
        [
            proj_grad.reshape(size, 2, emb_size),
            gain_one.reshape(size, 2, chunk),
            gain_two.reshape(size, 2, chunk),
            relative(query_bias_grad),
            relative(value_bias_grad),
            out_bias_grad.reshape(size, 2, chunk),
            shift_one.reshape(size, 2, chunk),
            ffn_bias_grad.reshape(size, 2, chunk),
            shift_two.reshape(size, 2, chunk),
            relative(up_bias_grad),
        ],
        axis=2,
    ).astype(BF16)
    small_grads = jnp.pad(small_grads, ((0, 0), (0, 0), (0, rows * extra - small_grads.shape[2])))
    small_grads = jnp.where(core == 0, small_grads, small_grads[:, ::-1])
    small_grads = jnp.moveaxis(small_grads, 1, 0).reshape(2, width, extra)

    qk, qs, qk_other, qs_other = project_back(
        after(here_t, u_sent, d_sent), g_qkv, g_branch, att, small_grads
    )
    d_came, u_came = after((d_came, u_came), qs)
    d_held = held + d_came.astype(F32)
    u_held = u_held + u_came.astype(F32)
    qs_came, qk_came = swap_cores(qs_other), swap_cores(qk_other)
    g_here = token_back(after(g_qkv, qs_other, d_held), g_res_one, perm, one_pieces)
    qs_came, qk_came = after((qs_came, qk_came), g_here)
    q_sent = low(qs, qs_came)
    q_came = ways.flip(q_sent, depth - 1)

    def outer(value, steps):
        for step in range(steps - 1, -1, -1):
            kept, sent = halves(value)
            value = kept + ways.flip(sent.astype(BF16), step).astype(F32)
        return value

    down_shard = outer(d_held, depth - 3)
    up_shard = outer(u_held, depth - 2)
    q_sent = low(halves(qk)[1], halves(qk_came)[1], halves(q_came)[1])
    q_held = added(halves(qk)[0], halves(qk_came)[0], halves(q_came)[0])
    q_held = q_held + ways.flip(q_sent, depth - 2).astype(F32)
    one_shard = outer(q_held, depth - 2)

    qkv_shard = jnp.stack([one_shard[:, i * cols : (i + 1) * cols] for i in range(3)])
    out_shard = one_shard[:, 3 * cols : wide].T
    tail = one_shard[:, wide:].reshape(-1)
    emb_shard = tail[:emb_size].reshape(embedding_projection_weight.shape)
    tail = tail[emb_size:]
    gain_shard = tail[: 2 * chunk].reshape(2, chunk)
    bias_shard = tail[2 * chunk : 8 * chunk].reshape(6, chunk)
    up_bias_shard = tail[8 * chunk : vector_size]

    def give_back(value, places_of):
        own = half_of(value, core)
        other = swap_cores(half_of(value, 1 - core))
        blank = jnp.zeros((2,) + own.shape, value.dtype)
        blank = lax.dynamic_update_slice(blank, own[None], (places_of[0], 0, 0))
        return lax.dynamic_update_slice(blank, other[None], (places_of[1], 0, 0))

    embeddings = give_back(emb, (core, 1 - core))
    grad_tokens = give_back(g_here, (mine, theirs))
    return (
        embeddings,
        grad_tokens,
        qkv_shard,
        out_shard,
        up_shard,
        down_shard.T,
        emb_shard,
        gain_shard,
        bias_shard,
        up_bias_shard,
    )


def solution(mesh):
    return jax.shard_map(
        body,
        mesh=mesh,
        in_specs=(
            P("dp", "tensor", None),
            P("dp"),
            P("dp", None),
            P("dp", None),
            P(None, "dp", "tensor"),
            P("tensor", "dp"),
            P("dp", "tensor"),
            P("tensor", "dp"),
            P(("dp", "tensor"), None),
            P(None, ("dp", "tensor")),
            P(None, ("dp", "tensor")),
            P(("dp", "tensor")),
            P("dp", "tensor", None),
        ),
        out_specs=(
            P("dp", "tensor", None),
            P("dp", "tensor", None),
            P(None, "dp", "tensor"),
            P("tensor", "dp"),
            P("dp", "tensor"),
            P("tensor", "dp"),
            P(("dp", "tensor"), None),
            P(None, ("dp", "tensor")),
            P(None, ("dp", "tensor")),
            P(("dp", "tensor")),
        ),
        check_vma=False,
    )
```

```python
import functools

import jax
import jax.numpy as jnp
import numpy as np
from jax import lax
from jax.experimental import pallas as pl
from jax.experimental.pallas import tpu as pltpu
from jax.sharding import PartitionSpec as P

HD = 64
LANES = 128
STRIP = 128
F32 = jnp.float32
BF16 = jnp.bfloat16
VMEM_LIMIT = 18 * 1024 * 1024


def nn(left, right):
    return lax.dot_general(left, right, (((1,), (0,)), ((), ())), preferred_element_type=F32)


def nt(left, right):
    return lax.dot_general(left, right, (((1,), (1,)), ((), ())), preferred_element_type=F32)


def swap_cores(value):
    return lax.ppermute(value, "tensor", [(0, 1), (1, 0)])


def after(value, *others):
    return lax.optimization_barrier((value, others))[0]


def together(*values):
    return lax.optimization_barrier(values)


def strips(count, size, step):
    def run(i, carry):
        step(pl.ds(pl.multiple_of(i * size, size), size))
        return carry

    lax.fori_loop(0, count // size, run, 0)


def columns_of(width, step):
    block = 256 if width % 256 == 0 else width

    def run(i, carry):
        step(pl.ds(pl.multiple_of(i * block, block), block))
        return carry

    lax.fori_loop(0, width // block, run, 0)


def call(body, outs, args, grid=None, in_specs=None, out_specs=None, scratch=(), flops=0):
    whole = pl.BlockSpec(memory_space=pltpu.VMEM)
    return pl.pallas_call(
        body,
        out_shape=outs,
        grid=grid or (),
        in_specs=in_specs or [whole] * len(args),
        out_specs=out_specs or jax.tree.map(lambda _: whole, outs),
        scratch_shapes=scratch,
        compiler_params=pltpu.CompilerParams(vmem_limit_bytes=VMEM_LIMIT),
        cost_estimate=pl.CostEstimate(flops=flops, bytes_accessed=1 << 20, transcendentals=0),
    )(*args)


def shaped(shape, dtype):
    return jax.ShapeDtypeStruct(shape, dtype)


ANY = pl.BlockSpec(memory_space=pl.ANY)
WHOLE = pl.BlockSpec(memory_space=pltpu.VMEM)


OTHER = (0, 2, 1, 3)


def load_weights(pieces, target, sems, first=0, last=None, at=(0,) * 8):
    quarter = target.shape[1] // 4
    columns = slice(first, last)
    copies = []
    for side in range(2):
        for place in range(4):
            source = place if side == 0 else 4 + OTHER[place]
            rows = pl.ds(at[source] * quarter, quarter)
            copies.append(
                pltpu.make_async_copy(
                    pieces[source].at[rows, columns],
                    target.at[side, pl.ds(place * quarter, quarter)],
                    sems.at[side, place],
                )
            )
    for copy in copies:
        copy.start()
    return copies


def attention_kernel(
    x_ref, perm_ref, bias_ref, mask_ref, vec_ref, *refs
):
    pieces, refs = refs[:8], refs[8:]
    qkv_ref, lse_ref, att_ref, res_ref, first_ref, low_ref, lowt_ref, xt_ref, w_ref = refs[:9]
    col_ref, rel_ref, sems = refs[9:]
    cols = qkv_ref.shape[2] // 3
    tokens = x_ref.shape[0]
    copies = load_weights(pieces, w_ref, sems, 0, 4 * cols)

    def reorder(span):
        rel_ref[:, span] = nn(x_ref[...], perm_ref[:, span]).astype(BF16)

    columns_of(x_ref.shape[1], reorder)
    xt_ref[...] = rel_ref[...].T
    col_ref[...] = jnp.broadcast_to(mask_ref[...], (LANES, tokens)).T
    for copy in copies:
        copy.wait()

    def project(i, carry):
        half, part = i // 3, i % 3
        span = pl.ds(pl.multiple_of(part * cols, cols), cols)
        made = nn(rel_ref[...], w_ref[half, :, span]) + bias_ref[pl.ds(half, 1), span]
        qkv_ref[half, :, span] = made.astype(BF16)
        return carry

    lax.fori_loop(0, 6, project, 0)
    lane = lax.broadcasted_iota(jnp.int32, (tokens, LANES), 1) < HD
    pairs = cols // LANES


    def pair(step, carry):
        half, i = step // pairs, step % pairs
        off = pl.multiple_of(i * LANES, LANES)
        query = qkv_ref[half, :, pl.ds(off, LANES)] * BF16(HD ** (-0.5))
        key = qkv_ref[half, :, pl.ds(pl.multiple_of(cols + off, LANES), LANES)]
        value = qkv_ref[half, :, pl.ds(pl.multiple_of(2 * cols + off, LANES), LANES)]
        value_t = value.T
        outs = []
        for head in range(2):
            kept = jnp.where(lane == (head == 0), key, jnp.zeros_like(key))
            scores = nt(kept, query)
            scores = scores + jnp.concatenate([col_ref[...]] * (tokens // LANES), axis=1)
            top = jnp.max(scores, axis=0, keepdims=True)
            shifted = jnp.exp(scores - top)
            total = jnp.sum(shifted, axis=0, keepdims=True)
            out = nn(value_t[head * HD : (head + 1) * HD], shifted.astype(BF16))
            outs.append(out / total)
            lse_ref[half, pl.ds(i * 2 + head, 1), :] = top + jnp.log(total)
        both = jnp.concatenate(outs, axis=0).T
        att_ref[half, :, pl.ds(off, LANES)] = both.astype(BF16)
        return carry

    lax.fori_loop(0, 2 * pairs, pair, 0)
    out = slice(3 * cols, 4 * cols)

    def branch(span):
        made = nt(att_ref[0], w_ref[0, span, out]) + nt(att_ref[1], w_ref[1, span, out])
        res_ref[:, span] = made

    columns_of(x_ref.shape[1], branch)

    def norm(rows):
        value = res_ref[rows, :] + vec_ref[4:5, :] + rel_ref[rows, :].astype(F32)
        res_ref[rows, :] = value
        average = jnp.mean(value, axis=-1, keepdims=True)
        centred = value - average
        inverse = lax.rsqrt(jnp.mean(centred * centred, axis=-1, keepdims=True) + 1e-12)
        first = centred * inverse * vec_ref[0:1, :] + vec_ref[5:6, :]
        first_ref[rows, :] = first
        low_ref[rows, :] = first.astype(BF16)

    strips(tokens, STRIP, norm)
    lowt_ref[...] = low_ref[...].T


def attention_forward(x, perm, head_bias, mask, vec, pieces, cols):
    tokens, width = x.shape
    heads = cols // HD
    outs = (
        shaped((2, tokens, 3 * cols), BF16),
        shaped((2, heads, tokens), F32),
        shaped((2, tokens, cols), BF16),
        shaped((tokens, width), F32),
        shaped((tokens, width), F32),
        shaped((tokens, width), BF16),
        shaped((width, tokens), BF16),
        shaped((width, tokens), BF16),
        shaped((2, width, 4 * cols), BF16),
    )
    return call(
        attention_kernel,
        outs,
        (x, perm, head_bias, mask, vec, *pieces),
        in_specs=[WHOLE] * 5 + [ANY] * 8,
        scratch=[
            pltpu.VMEM((tokens, LANES), F32),
            pltpu.VMEM((tokens, width), BF16),
            pltpu.SemaphoreType.DMA((2, 4)),
        ],
        flops=8 * tokens * width * width,
    )


ERF = (0.254829592, -0.284496736, 1.421413741, -1.453152027, 1.061405429)


def gelu_pair(value):
    size = jnp.abs(value)
    bell = jnp.exp(-0.5 * value * value)
    t = 1.0 / (1.0 + (0.3275911 * 0.5**0.5) * size)
    poly = ERF[4]
    for term in ERF[3::-1]:
        poly = poly * t + term
    tail = 0.5 * poly * t * bell
    phi = jnp.where(value >= 0, 1.0 - tail, tail)
    return value * phi, phi + value * bell * 0.3989422804014327


def join_rows(refs, target, swapped):
    quarter = target.shape[0] // 4
    for place in range(4):
        source = OTHER[place] if swapped else place
        target[place * quarter : (place + 1) * quarter, :] = refs[source][...]


def split_rows(value, keep_ref, send_ref, swapped):
    quarter = value.shape[0] // 4
    for place in range(4):
        source = OTHER[place] if swapped else place
        ref = (keep_ref, send_ref)[place // 2]
        rows = slice((place % 2) * quarter, (place % 2 + 1) * quarter)
        ref[rows, :] = value[source * quarter : (source + 1) * quarter, :]


def column_block(hidden):
    return 512 if hidden % 512 == 0 else hidden


def up_forward(low, pieces, bias, swapped):
    tokens, width = low.shape
    pieces, at = zip(*pieces)
    hidden = pieces[0].shape[1]
    block = column_block(hidden)

    def kernel(low_ref, a_ref, b_ref, c_ref, d_ref, bias_ref, hid_ref, slope_ref, acc_ref, w_ref):
        join_rows((a_ref, b_ref, c_ref, d_ref), w_ref, swapped)
        acc_ref[...] = nn(low_ref[...], w_ref[...])

        def act(rows):
            active, slope = gelu_pair(acc_ref[rows, :] + bias_ref[...])
            hid_ref[rows, :] = active.astype(BF16)
            slope_ref[rows, :] = slope.astype(BF16)

        strips(tokens, STRIP, act)

    outs = (shaped((tokens, hidden), BF16), shaped((tokens, hidden), BF16))
    chunk = pl.BlockSpec((tokens, block), lambda i: (0, i))
    parts = [pl.BlockSpec((width // 4, block), lambda i, row=row: (row, i)) for row in at]
    return call(
        kernel,
        outs,
        (low, *pieces, bias),
        grid=(hidden // block,),
        in_specs=[
            pl.BlockSpec((tokens, width), lambda i: (0, 0)),
            *parts,
            pl.BlockSpec((1, block), lambda i: (0, i)),
        ],
        out_specs=(chunk, chunk),
        scratch=[pltpu.VMEM((tokens, block), F32), pltpu.VMEM((width, block), BF16)],
        flops=2 * tokens * width * hidden,
    )


def down_kernel(
    at, len_ref, h0_ref, h1_ref, first_ref, vec_ref, proj_ref, cot_ref, *refs
):
    pieces, refs = refs[:8], refs[8:]
    emb_ref, low_ref, lowt_ref, res_ref, pgrad_ref, sums_ref = refs[:6]
    ffn_ref, norm_ref, sec_ref, gp_ref, gs_ref, inv_ref, prj_ref, w_ref, sems = refs[6:]
    copies = load_weights(pieces, w_ref, sems, at=at)
    tokens = first_ref.shape[0]
    length = len_ref[0]
    for copy in copies:
        copy.wait()

    def matmul(span):
        ffn_ref[:, span] = nt(h0_ref[...], w_ref[0, span]) + nt(h1_ref[...], w_ref[1, span])

    columns_of(ffn_ref.shape[1], matmul)

    def norm(rows):
        value = first_ref[rows, :] + ffn_ref[rows, :] + vec_ref[6:7, :]
        average = jnp.mean(value, axis=-1, keepdims=True)
        centred = value - average
        inverse = lax.rsqrt(jnp.mean(centred * centred, axis=-1, keepdims=True) + 1e-12)
        normed = centred * inverse
        norm_ref[rows, :] = normed
        inv_ref[rows, :] = jnp.broadcast_to(inverse, (STRIP, LANES))
        sec_ref[rows, :] = (normed * vec_ref[1:2, :] + vec_ref[7:8, :]).astype(BF16)

    strips(tokens, STRIP, norm)
    prj_ref[...] = nn(sec_ref[...], proj_ref[...])

    def embed(rows):
        projected = prj_ref[rows, :]
        valid = rows.start + lax.broadcasted_iota(jnp.int32, projected.shape, 0) < length
        valid = valid.astype(F32)
        scale = lax.rsqrt(jnp.sum(projected * projected, axis=-1, keepdims=True) + 1e-06)
        unit = projected * scale
        emb_ref[rows, :] = unit * valid
        cot = cot_ref[rows, :] * valid
        back = scale * (cot - unit * jnp.sum(unit * cot, axis=-1, keepdims=True))
        gp_ref[rows, :] = back.astype(BF16)

    strips(tokens, STRIP, embed)
    pgrad_ref[...] = nn(sec_ref[...].T, gp_ref[...])
    gs_ref[...] = nt(gp_ref[...], proj_ref[...])
    sums_ref[...] = jnp.zeros_like(sums_ref)

    def back(rows):
        grad = gs_ref[rows, :]
        normed = norm_ref[rows, :]
        scaled = grad * vec_ref[1:2, :]
        inside = (
            scaled
            - jnp.mean(scaled, axis=-1, keepdims=True)
            - normed * jnp.mean(scaled * normed, axis=-1, keepdims=True)
        )
        value = inside * inv_ref[rows, 0:1]
        low = value.astype(BF16)
        res_ref[rows, :] = value
        low_ref[rows, :] = low
        fold = lambda v: jnp.sum(v.reshape(STRIP // 8, 8, v.shape[1]), axis=0)
        sums_ref[0:8, :] += fold(grad * normed)
        sums_ref[8:16, :] += fold(grad)
        sums_ref[16:24, :] += fold(low.astype(F32))

    strips(tokens, STRIP, back)
    lowt_ref[...] = low_ref[...].T


def down_both(length, hidden, pieces, first, vec, proj, cot):
    tokens, width = first.shape
    embed = proj.shape[1]
    outs = (
        shaped((tokens, embed), F32),
        shaped((tokens, width), BF16),
        shaped((width, tokens), BF16),
        shaped((tokens, width), F32),
        shaped((width, embed), F32),
        shaped((24, width), F32),
    )
    pieces, at = zip(*pieces)
    args = (length, *hidden, first, vec, proj, cot, *pieces)
    return call(
        functools.partial(down_kernel, at),
        outs,
        args,
        in_specs=[pl.BlockSpec(memory_space=pltpu.SMEM)] + [WHOLE] * 6 + [ANY] * 8,
        scratch=[
            pltpu.VMEM((tokens, width), F32),
            pltpu.VMEM((tokens, width), F32),
            pltpu.VMEM((tokens, width), BF16),
            pltpu.VMEM((tokens, embed), BF16),
            pltpu.VMEM((tokens, width), F32),
            pltpu.VMEM((tokens, LANES), F32),
            pltpu.VMEM((tokens, embed), F32),
            pltpu.VMEM((2, width, hidden[0].shape[1]), BF16),
            pltpu.SemaphoreType.DMA((2, 4)),
        ],
        flops=2 * tokens * width * hidden[0].shape[1] * 2,
    )


def down_grad(g_low_t, hid, swapped):
    width, tokens = g_low_t.shape
    hidden = hid.shape[1]
    block = column_block(hidden)

    def kernel(gt_ref, hid_ref, keep_ref, send_ref):
        split_rows(nn(gt_ref[...], hid_ref[...]).astype(BF16), keep_ref, send_ref, swapped)

    piece = pl.BlockSpec((width // 2, block), lambda i: (0, i))
    out = shaped((width // 2, hidden), BF16)
    return call(
        kernel,
        (out, out),
        (g_low_t, hid),
        grid=(hidden // block,),
        in_specs=[
            pl.BlockSpec((width, tokens), lambda i: (0, 0)),
            pl.BlockSpec((tokens, block), lambda i: (0, i)),
        ],
        out_specs=(piece, piece),
        flops=2 * tokens * width * hidden,
    )


def up_grad(g_low, low_t, slope, down, up, start, swapped):
    tokens, width = g_low.shape
    pieces, at = zip(*down, *up)
    hidden = slope.shape[1]
    block = column_block(hidden)

    def kernel(g_ref, lowt_ref, slope_ref, start_ref, *refs):
        join_rows(refs[:4], wd_ref := refs[-2], swapped)
        join_rows(refs[4:8], wu_ref := refs[-1], swapped)
        keep_ref, send_ref, bias_ref, first_ref, gh_ref, gin_ref = refs[8:-2]
        def matmul(span):
            gh_ref[:, span] = nn(g_ref[...], wd_ref[:, span])

        columns_of(block, matmul)
        bias_ref[...] = jnp.zeros_like(bias_ref)

        def act(rows):
            grad = (gh_ref[rows, :] * slope_ref[rows, :].astype(F32)).astype(BF16)
            gin_ref[rows, :] = grad
            wide = grad.astype(F32)
            bias_ref[...] += jnp.sum(wide.reshape(STRIP // 8, 8, wide.shape[1]), axis=0)

        strips(tokens, STRIP, act)
        split_rows(nn(lowt_ref[...], gin_ref[...]).astype(BF16), keep_ref, send_ref, swapped)
        @pl.when(pl.program_id(0) == 0)
        def _():
            first_ref[...] = start_ref[...]

        def add(span):
            first_ref[:, span] += nt(gin_ref[...], wu_ref[span, :])

        columns_of(width, add)

    row = pl.BlockSpec((tokens, width), lambda i: (0, 0))
    turned = pl.BlockSpec((width, tokens), lambda i: (0, 0))
    act = pl.BlockSpec((tokens, block), lambda i: (0, i))
    piece = pl.BlockSpec((width // 2, block), lambda i: (0, i))
    parts = [pl.BlockSpec((width // 4, block), lambda i, row=row: (row, i)) for row in at]
    out = shaped((width // 2, hidden), BF16)
    return call(
        kernel,
        (out, out, shaped((8, hidden), F32), shaped((tokens, width), F32)),
        (g_low, low_t, slope, start, *pieces),
        grid=(hidden // block,),
        in_specs=[row, turned, act, row] + parts,
        out_specs=(piece, piece, pl.BlockSpec((8, block), lambda i: (0, i)), row),
        scratch=[
            pltpu.VMEM((tokens, block), F32),
            pltpu.VMEM((tokens, block), BF16),
            pltpu.VMEM((width, block), BF16),
            pltpu.VMEM((width, block), BF16),
        ],
        flops=6 * tokens * width * hidden,
    )


def norm_back(g_first, res, vec, weights, cols):
    tokens, width = g_first.shape

    def kernel(
        gf_ref, res_ref, vec_ref, w_ref, gres_ref, turn_ref, gatt_ref, sums_ref, low_ref
    ):
        sums_ref[...] = jnp.zeros_like(sums_ref)

        def back(rows):
            value = res_ref[rows, :]
            average = jnp.mean(value, axis=-1, keepdims=True)
            centred = value - average
            inverse = lax.rsqrt(jnp.mean(centred * centred, axis=-1, keepdims=True) + 1e-12)
            normed = centred * inverse
            grad = gf_ref[rows, :]
            scaled = grad * vec_ref[0:1, :]
            inside = (
                scaled
                - jnp.mean(scaled, axis=-1, keepdims=True)
                - normed * jnp.mean(scaled * normed, axis=-1, keepdims=True)
            )
            out = inside * inverse
            low = out.astype(BF16)
            gres_ref[rows, :] = out
            low_ref[rows, :] = low
            fold = lambda v: jnp.sum(v.reshape(STRIP // 8, 8, v.shape[1]), axis=0)
            sums_ref[0:8, :] += fold(grad * normed)
            sums_ref[8:16, :] += fold(grad)
            sums_ref[16:24, :] += fold(low.astype(F32))

        strips(tokens, STRIP, back)
        turn_ref[...] = low_ref[...].T
        for half in range(2):
            gatt_ref[half] = nn(low_ref[...], w_ref[half, :, 3 * cols :]).astype(BF16)

    outs = (
        shaped((tokens, width), F32),
        shaped((width, tokens), BF16),
        shaped((2, tokens, cols), BF16),
        shaped((24, width), F32),
    )
    return call(
        kernel,
        outs,
        (g_first, res, vec, weights),
        scratch=[pltpu.VMEM((tokens, width), BF16)],
        flops=4 * tokens * width * cols,
    )


def attention_back(pairs, g_att, att, qkv, lse, mask):
    tokens, cols = att.shape[1:]
    wide = len(pairs) * LANES
    scale = HD ** (-0.5)

    def kernel(gatt_ref, att_ref, qkv_ref, lse_ref, mask_ref, gqkv_ref, sums_ref, col_ref):
        col_ref[...] = jnp.broadcast_to(mask_ref[...], (LANES, tokens)).T
        lane = lax.broadcasted_iota(jnp.int32, (tokens, LANES), 1) < HD

        def pair(step, carry):
            half, place = step // len(pairs), step % len(pairs)
            i = pairs[0] + place
            off = pl.multiple_of(i * LANES, LANES)
            off_k = pl.multiple_of(cols + off, LANES)
            off_v = pl.multiple_of(2 * cols + off, LANES)
            query = qkv_ref[half, :, pl.ds(off, LANES)] * BF16(scale)
            key = qkv_ref[half, :, pl.ds(off_k, LANES)]
            value = qkv_ref[half, :, pl.ds(off_v, LANES)]
            grad = gatt_ref[half, :, pl.ds(off, LANES)]
            out = att_ref[half, :, pl.ds(off, LANES)]
            key_t = (key * BF16(scale)).T
            delta = (grad.astype(F32) * out.astype(F32)).T
            g_query, g_key, g_value = [], [], []
            for head in range(2):
                pick = lane == (head == 0)
                span = slice(head * HD, (head + 1) * HD)
                zero = jnp.zeros_like(key)
                scores = nt(jnp.where(pick, key, zero), query)
                scores = scores + jnp.concatenate([col_ref[...]] * (tokens // LANES), axis=1)
                probs = jnp.exp(scores - lse_ref[half, pl.ds(i * 2 + head, 1), :])
                g_probs = nt(jnp.where(pick, value, zero), grad)
                row_delta = jnp.sum(delta[span], axis=0, keepdims=True)
                g_scores = (probs * (g_probs - row_delta)).astype(BF16)
                g_value.append(nn(probs.astype(BF16), grad))
                g_key.append(nn(g_scores, query))
                g_query.append(nn(key_t[span], g_scores))
            g_q = jnp.concatenate(g_query, axis=0).T.astype(BF16)
            g_v = jnp.where(lane, *g_value).astype(BF16)
            to = pl.multiple_of(place * LANES, LANES)
            gqkv_ref[half, :, pl.ds(to, LANES)] = g_q
            to_k = pl.ds(pl.multiple_of(wide + to, LANES), LANES)
            gqkv_ref[half, :, to_k] = jnp.where(lane, *g_key).astype(BF16)
            gqkv_ref[half, :, pl.ds(pl.multiple_of(2 * wide + to, LANES), LANES)] = g_v
            for row, grads in ((0, g_q), (1, g_v)):
                total = jnp.sum(grads.astype(F32).reshape(-1, 8, LANES), axis=0)
                sums_ref[half, row, :, pl.ds(to, LANES)] = total
            return carry

        lax.fori_loop(0, 2 * len(pairs), pair, 0)

    return call(
        kernel,
        (shaped((2, tokens, 3 * wide), BF16), shaped((2, 2, 8, wide), F32)),
        (g_att, att, qkv, lse, mask),
        scratch=[pltpu.VMEM((tokens, LANES), F32)],
        flops=20 * tokens * tokens * wide * 2,
    )


def project_other(x_t, g_qkv, beside):
    width, tokens = x_t.shape
    columns = g_qkv.shape[2]
    extra = beside[1].shape[2] if beside else 0

    def kernel(xt_ref, g_ref, *refs):
        keep_ref, send_ref = refs[len(beside) :]
        span = slice(0, columns)
        made = nn(xt_ref[...], g_ref[1]).astype(BF16)
        split_rows(made, keep_ref.at[:, span], send_ref.at[:, span], True)
        if beside:
            span = slice(columns, columns + extra)
            made = nn(refs[0][...], refs[1][1]).astype(BF16)
            split_rows(made, keep_ref.at[:, span], send_ref.at[:, span], True)

    out = shaped((width // 2, columns + extra), BF16)
    return call(
        kernel,
        (out, out),
        (x_t, g_qkv, *beside),
        flops=2 * tokens * width * (columns + extra),
    )


def project_own(x_t, g_qkv, beside, small, keep_came, send_came):
    width, tokens = x_t.shape
    columns = g_qkv.shape[2]
    extra = beside[1].shape[2] if beside else 0
    tail = small[0].shape[1] if small else 0
    middle = width // 2
    count = len(beside) + len(small)

    def kernel(xt_ref, g_ref, kc_ref, sc_ref, *refs):
        keep_ref, send_ref = refs[count:]
        for out, came, first in ((keep_ref, kc_ref, 0), (send_ref, sc_ref, middle)):
            rows = slice(first, first + middle)
            span = slice(0, columns)
            made = nn(xt_ref[rows, :], g_ref[0])
            out[:, span] = (made + came[:, span].astype(F32)).astype(BF16)
            if beside:
                span = slice(columns, columns + extra)
                made = nn(refs[0][rows, :], refs[1][0])
                out[:, span] = (made + came[:, span].astype(F32)).astype(BF16)
            if small:
                total = refs[count - 2][rows, :].astype(F32) + refs[count - 1][rows, :].astype(F32)
                out[:, columns + extra :] = total.astype(BF16)

    out = shaped((middle, columns + extra + tail), BF16)
    return call(
        kernel,
        (out, out),
        (x_t, g_qkv, keep_came, send_came, *beside, *small),
        flops=2 * tokens * width * (columns + extra),
    )


def token_back(g_parts, start, perm, weights, cols):
    tokens, width = start.shape
    widths = [part.shape[2] // 3 for part in g_parts]

    def kernel(a_ref, b_ref, start_ref, perm_ref, w_ref, out_ref, g_ref, high_ref, rest_ref):
        for half in range(2):
            for kind in range(3):
                to = kind * cols
                for ref, wide in zip((a_ref, b_ref), widths):
                    taken = ref[half, :, kind * wide : (kind + 1) * wide]
                    g_ref[half, :, to : to + wide] = taken
                    to += wide
        used = slice(0, 3 * cols)

        def matmul(span):
            made = nt(g_ref[0], w_ref[0, span, used]) + nt(g_ref[1], w_ref[1, span, used])
            made = start_ref[:, span] + made
            high = made.astype(BF16)
            high_ref[:, span] = high
            rest_ref[:, span] = (made - high.astype(F32)).astype(BF16)

        columns_of(width, matmul)

        def reorder(span):
            turn = perm_ref[span, :]
            out_ref[:, span] = nt(high_ref[...], turn) + nt(rest_ref[...], turn)

        columns_of(width, reorder)

    return call(
        kernel,
        shaped((tokens, width), F32),
        (*g_parts, start, perm, weights),
        scratch=[
            pltpu.VMEM((2, tokens, 3 * cols), BF16),
            pltpu.VMEM((tokens, width), BF16),
            pltpu.VMEM((tokens, width), BF16),
        ],
        flops=16 * tokens * width * cols,
    )


class Exchange:
    def __init__(self, size):
        self.size = size
        self.depth = size.bit_length() - 1
        self.rank = lax.axis_index("dp")
        self.core = lax.axis_index("tensor")
        outer = list(range(self.depth - 1, 1, -1))
        self.bits = (outer + [1, 0], outer + [0, 1])

    def flip(self, value, step):
        pairs = []
        for i in range(self.size):
            for core in range(2):
                pairs.append((i * 2 + core, (i ^ (1 << self.bits[core][step])) * 2 + core))
        return lax.ppermute(value, ("dp", "tensor"), pairs)

    def blocks(self):
        tables = []
        for bits in self.bits:
            tables.append(
                [
                    sum(((j >> step) & 1) << bit for step, bit in enumerate(bits))
                    for j in range(self.size)
                ]
            )
        table = np.array(tables, np.int32)
        return jnp.where(self.core == 0, table[0], table[1]) ^ self.rank


def join(held, came):
    return jnp.concatenate([held, came], axis=0)


def added(*values):
    total = values[0].astype(F32)
    for value in values[1:]:
        total = total + value.astype(F32)
    return total


def halves(value):
    middle = value.shape[0] // 2
    return value[:middle], value[middle:]


def three_parts(value):
    high = lax.reduce_precision(value, 8, 7)
    rest = value - high
    middle = lax.reduce_precision(rest, 8, 7)
    return (high.astype(BF16), middle.astype(BF16), (rest - middle).astype(BF16))


SMALL = 48
UP = 32


def pack(qkv_w, out_w, emb_w, gains, biases, up_bias):
    rows, cols = out_w.shape
    chunk = gains.shape[1]
    args = (qkv_w, out_w, emb_w, gains, biases, up_bias[None])

    def kernel(*refs):
        one_ref, refs, vec_ref, sems = refs[6], (*refs[:6], *refs[7:13]), refs[13], refs[14]
        copies = []
        for place in range(6):
            copies.append(pltpu.make_async_copy(refs[place], refs[6 + place], sems.at[place]))
        for copy in copies:
            copy.start()
        for copy in copies:
            copy.wait()
        q_ref, o_ref, e_ref, g_ref, b_ref, u_ref = refs[6:]
        for part in range(3):
            one_ref[:, part * cols : (part + 1) * cols] = q_ref[part]
        one_ref[:, 3 * cols : 4 * cols] = o_ref[...]
        vec_ref[...] = jnp.zeros_like(vec_ref)
        vec_ref[0:2, 0:chunk] = g_ref[...]
        vec_ref[2:8, 0:chunk] = b_ref[...]
        vec_ref[0:1, UP : UP + u_ref.shape[1]] = u_ref[...]
        value = vec_ref[...]
        high = value.astype(BF16).astype(F32)
        middle = (value - high).astype(BF16).astype(F32)
        block = [e_ref[...].astype(F32), high, middle, value - high - middle]
        one_ref[:, 4 * cols :] = jnp.concatenate(block, axis=0).astype(BF16)

    return call(
        kernel,
        shaped((rows, 4 * cols + LANES), BF16),
        args,
        in_specs=[pl.BlockSpec(memory_space=pltpu.HBM)] * 6,
        scratch=[pltpu.VMEM(arg.shape, arg.dtype) for arg in args]
        + [pltpu.VMEM((8, LANES), F32), pltpu.SemaphoreType.DMA((6,))],
    )


def spreads(sides, width, hidden, chunk, up_chunk):
    lane = jnp.arange(LANES, dtype=jnp.int32)[:, None]
    column = jnp.arange(width, dtype=jnp.int32)[None]
    up_column = jnp.arange(hidden, dtype=jnp.int32)[None]
    thin, broad = [], []
    for side in sides:
        thin.append((lane < chunk) & (column % (2 * chunk) == side * chunk + lane))
        broad.append((lane >= UP) & (up_column % (2 * up_chunk) == side * up_chunk + lane - UP))
    return jnp.stack(thin).astype(BF16), jnp.stack(broad).astype(BF16)


def unpack(core, pieces, thin, broad, rel, absolute, up_rel, cols):
    width, hidden = thin.shape[2], broad.shape[2]
    count = width // SMALL

    def kernel(core_ref, thin_ref, broad_ref, rel_ref, abs_ref, up_ref, *refs):
        vec_ref, head_ref, side_ref, proj_ref, e_ref, sems = refs[8:]
        copies = load_weights(refs[:8], e_ref, sems, 4 * cols, 4 * cols + LANES)
        for copy in copies:
            copy.wait()
        first = core_ref[0] == 0
        blocks = [e_ref[side].astype(F32).reshape(count, SMALL, LANES) for side in range(2)]
        tops = [block[:, : SMALL // 2] for block in blocks]
        halves = [jnp.where(first, tops[0], tops[1]), jnp.where(first, tops[1], tops[0])]
        proj_ref[...] = jnp.concatenate(halves, axis=1).reshape(width, LANES).astype(BF16)
        flat = lax.broadcasted_iota(jnp.int32, (count, count * 8), 1)
        pick = flat == 8 * lax.broadcasted_iota(jnp.int32, (count, count * 8), 0)
        pick = pick.astype(F32).astype(BF16)
        vec = jnp.zeros((8, width), F32)
        plain = jnp.zeros((8, width), F32)
        wide = jnp.zeros((1, hidden), F32)
        index = lax.broadcasted_iota(jnp.int32, (count, hidden), 0)
        for side in range(2):
            placed, up_placed = None, None
            for part in (2, 1, 0):
                start = SMALL // 2 + 8 * part
                rows = blocks[side][:, start : start + 8].reshape(count * 8, LANES).astype(BF16)
                spread = nn(rows, thin_ref[side])
                up_spread = nn(nn(pick, rows).astype(BF16), broad_ref[side])
                placed = spread if placed is None else placed + spread
                up_placed = up_spread if up_placed is None else up_placed + up_spread
            for j in range(count):
                row = placed[8 * j : 8 * j + 8]
                vec = vec + jnp.where(rel_ref[...] == j, row, 0.0)
                plain = plain + jnp.where(abs_ref[...] == j, row, 0.0)
            chosen = jnp.where(up_ref[...] == index, up_placed, 0.0)
            wide = wide + jnp.sum(chosen, axis=0, keepdims=True)
        vec_ref[...] = vec
        for side in range(2):
            low_half = first if side == 0 else jnp.logical_not(first)
            part = jnp.where(low_half, plain[:, :cols], plain[:, cols:])
            head_ref[side : side + 1, :cols] = part[2:3]
            head_ref[side : side + 1, cols : 2 * cols] = jnp.zeros((1, cols), F32)
            head_ref[side : side + 1, 2 * cols :] = part[3:4]
            middle = hidden // 2
            side_ref[side : side + 1, :] = jnp.where(low_half, wide[:, :middle], wide[:, middle:])

    outs = (
        shaped((8, width), F32),
        shaped((2, 3 * cols), F32),
        shaped((2, hidden // 2), F32),
        shaped((width, LANES), BF16),
    )
    return call(
        kernel,
        outs,
        (core[None], thin, broad, rel, absolute, up_rel, *pieces),
        in_specs=[pl.BlockSpec(memory_space=pltpu.SMEM)] + [WHOLE] * 5 + [ANY] * 8,
        scratch=[pltpu.VMEM((2, width, LANES), BF16), pltpu.SemaphoreType.DMA((2, 4))],
    )


def pack_grads(
    core, thin, broad, rel, absolute, up_rel, sums_one, sums_two, up_own, up_other, qkv_a, qkv_b,
    proj_grad,
):
    width, hidden = thin.shape[2], broad.shape[2]
    count = width // SMALL

    def kernel(
        core_ref, thin_ref, broad_ref, rel_ref, abs_ref, up_ref, one_ref, two_ref, uo_ref, ux_ref,
        qa_ref, qb_ref, pg_ref, own_ref, other_ref,
    ):
        first = core_ref[0] == 0
        fold = lambda v: jnp.sum(v, axis=0, keepdims=True)

        def ordered(own, other):
            low, high = jnp.where(first, own, other), jnp.where(first, other, own)
            return jnp.concatenate([low, high], axis=1)

        def heads(half, kind):
            return jnp.concatenate([fold(qa_ref[half, kind]), fold(qb_ref[half, kind])], axis=1)

        rows = [
            fold(one_ref[0:8]),
            fold(two_ref[0:8]),
            ordered(heads(0, 0), heads(1, 0)),
            ordered(heads(0, 1), heads(1, 1)),
            fold(one_ref[16:24]),
            fold(one_ref[8:16]),
            fold(two_ref[16:24]),
            fold(two_ref[8:16]),
        ]
        grads = jnp.concatenate(rows, axis=0)
        row = lax.broadcasted_iota(jnp.int32, (8, width), 0)
        block = jnp.where((row == 2) | (row == 3), abs_ref[...], rel_ref[...])
        spread = [jnp.where(block == j, grads, 0.0) for j in range(count)]
        spread = jnp.concatenate(spread, axis=0)
        high = spread.astype(BF16)
        rest = (spread - high.astype(F32)).astype(BF16)
        up = ordered(fold(uo_ref[...]), fold(ux_ref[...]))
        index = lax.broadcasted_iota(jnp.int32, (count, hidden), 0)
        up = jnp.where(up_ref[...] == index, up, 0.0)
        up_high = up.astype(BF16)
        up_rest = (up - up_high.astype(F32)).astype(BF16)
        flat = lax.broadcasted_iota(jnp.int32, (count * 8, count), 0)
        put = flat == 8 * lax.broadcasted_iota(jnp.int32, (count * 8, count), 1)
        put = put.astype(F32).astype(BF16)
        tops = pg_ref[...].reshape(count, SMALL, LANES)
        for side, out_ref in enumerate((own_ref, other_ref)):
            low_half = first if side == 0 else jnp.logical_not(first)
            top = jnp.where(low_half, tops[:, : SMALL // 2], tops[:, SMALL // 2 :])
            thin_part = nt(high, thin_ref[side]) + nt(rest, thin_ref[side])
            up_part = nt(up_high, broad_ref[side]) + nt(up_rest, broad_ref[side])
            vec = (thin_part + nn(put, up_part.astype(BF16))).reshape(count, 8, LANES)
            blank = jnp.zeros((count, SMALL // 2 - 8, LANES), F32)
            made = jnp.concatenate([top, vec, blank], axis=1).reshape(width, LANES).astype(BF16)
            quarter = width // 4
            for place in range(4):
                source = OTHER[place] if side == 1 else place
                out_ref[place * quarter : (place + 1) * quarter, :] = made[
                    source * quarter : (source + 1) * quarter
                ]

    out = shaped((width, LANES), BF16)
    return call(
        kernel,
        (out, out),
        (
            core[None], thin, broad, rel, absolute, up_rel, sums_one, sums_two, up_own, up_other,
            qkv_a, qkv_b, proj_grad,
        ),
        in_specs=[pl.BlockSpec(memory_space=pltpu.SMEM)] + [WHOLE] * 12,
    )


def finish(a_kept, a_came, b_kept, b_came, cols, chunk, up_chunk, emb_shape):
    rows = a_kept.shape[0]
    a_wide = (a_kept.shape[1] - cols) // 3
    b_wide = cols - a_wide

    def kernel(
        ak_ref, ac_ref, bk_ref, bc_ref, qkv_ref, out_ref, emb_ref, gain_ref, bias_ref, up_ref,
        a_ref, b_ref,
    ):
        a_ref[...] = ak_ref[...] + ac_ref[...].astype(F32)
        b_ref[...] = bk_ref[...] + bc_ref[...].astype(F32)
        for part in range(3):
            qkv_ref[part, :, :a_wide] = a_ref[:, part * a_wide : (part + 1) * a_wide]
            qkv_ref[part, :, a_wide:] = b_ref[:, part * b_wide : (part + 1) * b_wide]
        out_ref[...] = a_ref[:, 3 * a_wide :]
        first = 3 * b_wide
        half = SMALL // 2
        emb_ref[...] = b_ref[0:half, first:]
        gain_ref[...] = b_ref[half : half + 2, first : first + chunk]
        bias_ref[...] = b_ref[half + 2 : half + 8, first : first + chunk]
        up_ref[...] = b_ref[half : half + 1, first + UP : first + UP + up_chunk]

    outs = (
        shaped((3, rows, cols), F32),
        shaped((rows, cols), F32),
        shaped(emb_shape, F32),
        shaped((2, chunk), F32),
        shaped((6, chunk), F32),
        shaped((1, up_chunk), F32),
    )
    return call(
        kernel,
        outs,
        (a_kept, a_came, b_kept, b_came),
        scratch=[pltpu.VMEM(a_kept.shape, F32), pltpu.VMEM(b_kept.shape, F32)],
    )


def pack_plain(qkv_w, out_w, emb_w, gains, biases, up_bias):
    rows = out_w.shape[0]
    vector = jnp.concatenate([gains.reshape(-1), biases.reshape(-1), up_bias])
    pad_to = -(-vector.size // LANES) * LANES
    padded = jnp.pad(vector, (0, pad_to - vector.size))
    flat = jnp.concatenate([emb_w.reshape(-1), *three_parts(padded)])
    extra = -(-flat.size // (rows * LANES)) * LANES
    flat = jnp.pad(flat, (0, rows * extra - flat.size)).reshape(rows, extra)
    one = jnp.concatenate([qkv_w[0], qkv_w[1], qkv_w[2], out_w, flat], axis=1)
    sizes = (rows, extra, emb_w.size, gains.shape[1], up_bias.size, pad_to)
    return one, sizes


def unpack_plain(core, sides, pieces, blocks, sizes):
    rows, extra, emb_size, chunk, up_chunk, pad_to = sizes
    size = blocks.shape[0]
    width = size * rows
    cols = width // 2
    ff_local = size * up_chunk
    pieces = [part[:, 4 * cols :] for part in pieces]
    own = jnp.concatenate(pieces[:4])
    other = jnp.concatenate([pieces[4 + place] for place in OTHER])
    small = [part.reshape(size, rows * extra) for part in (own, other)]
    small = jnp.where(core == 0, jnp.stack(small, 1), jnp.stack(small[::-1], 1))
    proj = small[:, :, :emb_size].reshape(width, -1)
    thirds = small[:, :, emb_size : emb_size + 3 * pad_to].astype(F32)
    thirds = thirds.reshape(size, 2, 3, pad_to)
    vectors = thirds[:, :, 0] + (thirds[:, :, 1] + thirds[:, :, 2])
    plain = vectors[jnp.argsort(blocks)].reshape(size * 2, pad_to)
    vectors = vectors.reshape(size * 2, pad_to)
    vec = jnp.moveaxis(vectors[:, : 8 * chunk].reshape(-1, 8, chunk), 1, 0).reshape(8, width)
    query_bias = plain[:, 2 * chunk : 3 * chunk].reshape(-1)
    value_bias = plain[:, 3 * chunk : 4 * chunk].reshape(-1)
    up_bias = plain[:, 8 * chunk : 8 * chunk + up_chunk].reshape(-1)
    head_bias, side_bias = [], []
    for side in sides:
        query_part = lax.dynamic_slice_in_dim(query_bias, side * cols, cols)
        value_part = lax.dynamic_slice_in_dim(value_bias, side * cols, cols)
        head_bias.append(jnp.concatenate([query_part, jnp.zeros_like(query_part), value_part]))
        side_bias.append(lax.dynamic_slice_in_dim(up_bias, side * ff_local, ff_local))
    return vec, jnp.stack(head_bias), jnp.stack(side_bias), proj


def pack_grads_plain(
    core, blocks, sizes, sums_one, sums_two, up_own, up_other, qkv_a, qkv_b, proj_grad
):
    rows, extra, emb_size, chunk, up_chunk, pad_to = sizes
    size = blocks.shape[0]

    def fold(value):
        return jnp.sum(value.reshape(-1, 8, value.shape[-1]), axis=1)

    def absolute(own, other):
        return jnp.where(
            core == 0, jnp.concatenate([own, other]), jnp.concatenate([other, own])
        )

    def relative(value):
        return value.reshape(size, 2, -1)[blocks]

    gain_two, shift_two, ffn_bias = (row.reshape(size, 2, chunk) for row in fold(sums_two))
    gain_one, shift_one, out_bias = (row.reshape(size, 2, chunk) for row in fold(sums_one))
    own, other = jnp.sum(jnp.concatenate([qkv_a, qkv_b], axis=3), axis=2)
    small = jnp.concatenate(
        [
            proj_grad.reshape(size, 2, emb_size),
            gain_one,
            gain_two,
            relative(absolute(own[0], other[0])),
            relative(absolute(own[1], other[1])),
            out_bias,
            shift_one,
            ffn_bias,
            shift_two,
            relative(absolute(fold(up_own)[0], fold(up_other)[0])),
        ],
        axis=2,
    ).astype(BF16)
    small = jnp.pad(small, ((0, 0), (0, 0), (0, rows * extra - small.shape[2])))
    small = jnp.where(core == 0, small, small[:, ::-1])
    own, other = jnp.moveaxis(small, 1, 0).reshape(2, size * rows, extra)
    first, second, third, fourth = jnp.split(other, 4)
    return own, jnp.concatenate([first, third, second, fourth])


def body(
    tokens,
    lengths,
    key_mask,
    order,
    query_key_value_weight,
    output_projection_weight,
    up_projection_weight,
    down_projection_weight,
    embedding_projection_weight,
    gains,
    biases,
    up_bias_vector,
    cotangent,
):
    size = lax.axis_size("dp")
    core = lax.axis_index("tensor")
    ways = Exchange(size)
    depth = ways.depth
    half_len = tokens.shape[1]
    full_len = key_mask.shape[1]
    width = tokens.shape[2]
    cols = output_projection_weight.shape[0]
    rows = output_projection_weight.shape[1]
    ff_local = up_projection_weight.shape[1]
    chunk = gains.shape[1]
    emb_size = embedding_projection_weight.size
    sides = (core, 1 - core)

    fast = rows == SMALL and emb_size == SMALL // 2 * LANES and up_bias_vector.size <= LANES - UP
    small_args = (
        query_key_value_weight,
        output_projection_weight.T,
        embedding_projection_weight,
        gains,
        biases,
        up_bias_vector,
    )
    if fast:
        one = pack(*small_args)
    else:
        one, small_sizes = pack_plain(*small_args)

    wide = 4 * cols
    seconds, lasts = depth - 2, depth - 1
    for step in range(depth - 3):
        one = join(one, ways.flip(one, step))
    tokens, order, lengths, key_mask = after((tokens, order, lengths, key_mask), one)
    mine = order[0, core]
    theirs = order[0, 1 - core]
    my_half = lax.dynamic_index_in_dim(tokens, mine, 0, keepdims=False)
    their_half = lax.dynamic_index_in_dim(tokens, theirs, 0, keepdims=False)
    blocks = ways.blocks()
    one_came = ways.flip(one, depth - 3)
    if fast:
        thin, broad = spreads(sides, width, 2 * ff_local, chunk, up_bias_vector.size)
        places_of = jnp.argsort(blocks)
        rel = (jnp.arange(width, dtype=jnp.int32) // rows)[None]
        absolute = jnp.repeat(places_of, rows)[None].astype(jnp.int32)
        up_rel = jnp.repeat(places_of, 2 * up_bias_vector.size)[None].astype(jnp.int32)
        one_came, thin, broad, rel, absolute, up_rel = together(
            one_came, thin, broad, rel, absolute, up_rel
        )
        tables = (core, thin, broad, rel, absolute, up_rel)

    def in_order(own, other):
        return jnp.where(
            core == 0, jnp.concatenate([own, other]), jnp.concatenate([other, own])
        )

    def half_of(value, which):
        return lax.dynamic_slice_in_dim(value, which * half_len, half_len)

    seq_len = lengths[mine]
    marks = lax.dynamic_index_in_dim(key_mask, mine, 0, keepdims=False)
    places = jnp.arange(full_len, dtype=jnp.int32)
    key_ok = (places < seq_len) & ((marks == 1) | (places == 0))
    mask = jnp.where(key_ok, 0.0, -1e30).astype(F32)[None, :]
    where = (blocks[:, None] * rows + jnp.arange(rows, dtype=jnp.int32)[None]).reshape(-1)
    perm = (jnp.arange(width, dtype=jnp.int32)[:, None] == where[None]).astype(BF16)
    two, three = after((up_projection_weight, down_projection_weight.T), order)
    for step in range(depth - 4):
        two = join(two, ways.flip(two, step))
        three = join(three, ways.flip(three, step))
    two_came = ways.flip(two, depth - 4)
    one_came, two_came = together(one_came, two_came)
    one = join(one, one_came)
    two = join(two, two_came)
    here = in_order(my_half, swap_cores(after(their_half, one)))
    one_b, one_c, two_came, three_came, here, mask, perm = together(
        ways.flip(one, seconds),
        ways.flip(one, lasts),
        ways.flip(two, depth - 3),
        ways.flip(after(three, two), depth - 4),
        here,
        mask,
        perm,
    )
    two = join(two, two_came)
    three = join(three, three_came)
    one_d, two_b, three_came, *one_other = together(
        ways.flip(one_b, lasts),
        ways.flip(two, seconds),
        ways.flip(three, depth - 3),
        swap_cores(one),
        swap_cores(one_b),
        swap_cores(one_c),
    )
    three = join(three, three_came)
    two_both = join(two, two_b)
    one_pieces = (one, one_b, one_c, one_d, *one_other, swap_cores(one_d))
    two_more, three_b = ways.flip(two_both, lasts), ways.flip(three, seconds)
    one_pieces = together(*one_pieces, two_both, three)[:8]
    if fast:
        vec, head_bias, side_bias, proj = unpack(core, one_pieces, *tables[1:], cols)
    else:
        vec, head_bias, side_bias, proj = unpack_plain(
            core, sides, one_pieces, blocks, small_sizes
        )
    side_bias = (side_bias[0:1], side_bias[1:2])

    qkv, lse, att, res_one, first, first_low, first_low_t, here_t, weights = attention_forward(
        here, perm, head_bias, mask, vec, one_pieces, cols
    )
    two_more, three_b = after((two_more, three_b), first_low)
    three_both = join(three, three_b)
    three_more = ways.flip(three_both, lasts)
    two_other = [swap_cores(part) for part in (two_both, two_more)]

    def quarters(both, more):
        return ((both, 0), (both, 1), (more, 0), (more, 1))

    two_own = quarters(two_both, two_more)
    hid_own, slope_own = up_forward(
        after(first_low, three_both, two_more), two_own, side_bias[0], False
    )
    two_other = quarters(*after(two_other, hid_own))
    three_both_other = swap_cores(three_both)
    hid_other, slope_other = up_forward(first_low, two_other, side_bias[1], True)
    three_more, three_both_other = after((three_more, three_both_other), hid_other)
    cot_mine = lax.dynamic_index_in_dim(cotangent, core, 0, keepdims=False)
    cot_other = lax.dynamic_index_in_dim(cotangent, 1 - core, 0, keepdims=False)
    cot = in_order(cot_mine, after(swap_cores(cot_other), hid_other))
    three_own = quarters(three_both, three_more)
    three_other = quarters(three_both_other, swap_cores(three_more))
    emb, g_ffn, g_ffn_t, g_res_two, proj_grad, sums_two = down_both(
        seq_len[None], (hid_own, hid_other), (*three_own, *three_other), first, vec, proj, cot
    )

    def low(*values):
        return added(*values).astype(BF16)

    def spread(value):
        kept, sent = halves(value)
        return kept, sent.astype(BF16)

    dk_other, ds_other = down_grad(g_ffn_t, hid_other, True)
    ds_came, dk_came = swap_cores(ds_other), swap_cores(dk_other)
    dk, ds = down_grad(g_ffn_t, after(hid_own, ds_other), False)
    ds_came, dk_came = after((ds_came, dk_came), ds)
    d_sent = low(ds, ds_came)
    d_came = ways.flip(d_sent, lasts)
    uk_other, us_other, up_bias_other, part = up_grad(
        after(g_ffn, d_sent),
        first_low_t,
        slope_other,
        three_other,
        two_other,
        g_res_two,
        True,
    )
    us_came, uk_came = swap_cores(us_other), swap_cores(uk_other)
    d_came = after(d_came, us_other)
    d_sent = low(halves(dk)[1], halves(dk_came)[1], halves(d_came)[1])
    d_held = added(halves(dk)[0], halves(dk_came)[0], halves(d_came)[0])
    d_came = ways.flip(d_sent, seconds)
    uk, us, up_bias_own, g_first = up_grad(
        after(g_ffn, us_other, d_sent),
        first_low_t,
        slope_own,
        three_own,
        two_own,
        part,
        False,
    )
    d_came, us_came, uk_came = after((d_came, us_came, uk_came), us)
    u_sent = low(us, us_came)
    u_came = ways.flip(u_sent, lasts)
    d_held, d_sent = spread(d_held + d_came.astype(F32))
    d_came = ways.flip(d_sent, depth - 3)
    g_res_one, g_branch_t, g_att, sums_one = norm_back(
        after(g_first, u_sent, d_sent), res_one, vec, weights, cols
    )
    pairs = list(range(cols // LANES))
    split = (len(pairs) + 1) // 2
    g_a, bias_a = attention_back(pairs[:split], g_att, att, qkv, lse, mask)
    beside = (g_branch_t, att)
    ak_other, as_other = project_other(here_t, g_a, beside)
    as_came, ak_came = swap_cores(as_other), swap_cores(ak_other)
    g_b, bias_b = attention_back(pairs[split:], after(g_att, as_other), att, qkv, lse, mask)
    as_came, ak_came = after((as_came, ak_came), g_b)
    a_keep, a_send = project_own(here_t, g_a, beside, (), ak_came, as_came)
    d_came, u_came = after((d_came, u_came), a_send)
    a_came = ways.flip(a_send, lasts)
    u_sent = low(halves(uk)[1], halves(uk_came)[1], halves(u_came)[1])
    u_held = added(halves(uk)[0], halves(uk_came)[0], halves(u_came)[0])
    u_came = ways.flip(u_sent, seconds)
    d_held, d_sent = spread(d_held + d_came.astype(F32))
    d_came = ways.flip(d_sent, depth - 4)
    bk_other, bs_other = project_other(here_t, after(g_b, a_send, u_sent, d_sent), ())
    bs_came, bk_came = swap_cores(bs_other), swap_cores(bk_other)
    if fast:
        small_own, small_other = pack_grads(
            *tables, sums_one, after(sums_two, bs_other), up_bias_own, up_bias_other, bias_a,
            bias_b, proj_grad,
        )
    else:
        small_own, small_other = pack_grads_plain(
            core, blocks, small_sizes, sums_one, sums_two, up_bias_own, up_bias_other, bias_a,
            bias_b, proj_grad,
        )
    small_came = swap_cores(small_other)
    bs_came, bk_came = after((bs_came, bk_came), small_other)
    b_keep, b_send = project_own(here_t, g_b, (), (small_own, small_came), bk_came, bs_came)
    d_came, u_came, a_came = after((d_came, u_came, a_came), b_send)
    b_came = ways.flip(b_send, lasts)
    a_sent = low(halves(a_keep)[1], halves(a_came)[1])
    a_held = added(halves(a_keep)[0], halves(a_came)[0])
    a_came = ways.flip(a_sent, seconds)
    u_held, u_sent = spread(u_held + u_came.astype(F32))
    u_came = ways.flip(u_sent, depth - 3)
    d_held = d_held + d_came.astype(F32)
    g_here = token_back(
        (after(g_a, b_send, a_sent, u_sent), g_b), g_res_one, perm, weights, cols
    )
    a_came, b_came, u_came = after((a_came, b_came, u_came), g_here)
    b_sent = low(halves(b_keep)[1], halves(b_came)[1])
    b_held = added(halves(b_keep)[0], halves(b_came)[0])
    b_came = ways.flip(b_sent, seconds)
    a_held, a_sent = spread(a_held + a_came.astype(F32))
    a_came = ways.flip(a_sent, depth - 3)
    u_held, u_sent = spread(u_held + u_came.astype(F32))
    u_came = ways.flip(u_sent, depth - 4)
    for step in range(depth - 5, -1, -1):
        d_held, sent = spread(d_held)
        d_held = d_held + ways.flip(sent, step).astype(F32)
        u_held, sent = spread(u_held + u_came.astype(F32))
        u_came = ways.flip(sent, step)
    down_shard, up_shard = d_held, u_held + u_came.astype(F32)
    b_held, b_sent = spread(b_held + b_came.astype(F32))
    b_came = ways.flip(b_sent, depth - 3)
    for step in range(depth - 4, -1, -1):
        a_held, sent = spread(a_held + a_came.astype(F32))
        a_came = ways.flip(sent, step)
        b_held, sent = spread(b_held + b_came.astype(F32))
        b_came = ways.flip(sent, step)
    if fast:
        qkv_shard, out_shard, emb_shard, gain_shard, bias_shard, up_bias_shard = finish(
            a_held,
            a_came,
            b_held,
            b_came,
            cols,
            chunk,
            up_bias_vector.size,
            embedding_projection_weight.shape,
        )
        out_shard, up_bias_shard = out_shard.T, up_bias_shard[0]
    else:
        a_shard = a_held + a_came.astype(F32)
        b_shard = b_held + b_came.astype(F32)
        a_wide, b_wide = split * LANES, (len(pairs) - split) * LANES
        qkv_shard = jnp.stack(
            [
                jnp.concatenate(
                    [
                        a_shard[:, i * a_wide : (i + 1) * a_wide],
                        b_shard[:, i * b_wide : (i + 1) * b_wide],
                    ],
                    axis=1,
                )
                for i in range(3)
            ]
        )
        out_shard = a_shard[:, 3 * a_wide :].T
        tail = b_shard[:, 3 * b_wide :].reshape(-1)
        emb_shard = tail[:emb_size].reshape(embedding_projection_weight.shape)
        tail = tail[emb_size:]
        gain_shard = tail[: 2 * chunk].reshape(2, chunk)
        bias_shard = tail[2 * chunk : 8 * chunk].reshape(6, chunk)
        up_bias_shard = tail[8 * chunk : 8 * chunk + up_bias_vector.size]

    def give_back(value, places_of):
        own = half_of(value, core)
        other = swap_cores(half_of(value, 1 - core))
        blank = jnp.zeros((2,) + own.shape, value.dtype)
        blank = lax.dynamic_update_slice(blank, own[None], (places_of[0], 0, 0))
        return lax.dynamic_update_slice(blank, other[None], (places_of[1], 0, 0))

    embeddings = give_back(emb, (core, 1 - core))
    grad_tokens = give_back(g_here, (mine, theirs))
    return (
        embeddings,
        grad_tokens,
        qkv_shard,
        out_shard,
        up_shard,
        down_shard.T,
        emb_shard,
        gain_shard,
        bias_shard,
        up_bias_shard,
    )


def solution(mesh):
    return jax.shard_map(
        body,
        mesh=mesh,
        in_specs=(
            P("dp", "tensor", None),
            P("dp"),
            P("dp", None),
            P("dp", None),
            P(None, "dp", "tensor"),
            P("tensor", "dp"),
            P("dp", "tensor"),
            P("tensor", "dp"),
            P(("dp", "tensor"), None),
            P(None, ("dp", "tensor")),
            P(None, ("dp", "tensor")),
            P(("dp", "tensor")),
            P("dp", "tensor", None),
        ),
        out_specs=(
            P("dp", "tensor", None),
            P("dp", "tensor", None),
            P(None, "dp", "tensor"),
            P("tensor", "dp"),
            P("dp", "tensor"),
            P("tensor", "dp"),
            P(("dp", "tensor"), None),
            P(None, ("dp", "tensor")),
            P(None, ("dp", "tensor")),
            P(("dp", "tensor")),
        ),
        check_vma=False,
    )
```

```python
import functools

import jax
import jax.numpy as jnp
import numpy as np
from jax import lax
from jax.experimental import pallas as pl
from jax.experimental.pallas import tpu as pltpu
from jax.sharding import PartitionSpec as P

HD = 64
LANES = 128
STRIP = 128
F32 = jnp.float32
BF16 = jnp.bfloat16
VMEM_LIMIT = 18 * 1024 * 1024


def nn(left, right):
    return lax.dot_general(left, right, (((1,), (0,)), ((), ())), preferred_element_type=F32)


def nt(left, right):
    return lax.dot_general(left, right, (((1,), (1,)), ((), ())), preferred_element_type=F32)


def swap_cores(value):
    return lax.ppermute(value, "tensor", [(0, 1), (1, 0)])


def after(value, *others):
    return lax.optimization_barrier((value, others))[0]


def together(*values):
    return lax.optimization_barrier(values)


def strips(count, size, step):
    def run(i, carry):
        step(pl.ds(pl.multiple_of(i * size, size), size))
        return carry

    lax.fori_loop(0, count // size, run, 0)


def columns_of(width, step):
    block = 256 if width % 256 == 0 else width

    def run(i, carry):
        step(pl.ds(pl.multiple_of(i * block, block), block))
        return carry

    lax.fori_loop(0, width // block, run, 0)


def call(
    body, outs, args, grid=None, in_specs=None, out_specs=None, scratch=(), flops=0, grant=VMEM_LIMIT
):
    whole = pl.BlockSpec(memory_space=pltpu.VMEM)
    return pl.pallas_call(
        body,
        out_shape=outs,
        grid=grid or (),
        in_specs=in_specs or [whole] * len(args),
        out_specs=out_specs or jax.tree.map(lambda _: whole, outs),
        scratch_shapes=scratch,
        compiler_params=pltpu.CompilerParams(vmem_limit_bytes=grant),
        cost_estimate=pl.CostEstimate(flops=flops, bytes_accessed=1 << 20, transcendentals=0),
    )(*args)


def shaped(shape, dtype):
    return jax.ShapeDtypeStruct(shape, dtype)


ANY = pl.BlockSpec(memory_space=pl.ANY)
WHOLE = pl.BlockSpec(memory_space=pltpu.VMEM)


OTHER = (0, 2, 1, 3)


def load_weights(pieces, target, sems, first=0, last=None, at=(0,) * 8):
    quarter = target.shape[1] // 4
    columns = slice(first, last)
    copies = []
    for side in range(2):
        for place in range(4):
            source = place if side == 0 else 4 + OTHER[place]
            rows = pl.ds(at[source] * quarter, quarter)
            copies.append(
                pltpu.make_async_copy(
                    pieces[source].at[rows, columns],
                    target.at[side, pl.ds(place * quarter, quarter)],
                    sems.at[side, place],
                )
            )
    for copy in copies:
        copy.start()
    return copies


def attention_kernel(
    x_ref, perm_ref, bias_ref, mask_ref, vec_ref, *refs
):
    pieces, refs = refs[:8], refs[8:]
    qkv_ref, lse_ref, att_ref, res_ref, first_ref, low_ref, lowt_ref, xt_ref, w_ref = refs[:9]
    col_ref, rel_ref, sems = refs[9:]
    cols = qkv_ref.shape[2] // 3
    tokens = x_ref.shape[0]
    copies = load_weights(pieces, w_ref, sems, 0, 4 * cols)

    def reorder(span):
        rel_ref[:, span] = nn(x_ref[...], perm_ref[:, span]).astype(BF16)

    columns_of(x_ref.shape[1], reorder)
    xt_ref[...] = rel_ref[...].T
    col_ref[...] = jnp.broadcast_to(mask_ref[...], (LANES, tokens)).T
    for copy in copies:
        copy.wait()

    def project(i, carry):
        half, part = i // 3, i % 3
        span = pl.ds(pl.multiple_of(part * cols, cols), cols)
        made = nn(rel_ref[...], w_ref[half, :, span]) + bias_ref[pl.ds(half, 1), span]
        qkv_ref[half, :, span] = made.astype(BF16)
        return carry

    lax.fori_loop(0, 6, project, 0)
    lane = lax.broadcasted_iota(jnp.int32, (tokens, LANES), 1) < HD
    pairs = cols // LANES


    def pair(step, carry):
        half, i = step // pairs, step % pairs
        off = pl.multiple_of(i * LANES, LANES)
        query = qkv_ref[half, :, pl.ds(off, LANES)] * BF16(HD ** (-0.5))
        key = qkv_ref[half, :, pl.ds(pl.multiple_of(cols + off, LANES), LANES)]
        value = qkv_ref[half, :, pl.ds(pl.multiple_of(2 * cols + off, LANES), LANES)]
        value_t = value.T
        outs = []
        for head in range(2):
            kept = jnp.where(lane == (head == 0), key, jnp.zeros_like(key))
            scores = nt(kept, query)
            scores = scores + jnp.concatenate([col_ref[...]] * (tokens // LANES), axis=1)
            top = jnp.max(scores, axis=0, keepdims=True)
            shifted = jnp.exp(scores - top)
            total = jnp.sum(shifted, axis=0, keepdims=True)
            out = nn(value_t[head * HD : (head + 1) * HD], shifted.astype(BF16))
            outs.append(out / total)
            lse_ref[half, pl.ds(i * 2 + head, 1), :] = top + jnp.log(total)
        both = jnp.concatenate(outs, axis=0).T
        att_ref[half, :, pl.ds(off, LANES)] = both.astype(BF16)
        return carry

    lax.fori_loop(0, 2 * pairs, pair, 0)
    out = slice(3 * cols, 4 * cols)

    def branch(span):
        made = nt(att_ref[0], w_ref[0, span, out]) + nt(att_ref[1], w_ref[1, span, out])
        res_ref[:, span] = made

    columns_of(x_ref.shape[1], branch)

    def norm(rows):
        value = res_ref[rows, :] + vec_ref[4:5, :] + rel_ref[rows, :].astype(F32)
        res_ref[rows, :] = value
        average = jnp.mean(value, axis=-1, keepdims=True)
        centred = value - average
        inverse = lax.rsqrt(jnp.mean(centred * centred, axis=-1, keepdims=True) + 1e-12)
        first = centred * inverse * vec_ref[0:1, :] + vec_ref[5:6, :]
        first_ref[rows, :] = first
        low_ref[rows, :] = first.astype(BF16)

    strips(tokens, STRIP, norm)
    lowt_ref[...] = low_ref[...].T


def attention_forward(x, perm, head_bias, mask, vec, pieces, cols):
    tokens, width = x.shape
    heads = cols // HD
    outs = (
        shaped((2, tokens, 3 * cols), BF16),
        shaped((2, heads, tokens), F32),
        shaped((2, tokens, cols), BF16),
        shaped((tokens, width), F32),
        shaped((tokens, width), F32),
        shaped((tokens, width), BF16),
        shaped((width, tokens), BF16),
        shaped((width, tokens), BF16),
        shaped((2, width, 4 * cols), BF16),
    )
    return call(
        attention_kernel,
        outs,
        (x, perm, head_bias, mask, vec, *pieces),
        in_specs=[WHOLE] * 5 + [ANY] * 8,
        scratch=[
            pltpu.VMEM((tokens, LANES), F32),
            pltpu.VMEM((tokens, width), BF16),
            pltpu.SemaphoreType.DMA((2, 4)),
        ],
        flops=8 * tokens * width * width,
    )


ERF = (0.254829592, -0.284496736, 1.421413741, -1.453152027, 1.061405429)


def gelu_pair(value):
    size = jnp.abs(value)
    bell = jnp.exp(-0.5 * value * value)
    t = 1.0 / (1.0 + (0.3275911 * 0.5**0.5) * size)
    poly = ERF[4]
    for term in ERF[3::-1]:
        poly = poly * t + term
    tail = 0.5 * poly * t * bell
    phi = jnp.where(value >= 0, 1.0 - tail, tail)
    return value * phi, phi + value * bell * 0.3989422804014327


def join_rows(refs, target, swapped):
    quarter = target.shape[0] // 4
    for place in range(4):
        source = OTHER[place] if swapped else place
        target[place * quarter : (place + 1) * quarter, :] = refs[source][...]


def split_rows(value, keep_ref, send_ref, swapped):
    quarter = value.shape[0] // 4
    for place in range(4):
        source = OTHER[place] if swapped else place
        ref = (keep_ref, send_ref)[place // 2]
        rows = slice((place % 2) * quarter, (place % 2 + 1) * quarter)
        ref[rows, :] = value[source * quarter : (source + 1) * quarter, :]


def column_block(hidden):
    return 512 if hidden % 512 == 0 else hidden


def up_forward(low, pieces, bias, swapped):
    tokens, width = low.shape
    pieces, at = zip(*pieces)
    hidden = pieces[0].shape[1]
    block = column_block(hidden)

    def kernel(low_ref, a_ref, b_ref, c_ref, d_ref, bias_ref, hid_ref, slope_ref, acc_ref, w_ref):
        join_rows((a_ref, b_ref, c_ref, d_ref), w_ref, swapped)
        acc_ref[...] = nn(low_ref[...], w_ref[...])

        def act(rows):
            active, slope = gelu_pair(acc_ref[rows, :] + bias_ref[...])
            hid_ref[rows, :] = active.astype(BF16)
            slope_ref[rows, :] = slope.astype(BF16)

        strips(tokens, STRIP, act)

    outs = (shaped((tokens, hidden), BF16), shaped((tokens, hidden), BF16))
    chunk = pl.BlockSpec((tokens, block), lambda i: (0, i))
    parts = [pl.BlockSpec((width // 4, block), lambda i, row=row: (row, i)) for row in at]
    return call(
        kernel,
        outs,
        (low, *pieces, bias),
        grid=(hidden // block,),
        in_specs=[
            pl.BlockSpec((tokens, width), lambda i: (0, 0)),
            *parts,
            pl.BlockSpec((1, block), lambda i: (0, i)),
        ],
        out_specs=(chunk, chunk),
        scratch=[pltpu.VMEM((tokens, block), F32), pltpu.VMEM((width, block), BF16)],
        flops=2 * tokens * width * hidden,
    )


def down_kernel(
    len_ref, h0_ref, h1_ref, first_ref, vec_ref, proj_ref, cot_ref, *refs
):
    both_ref, more_ref, both_other, more_other, *refs = refs
    emb_ref, low_ref, lowt_ref, res_ref, pgrad_ref, sums_ref = refs[:6]
    ffn_ref, norm_ref, sec_ref, gp_ref, gs_ref, inv_ref, prj_ref, w_ref = refs[6:]
    tokens = first_ref.shape[0]
    length = len_ref[0]
    quarter = w_ref.shape[0] // 4
    for place, ref, part in ((0, both_other, 0), (1, more_other, 0), (2, both_other, 1), (3, more_other, 1)):
        w_ref[place * quarter : (place + 1) * quarter] = ref[part * quarter : (part + 1) * quarter]
    for ref, first in ((both_ref, 0), (more_ref, 2 * quarter)):
        span = slice(first, first + 2 * quarter)
        ffn_ref[:, span] = nt(h0_ref[...], ref[...]) + nt(h1_ref[...], w_ref[span])

    def norm(rows):
        value = first_ref[rows, :] + ffn_ref[rows, :] + vec_ref[6:7, :]
        average = jnp.mean(value, axis=-1, keepdims=True)
        centred = value - average
        inverse = lax.rsqrt(jnp.mean(centred * centred, axis=-1, keepdims=True) + 1e-12)
        normed = centred * inverse
        norm_ref[rows, :] = normed
        inv_ref[rows, :] = jnp.broadcast_to(inverse, (STRIP, LANES))
        sec_ref[rows, :] = (normed * vec_ref[1:2, :] + vec_ref[7:8, :]).astype(BF16)

    strips(tokens, STRIP, norm)
    prj_ref[...] = nn(sec_ref[...], proj_ref[...])

    def embed(rows):
        projected = prj_ref[rows, :]
        valid = rows.start + lax.broadcasted_iota(jnp.int32, projected.shape, 0) < length
        valid = valid.astype(F32)
        scale = lax.rsqrt(jnp.sum(projected * projected, axis=-1, keepdims=True) + 1e-06)
        unit = projected * scale
        emb_ref[rows, :] = unit * valid
        cot = cot_ref[rows, :] * valid
        back = scale * (cot - unit * jnp.sum(unit * cot, axis=-1, keepdims=True))
        gp_ref[rows, :] = back.astype(BF16)

    strips(tokens, STRIP, embed)
    pgrad_ref[...] = nn(sec_ref[...].T, gp_ref[...])
    gs_ref[...] = nt(gp_ref[...], proj_ref[...])
    sums_ref[...] = jnp.zeros_like(sums_ref)

    def back(rows):
        grad = gs_ref[rows, :]
        normed = norm_ref[rows, :]
        scaled = grad * vec_ref[1:2, :]
        inside = (
            scaled
            - jnp.mean(scaled, axis=-1, keepdims=True)
            - normed * jnp.mean(scaled * normed, axis=-1, keepdims=True)
        )
        value = inside * inv_ref[rows, 0:1]
        low = value.astype(BF16)
        res_ref[rows, :] = value
        low_ref[rows, :] = low
        fold = lambda v: jnp.sum(v.reshape(STRIP // 8, 8, v.shape[1]), axis=0)
        sums_ref[0:8, :] += fold(grad * normed)
        sums_ref[8:16, :] += fold(grad)
        sums_ref[16:24, :] += fold(low.astype(F32))

    strips(tokens, STRIP, back)
    lowt_ref[...] = low_ref[...].T


def down_both(length, hidden, pieces, first, vec, proj, cot):
    tokens, width = first.shape
    embed = proj.shape[1]
    outs = (
        shaped((tokens, embed), F32),
        shaped((tokens, width), BF16),
        shaped((width, tokens), BF16),
        shaped((tokens, width), F32),
        shaped((width, embed), F32),
        shaped((24, width), F32),
    )
    args = (length, *hidden, first, vec, proj, cot, *pieces)
    return call(
        down_kernel,
        outs,
        args,
        in_specs=[pl.BlockSpec(memory_space=pltpu.SMEM)] + [WHOLE] * 10,
        scratch=[
            pltpu.VMEM((tokens, width), F32),
            pltpu.VMEM((tokens, width), F32),
            pltpu.VMEM((tokens, width), BF16),
            pltpu.VMEM((tokens, embed), BF16),
            pltpu.VMEM((tokens, width), F32),
            pltpu.VMEM((tokens, LANES), F32),
            pltpu.VMEM((tokens, embed), F32),
            pltpu.VMEM((width, hidden[0].shape[1]), BF16),
        ],
        flops=2 * tokens * width * hidden[0].shape[1] * 2,
    )


def down_grad(g_low_t, hid, swapped):
    width, tokens = g_low_t.shape
    hidden = hid.shape[1]
    block = column_block(hidden)

    def kernel(gt_ref, hid_ref, keep_ref, send_ref):
        split_rows(nn(gt_ref[...], hid_ref[...]).astype(BF16), keep_ref, send_ref, swapped)

    piece = pl.BlockSpec((width // 2, block), lambda i: (0, i))
    out = shaped((width // 2, hidden), BF16)
    return call(
        kernel,
        (out, out),
        (g_low_t, hid),
        grid=(hidden // block,),
        in_specs=[
            pl.BlockSpec((width, tokens), lambda i: (0, 0)),
            pl.BlockSpec((tokens, block), lambda i: (0, i)),
        ],
        out_specs=(piece, piece),
        flops=2 * tokens * width * hidden,
    )


def up_grad(g_low, low_t, slope, down, up, start, swapped, biases):
    tokens, width = g_low.shape
    pieces, at = zip(*down, *up)
    hidden = slope.shape[1]
    block = column_block(hidden)

    def kernel(g_ref, lowt_ref, slope_ref, start_ref, *refs):
        wd_ref, wu_ref = refs[-2:]
        join_rows(refs[:4], wd_ref, swapped)
        join_rows(refs[4:8], wu_ref, swapped)
        more, refs = refs[8 : 8 + len(biases)], refs[8 + len(biases) :]
        keep_ref, send_ref, bias_ref, first_ref, gh_ref, gin_ref = refs[:-2]
        def matmul(span):
            gh_ref[:, span] = nn(g_ref[...], wd_ref[:, span])

        columns_of(block, matmul)
        bias_ref[...] = jnp.zeros_like(bias_ref)
        for ref in more:
            bias_ref[8:16, :] = ref[...]

        def act(rows):
            grad = (gh_ref[rows, :] * slope_ref[rows, :].astype(F32)).astype(BF16)
            gin_ref[rows, :] = grad
            wide = grad.astype(F32)
            bias_ref[0:8, :] += jnp.sum(wide.reshape(STRIP // 8, 8, wide.shape[1]), axis=0)

        strips(tokens, STRIP, act)
        split_rows(nn(lowt_ref[...], gin_ref[...]).astype(BF16), keep_ref, send_ref, swapped)
        @pl.when(pl.program_id(0) == 0)
        def _():
            first_ref[...] = start_ref[...]

        def add(span):
            first_ref[:, span] += nt(gin_ref[...], wu_ref[span, :])

        columns_of(width, add)

    row = pl.BlockSpec((tokens, width), lambda i: (0, 0))
    turned = pl.BlockSpec((width, tokens), lambda i: (0, 0))
    act = pl.BlockSpec((tokens, block), lambda i: (0, i))
    piece = pl.BlockSpec((width // 2, block), lambda i: (0, i))
    parts = [pl.BlockSpec((width // 4, block), lambda i, row=row: (row, i)) for row in at]
    thin = pl.BlockSpec((8, block), lambda i: (0, i))
    out = shaped((width // 2, hidden), BF16)
    return call(
        kernel,
        (out, out, shaped((8 * (1 + len(biases)), hidden), F32), shaped((tokens, width), F32)),
        (g_low, low_t, slope, start, *pieces, *biases),
        grid=(hidden // block,),
        in_specs=[row, turned, act, row] + parts + [thin] * len(biases),
        out_specs=(
            piece,
            piece,
            pl.BlockSpec((8 * (1 + len(biases)), block), lambda i: (0, i)),
            row,
        ),
        scratch=[
            pltpu.VMEM((tokens, block), F32),
            pltpu.VMEM((tokens, block), BF16),
            pltpu.VMEM((width, block), BF16),
            pltpu.VMEM((width, block), BF16),
        ],
        flops=6 * tokens * width * hidden,
    )


def norm_back(g_first, res, vec, weights, sums_two, cols):
    tokens, width = g_first.shape

    def kernel(
        gf_ref, res_ref, vec_ref, w_ref, two_ref, gres_ref, turn_ref, gatt_ref, sums_ref, low_ref
    ):
        sums_ref[0:24, :] = jnp.zeros((24, width), F32)
        sums_ref[24:48, :] = two_ref[...]

        def back(rows):
            value = res_ref[rows, :]
            average = jnp.mean(value, axis=-1, keepdims=True)
            centred = value - average
            inverse = lax.rsqrt(jnp.mean(centred * centred, axis=-1, keepdims=True) + 1e-12)
            normed = centred * inverse
            grad = gf_ref[rows, :]
            scaled = grad * vec_ref[0:1, :]
            inside = (
                scaled
                - jnp.mean(scaled, axis=-1, keepdims=True)
                - normed * jnp.mean(scaled * normed, axis=-1, keepdims=True)
            )
            out = inside * inverse
            low = out.astype(BF16)
            gres_ref[rows, :] = out
            low_ref[rows, :] = low
            fold = lambda v: jnp.sum(v.reshape(STRIP // 8, 8, v.shape[1]), axis=0)
            sums_ref[0:8, :] += fold(grad * normed)
            sums_ref[8:16, :] += fold(grad)
            sums_ref[16:24, :] += fold(low.astype(F32))

        strips(tokens, STRIP, back)
        turn_ref[...] = low_ref[...].T
        for half in range(2):
            gatt_ref[half] = nn(low_ref[...], w_ref[half, :, 3 * cols :]).astype(BF16)

    outs = (
        shaped((tokens, width), F32),
        shaped((width, tokens), BF16),
        shaped((2, tokens, cols), BF16),
        shaped((48, width), F32),
    )
    return call(
        kernel,
        outs,
        (g_first, res, vec, weights, sums_two),
        scratch=[pltpu.VMEM((tokens, width), BF16)],
        flops=4 * tokens * width * cols,
    )


def attention_back(pairs, g_att, att, qkv, lse, mask, earlier=()):
    tokens, cols = att.shape[1:]
    wide = len(pairs) * LANES
    scale = HD ** (-0.5)

    before = sum(part.shape[3] for part in earlier)

    def kernel(gatt_ref, att_ref, qkv_ref, lse_ref, mask_ref, *refs):
        gqkv_ref, sums_ref, col_ref = refs[len(earlier) :]
        for ref in refs[: len(earlier)]:
            sums_ref[:, :, :, 0:before] = ref[...]
        col_ref[...] = jnp.broadcast_to(mask_ref[...], (LANES, tokens)).T
        lane = lax.broadcasted_iota(jnp.int32, (tokens, LANES), 1) < HD

        def pair(step, carry):
            half, place = step // len(pairs), step % len(pairs)
            i = pairs[0] + place
            off = pl.multiple_of(i * LANES, LANES)
            off_k = pl.multiple_of(cols + off, LANES)
            off_v = pl.multiple_of(2 * cols + off, LANES)
            query = qkv_ref[half, :, pl.ds(off, LANES)] * BF16(scale)
            key = qkv_ref[half, :, pl.ds(off_k, LANES)]
            value = qkv_ref[half, :, pl.ds(off_v, LANES)]
            grad = gatt_ref[half, :, pl.ds(off, LANES)]
            out = att_ref[half, :, pl.ds(off, LANES)]
            key_t = (key * BF16(scale)).T
            delta = (grad.astype(F32) * out.astype(F32)).T
            g_query, g_key, g_value = [], [], []
            for head in range(2):
                pick = lane == (head == 0)
                span = slice(head * HD, (head + 1) * HD)
                zero = jnp.zeros_like(key)
                scores = nt(jnp.where(pick, key, zero), query)
                scores = scores + jnp.concatenate([col_ref[...]] * (tokens // LANES), axis=1)
                probs = jnp.exp(scores - lse_ref[half, pl.ds(i * 2 + head, 1), :])
                g_probs = nt(jnp.where(pick, value, zero), grad)
                row_delta = jnp.sum(delta[span], axis=0, keepdims=True)
                g_scores = (probs * (g_probs - row_delta)).astype(BF16)
                g_value.append(nn(probs.astype(BF16), grad))
                g_key.append(nn(g_scores, query))
                g_query.append(nn(key_t[span], g_scores))
            g_q = jnp.concatenate(g_query, axis=0).T.astype(BF16)
            g_v = jnp.where(lane, *g_value).astype(BF16)
            to = pl.multiple_of(place * LANES, LANES)
            gqkv_ref[half, :, pl.ds(to, LANES)] = g_q
            to_k = pl.ds(pl.multiple_of(wide + to, LANES), LANES)
            gqkv_ref[half, :, to_k] = jnp.where(lane, *g_key).astype(BF16)
            gqkv_ref[half, :, pl.ds(pl.multiple_of(2 * wide + to, LANES), LANES)] = g_v
            for row, grads in ((0, g_q), (1, g_v)):
                total = jnp.sum(grads.astype(F32).reshape(-1, 8, LANES), axis=0)
                place_to = pl.ds(pl.multiple_of(before + to, LANES), LANES)
                sums_ref[half, row, :, place_to] = total
            return carry

        lax.fori_loop(0, 2 * len(pairs), pair, 0)

    return call(
        kernel,
        (shaped((2, tokens, 3 * wide), BF16), shaped((2, 2, 8, before + wide), F32)),
        (g_att, att, qkv, lse, mask, *earlier),
        scratch=[pltpu.VMEM((tokens, LANES), F32)],
        flops=20 * tokens * tokens * wide * 2,
    )


def project_other(x_t, g_qkv, beside):
    width, tokens = x_t.shape
    columns = g_qkv.shape[2]
    extra = beside[1].shape[2] if beside else 0

    def kernel(xt_ref, g_ref, *refs):
        keep_ref, send_ref = refs[len(beside) :]
        span = slice(0, columns)
        made = nn(xt_ref[...], g_ref[1]).astype(BF16)
        split_rows(made, keep_ref.at[:, span], send_ref.at[:, span], True)
        if beside:
            span = slice(columns, columns + extra)
            made = nn(refs[0][...], refs[1][1]).astype(BF16)
            split_rows(made, keep_ref.at[:, span], send_ref.at[:, span], True)

    out = shaped((width // 2, columns + extra), BF16)
    return call(
        kernel,
        (out, out),
        (x_t, g_qkv, *beside),
        flops=2 * tokens * width * (columns + extra),
    )


def project_own(x_t, g_qkv, beside, small, keep_came, send_came):
    width, tokens = x_t.shape
    columns = g_qkv.shape[2]
    extra = beside[1].shape[2] if beside else 0
    tail = small[0].shape[1] if small else 0
    middle = width // 2
    count = len(beside) + len(small)

    def kernel(xt_ref, g_ref, kc_ref, sc_ref, *refs):
        keep_ref, send_ref = refs[count:]
        for out, came, first in ((keep_ref, kc_ref, 0), (send_ref, sc_ref, middle)):
            rows = slice(first, first + middle)
            span = slice(0, columns)
            made = nn(xt_ref[rows, :], g_ref[0])
            out[:, span] = (made + came[:, span].astype(F32)).astype(BF16)
            if beside:
                span = slice(columns, columns + extra)
                made = nn(refs[0][rows, :], refs[1][0])
                out[:, span] = (made + came[:, span].astype(F32)).astype(BF16)
            if small:
                total = refs[count - 2][rows, :].astype(F32) + refs[count - 1][rows, :].astype(F32)
                out[:, columns + extra :] = total.astype(BF16)

    out = shaped((middle, columns + extra + tail), BF16)
    return call(
        kernel,
        (out, out),
        (x_t, g_qkv, keep_came, send_came, *beside, *small),
        flops=2 * tokens * width * (columns + extra),
    )


def token_back(g_parts, start, perm, weights, cols):
    tokens, width = start.shape
    widths = [part.shape[2] // 3 for part in g_parts]

    def kernel(a_ref, b_ref, start_ref, perm_ref, w_ref, out_ref, g_ref, high_ref, rest_ref):
        for half in range(2):
            for kind in range(3):
                to = kind * cols
                for ref, wide in zip((a_ref, b_ref), widths):
                    taken = ref[half, :, kind * wide : (kind + 1) * wide]
                    g_ref[half, :, to : to + wide] = taken
                    to += wide
        used = slice(0, 3 * cols)

        def matmul(span):
            made = nt(g_ref[0], w_ref[0, span, used]) + nt(g_ref[1], w_ref[1, span, used])
            made = start_ref[:, span] + made
            high = made.astype(BF16)
            high_ref[:, span] = high
            rest_ref[:, span] = (made - high.astype(F32)).astype(BF16)

        columns_of(width, matmul)

        def reorder(span):
            turn = perm_ref[span, :]
            out_ref[:, span] = nt(high_ref[...], turn) + nt(rest_ref[...], turn)

        columns_of(width, reorder)

    return call(
        kernel,
        shaped((tokens, width), F32),
        (*g_parts, start, perm, weights),
        scratch=[
            pltpu.VMEM((2, tokens, 3 * cols), BF16),
            pltpu.VMEM((tokens, width), BF16),
            pltpu.VMEM((tokens, width), BF16),
        ],
        flops=16 * tokens * width * cols,
    )


class Exchange:
    def __init__(self, size):
        self.size = size
        self.depth = size.bit_length() - 1
        self.rank = lax.axis_index("dp")
        self.core = lax.axis_index("tensor")
        outer = list(range(self.depth - 1, 1, -1))
        self.bits = (outer + [1, 0], outer + [0, 1])

    def flip(self, value, step):
        pairs = []
        for i in range(self.size):
            for core in range(2):
                pairs.append((i * 2 + core, (i ^ (1 << self.bits[core][step])) * 2 + core))
        return lax.ppermute(value, ("dp", "tensor"), pairs)

    def blocks(self):
        tables = []
        for bits in self.bits:
            tables.append(
                [
                    sum(((j >> step) & 1) << bit for step, bit in enumerate(bits))
                    for j in range(self.size)
                ]
            )
        table = np.array(tables, np.int32)
        return jnp.where(self.core == 0, table[0], table[1]) ^ self.rank


def join(held, came):
    return jnp.concatenate([held, came], axis=0)


def added(*values):
    total = values[0].astype(F32)
    for value in values[1:]:
        total = total + value.astype(F32)
    return total


def halves(value):
    middle = value.shape[0] // 2
    return value[:middle], value[middle:]


def three_parts(value):
    high = lax.reduce_precision(value, 8, 7)
    rest = value - high
    middle = lax.reduce_precision(rest, 8, 7)
    return (high.astype(BF16), middle.astype(BF16), (rest - middle).astype(BF16))


SMALL = 48
UP = 32


def pack(qkv_w, out_w, emb_w, gains, biases, up_bias):
    rows, cols = out_w.shape
    chunk = gains.shape[1]
    args = (qkv_w, out_w, emb_w, gains, biases, up_bias[None])

    def kernel(*refs):
        one_ref, refs, vec_ref, sems = refs[6], (*refs[:6], *refs[7:13]), refs[13], refs[14]
        copies = []
        for place in range(6):
            copies.append(pltpu.make_async_copy(refs[place], refs[6 + place], sems.at[place]))
        for copy in copies:
            copy.start()
        for copy in copies:
            copy.wait()
        q_ref, o_ref, e_ref, g_ref, b_ref, u_ref = refs[6:]
        for part in range(3):
            one_ref[:, part * cols : (part + 1) * cols] = q_ref[part]
        one_ref[:, 3 * cols : 4 * cols] = o_ref[...]
        vec_ref[...] = jnp.zeros_like(vec_ref)
        vec_ref[0:2, 0:chunk] = g_ref[...]
        vec_ref[2:8, 0:chunk] = b_ref[...]
        vec_ref[0:1, UP : UP + u_ref.shape[1]] = u_ref[...]
        value = vec_ref[...]
        high = value.astype(BF16).astype(F32)
        middle = (value - high).astype(BF16).astype(F32)
        block = [e_ref[...].astype(F32), high, middle, value - high - middle]
        one_ref[:, 4 * cols :] = jnp.concatenate(block, axis=0).astype(BF16)

    return call(
        kernel,
        shaped((rows, 4 * cols + LANES), BF16),
        args,
        in_specs=[pl.BlockSpec(memory_space=pltpu.HBM)] * 6,
        scratch=[pltpu.VMEM(arg.shape, arg.dtype) for arg in args]
        + [pltpu.VMEM((8, LANES), F32), pltpu.SemaphoreType.DMA((6,))],
        grant=60 * 1024 * 1024,
    )


def spreads(sides, width, hidden, chunk, up_chunk):
    lane = jnp.arange(LANES, dtype=jnp.int32)[:, None]
    column = jnp.arange(width, dtype=jnp.int32)[None]
    up_column = jnp.arange(hidden, dtype=jnp.int32)[None]
    thin, broad = [], []
    for side in sides:
        thin.append((lane < chunk) & (column % (2 * chunk) == side * chunk + lane))
        broad.append((lane >= UP) & (up_column % (2 * up_chunk) == side * up_chunk + lane - UP))
    return jnp.stack(thin).astype(BF16), jnp.stack(broad).astype(BF16)


def unpack(core, pieces, thin, broad, rel, absolute, up_rel, cols):
    width, hidden = thin.shape[2], broad.shape[2]
    count = width // SMALL

    def kernel(core_ref, thin_ref, broad_ref, rel_ref, abs_ref, up_ref, *refs):
        vec_ref, head_ref, side_ref, proj_ref, e_ref, sems = refs[8:]
        copies = load_weights(refs[:8], e_ref, sems, 4 * cols, 4 * cols + LANES)
        for copy in copies:
            copy.wait()
        first = core_ref[0] == 0
        blocks = [e_ref[side].astype(F32).reshape(count, SMALL, LANES) for side in range(2)]
        tops = [block[:, : SMALL // 2] for block in blocks]
        halves = [jnp.where(first, tops[0], tops[1]), jnp.where(first, tops[1], tops[0])]
        proj_ref[...] = jnp.concatenate(halves, axis=1).reshape(width, LANES).astype(BF16)
        flat = lax.broadcasted_iota(jnp.int32, (count, count * 8), 1)
        pick = flat == 8 * lax.broadcasted_iota(jnp.int32, (count, count * 8), 0)
        pick = pick.astype(F32).astype(BF16)
        vec = jnp.zeros((8, width), F32)
        plain = jnp.zeros((8, width), F32)
        wide = jnp.zeros((1, hidden), F32)
        index = lax.broadcasted_iota(jnp.int32, (count, hidden), 0)
        for side in range(2):
            placed, up_placed = None, None
            for part in (2, 1, 0):
                start = SMALL // 2 + 8 * part
                rows = blocks[side][:, start : start + 8].reshape(count * 8, LANES).astype(BF16)
                spread = nn(rows, thin_ref[side])
                up_spread = nn(nn(pick, rows).astype(BF16), broad_ref[side])
                placed = spread if placed is None else placed + spread
                up_placed = up_spread if up_placed is None else up_placed + up_spread
            for j in range(count):
                row = placed[8 * j : 8 * j + 8]
                vec = vec + jnp.where(rel_ref[...] == j, row, 0.0)
                plain = plain + jnp.where(abs_ref[...] == j, row, 0.0)
            chosen = jnp.where(up_ref[...] == index, up_placed, 0.0)
            wide = wide + jnp.sum(chosen, axis=0, keepdims=True)
        vec_ref[...] = vec
        for side in range(2):
            low_half = first if side == 0 else jnp.logical_not(first)
            part = jnp.where(low_half, plain[:, :cols], plain[:, cols:])
            head_ref[side : side + 1, :cols] = part[2:3]
            head_ref[side : side + 1, cols : 2 * cols] = jnp.zeros((1, cols), F32)
            head_ref[side : side + 1, 2 * cols :] = part[3:4]
            middle = hidden // 2
            side_ref[side : side + 1, :] = jnp.where(low_half, wide[:, :middle], wide[:, middle:])

    outs = (
        shaped((8, width), F32),
        shaped((2, 3 * cols), F32),
        shaped((2, hidden // 2), F32),
        shaped((width, LANES), BF16),
    )
    return call(
        kernel,
        outs,
        (core[None], thin, broad, rel, absolute, up_rel, *pieces),
        in_specs=[pl.BlockSpec(memory_space=pltpu.SMEM)] + [WHOLE] * 5 + [ANY] * 8,
        scratch=[pltpu.VMEM((2, width, LANES), BF16), pltpu.SemaphoreType.DMA((2, 4))],
    )


def pack_grads(
    core, thin, broad, rel, absolute, up_rel, sums, up_sums, head_sums, proj_grad,
):
    width, hidden = thin.shape[2], broad.shape[2]
    count = width // SMALL

    def kernel(
        core_ref, thin_ref, broad_ref, rel_ref, abs_ref, up_ref, sums_ref, ups_ref, heads_ref,
        pg_ref, own_ref, other_ref,
    ):
        first = core_ref[0] == 0
        fold = lambda v: jnp.sum(v, axis=0, keepdims=True)

        def ordered(own, other):
            low, high = jnp.where(first, own, other), jnp.where(first, other, own)
            return jnp.concatenate([low, high], axis=1)

        def heads(half, kind):
            return fold(heads_ref[half, kind])

        rows = [
            fold(sums_ref[0:8]),
            fold(sums_ref[24:32]),
            ordered(heads(0, 0), heads(1, 0)),
            ordered(heads(0, 1), heads(1, 1)),
            fold(sums_ref[16:24]),
            fold(sums_ref[8:16]),
            fold(sums_ref[40:48]),
            fold(sums_ref[32:40]),
        ]
        grads = jnp.concatenate(rows, axis=0)
        row = lax.broadcasted_iota(jnp.int32, (8, width), 0)
        block = jnp.where((row == 2) | (row == 3), abs_ref[...], rel_ref[...])
        spread = [jnp.where(block == j, grads, 0.0) for j in range(count)]
        spread = jnp.concatenate(spread, axis=0)
        high = spread.astype(BF16)
        rest = (spread - high.astype(F32)).astype(BF16)
        up = ordered(fold(ups_ref[0:8]), fold(ups_ref[8:16]))
        index = lax.broadcasted_iota(jnp.int32, (count, hidden), 0)
        up = jnp.where(up_ref[...] == index, up, 0.0)
        up_high = up.astype(BF16)
        up_rest = (up - up_high.astype(F32)).astype(BF16)
        flat = lax.broadcasted_iota(jnp.int32, (count * 8, count), 0)
        put = flat == 8 * lax.broadcasted_iota(jnp.int32, (count * 8, count), 1)
        put = put.astype(F32).astype(BF16)
        tops = pg_ref[...].reshape(count, SMALL, LANES)
        for side, out_ref in enumerate((own_ref, other_ref)):
            low_half = first if side == 0 else jnp.logical_not(first)
            top = jnp.where(low_half, tops[:, : SMALL // 2], tops[:, SMALL // 2 :])
            thin_part = nt(high, thin_ref[side]) + nt(rest, thin_ref[side])
            up_part = nt(up_high, broad_ref[side]) + nt(up_rest, broad_ref[side])
            vec = (thin_part + nn(put, up_part.astype(BF16))).reshape(count, 8, LANES)
            blank = jnp.zeros((count, SMALL // 2 - 8, LANES), F32)
            made = jnp.concatenate([top, vec, blank], axis=1).reshape(width, LANES).astype(BF16)
            quarter = width // 4
            for place in range(4):
                source = OTHER[place] if side == 1 else place
                out_ref[place * quarter : (place + 1) * quarter, :] = made[
                    source * quarter : (source + 1) * quarter
                ]

    out = shaped((width, LANES), BF16)
    return call(
        kernel,
        (out, out),
        (
            core[None], thin, broad, rel, absolute, up_rel, sums, up_sums, head_sums, proj_grad,
        ),
        in_specs=[pl.BlockSpec(memory_space=pltpu.SMEM)] + [WHOLE] * 9,
    )


def finish(kept, came, a_wide, cols, chunk, up_chunk, emb_shape):
    rows = kept.shape[0]
    b_wide = cols - a_wide
    beside = 3 * a_wide
    second = beside + cols

    def kernel(kept_ref, came_ref, qkv_ref, out_ref, emb_ref, gain_ref, bias_ref, up_ref, sum_ref):
        sum_ref[...] = kept_ref[...] + came_ref[...].astype(F32)
        for part in range(3):
            qkv_ref[part, :, :a_wide] = sum_ref[:, part * a_wide : (part + 1) * a_wide]
            start = second + part * b_wide
            qkv_ref[part, :, a_wide:] = sum_ref[:, start : start + b_wide]
        out_ref[...] = sum_ref[:, beside:second]
        first = second + 3 * b_wide
        half = SMALL // 2
        emb_ref[...] = sum_ref[0:half, first:]
        gain_ref[...] = sum_ref[half : half + 2, first : first + chunk]
        bias_ref[...] = sum_ref[half + 2 : half + 8, first : first + chunk]
        up_ref[...] = sum_ref[half : half + 1, first + UP : first + UP + up_chunk]

    outs = (
        shaped((3, rows, cols), F32),
        shaped((rows, cols), F32),
        shaped(emb_shape, F32),
        shaped((2, chunk), F32),
        shaped((6, chunk), F32),
        shaped((1, up_chunk), F32),
    )
    return call(kernel, outs, (kept, came), scratch=[pltpu.VMEM(kept.shape, F32)])


def pack_plain(qkv_w, out_w, emb_w, gains, biases, up_bias):
    rows = out_w.shape[0]
    vector = jnp.concatenate([gains.reshape(-1), biases.reshape(-1), up_bias])
    pad_to = -(-vector.size // LANES) * LANES
    padded = jnp.pad(vector, (0, pad_to - vector.size))
    flat = jnp.concatenate([emb_w.reshape(-1), *three_parts(padded)])
    extra = -(-flat.size // (rows * LANES)) * LANES
    flat = jnp.pad(flat, (0, rows * extra - flat.size)).reshape(rows, extra)
    one = jnp.concatenate([qkv_w[0], qkv_w[1], qkv_w[2], out_w, flat], axis=1)
    sizes = (rows, extra, emb_w.size, gains.shape[1], up_bias.size, pad_to)
    return one, sizes


def unpack_plain(core, sides, pieces, blocks, sizes):
    rows, extra, emb_size, chunk, up_chunk, pad_to = sizes
    size = blocks.shape[0]
    width = size * rows
    cols = width // 2
    ff_local = size * up_chunk
    pieces = [part[:, 4 * cols :] for part in pieces]
    own = jnp.concatenate(pieces[:4])
    other = jnp.concatenate([pieces[4 + place] for place in OTHER])
    small = [part.reshape(size, rows * extra) for part in (own, other)]
    small = jnp.where(core == 0, jnp.stack(small, 1), jnp.stack(small[::-1], 1))
    proj = small[:, :, :emb_size].reshape(width, -1)
    thirds = small[:, :, emb_size : emb_size + 3 * pad_to].astype(F32)
    thirds = thirds.reshape(size, 2, 3, pad_to)
    vectors = thirds[:, :, 0] + (thirds[:, :, 1] + thirds[:, :, 2])
    plain = vectors[jnp.argsort(blocks)].reshape(size * 2, pad_to)
    vectors = vectors.reshape(size * 2, pad_to)
    vec = jnp.moveaxis(vectors[:, : 8 * chunk].reshape(-1, 8, chunk), 1, 0).reshape(8, width)
    query_bias = plain[:, 2 * chunk : 3 * chunk].reshape(-1)
    value_bias = plain[:, 3 * chunk : 4 * chunk].reshape(-1)
    up_bias = plain[:, 8 * chunk : 8 * chunk + up_chunk].reshape(-1)
    head_bias, side_bias = [], []
    for side in sides:
        query_part = lax.dynamic_slice_in_dim(query_bias, side * cols, cols)
        value_part = lax.dynamic_slice_in_dim(value_bias, side * cols, cols)
        head_bias.append(jnp.concatenate([query_part, jnp.zeros_like(query_part), value_part]))
        side_bias.append(lax.dynamic_slice_in_dim(up_bias, side * ff_local, ff_local))
    return vec, jnp.stack(head_bias), jnp.stack(side_bias), proj


def pack_grads_plain(
    core, blocks, sizes, sums, up_sums, head_sums, proj_grad
):
    rows, extra, emb_size, chunk, up_chunk, pad_to = sizes
    size = blocks.shape[0]

    def fold(value):
        return jnp.sum(value.reshape(-1, 8, value.shape[-1]), axis=1)

    def absolute(own, other):
        return jnp.where(
            core == 0, jnp.concatenate([own, other]), jnp.concatenate([other, own])
        )

    def relative(value):
        return value.reshape(size, 2, -1)[blocks]

    gain_one, shift_one, out_bias, gain_two, shift_two, ffn_bias = (
        row.reshape(size, 2, chunk) for row in fold(sums)
    )
    own, other = jnp.sum(head_sums, axis=2)
    small = jnp.concatenate(
        [
            proj_grad.reshape(size, 2, emb_size),
            gain_one,
            gain_two,
            relative(absolute(own[0], other[0])),
            relative(absolute(own[1], other[1])),
            out_bias,
            shift_one,
            ffn_bias,
            shift_two,
            relative(absolute(*fold(up_sums))),
        ],
        axis=2,
    ).astype(BF16)
    small = jnp.pad(small, ((0, 0), (0, 0), (0, rows * extra - small.shape[2])))
    small = jnp.where(core == 0, small, small[:, ::-1])
    own, other = jnp.moveaxis(small, 1, 0).reshape(2, size * rows, extra)
    first, second, third, fourth = jnp.split(other, 4)
    return own, jnp.concatenate([first, third, second, fourth])


def body(
    tokens,
    lengths,
    key_mask,
    order,
    query_key_value_weight,
    output_projection_weight,
    up_projection_weight,
    down_projection_weight,
    embedding_projection_weight,
    gains,
    biases,
    up_bias_vector,
    cotangent,
):
    size = lax.axis_size("dp")
    core = lax.axis_index("tensor")
    ways = Exchange(size)
    depth = ways.depth
    half_len = tokens.shape[1]
    full_len = key_mask.shape[1]
    width = tokens.shape[2]
    cols = output_projection_weight.shape[0]
    rows = output_projection_weight.shape[1]
    ff_local = up_projection_weight.shape[1]
    chunk = gains.shape[1]
    emb_size = embedding_projection_weight.size
    sides = (core, 1 - core)

    fast = rows == SMALL and emb_size == SMALL // 2 * LANES and up_bias_vector.size <= LANES - UP
    small_args = (
        query_key_value_weight,
        output_projection_weight.T,
        embedding_projection_weight,
        gains,
        biases,
        up_bias_vector,
    )
    if fast:
        one = pack(*small_args)
    else:
        one, small_sizes = pack_plain(*small_args)

    wide = 4 * cols
    seconds, lasts = depth - 2, depth - 1
    for step in range(depth - 3):
        one = join(one, ways.flip(one, step))
    tokens, order, lengths, key_mask = after((tokens, order, lengths, key_mask), one)
    mine = order[0, core]
    theirs = order[0, 1 - core]
    my_half = lax.dynamic_index_in_dim(tokens, mine, 0, keepdims=False)
    their_half = lax.dynamic_index_in_dim(tokens, theirs, 0, keepdims=False)
    blocks = ways.blocks()
    one_came = ways.flip(one, depth - 3)
    if fast:
        thin, broad = spreads(sides, width, 2 * ff_local, chunk, up_bias_vector.size)
        places_of = jnp.argsort(blocks)
        rel = (jnp.arange(width, dtype=jnp.int32) // rows)[None]
        absolute = jnp.repeat(places_of, rows)[None].astype(jnp.int32)
        up_rel = jnp.repeat(places_of, 2 * up_bias_vector.size)[None].astype(jnp.int32)
        one_came, thin, broad, rel, absolute, up_rel = together(
            one_came, thin, broad, rel, absolute, up_rel
        )
        tables = (core, thin, broad, rel, absolute, up_rel)

    def in_order(own, other):
        return jnp.where(
            core == 0, jnp.concatenate([own, other]), jnp.concatenate([other, own])
        )

    def half_of(value, which):
        return lax.dynamic_slice_in_dim(value, which * half_len, half_len)

    seq_len = lengths[mine]
    marks = lax.dynamic_index_in_dim(key_mask, mine, 0, keepdims=False)
    places = jnp.arange(full_len, dtype=jnp.int32)
    key_ok = (places < seq_len) & ((marks == 1) | (places == 0))
    mask = jnp.where(key_ok, 0.0, -1e30).astype(F32)[None, :]
    where = (blocks[:, None] * rows + jnp.arange(rows, dtype=jnp.int32)[None]).reshape(-1)
    perm = (jnp.arange(width, dtype=jnp.int32)[:, None] == where[None]).astype(BF16)
    two, three = after((up_projection_weight, down_projection_weight.T), order)
    for step in range(depth - 4):
        two = join(two, ways.flip(two, step))
        three = join(three, ways.flip(three, step))
    two_came = ways.flip(two, depth - 4)
    one_came, two_came = together(one_came, two_came)
    one = join(one, one_came)
    two = join(two, two_came)
    here = in_order(my_half, swap_cores(after(their_half, one)))
    one_b, one_c, two_came, three_came, here, mask, perm = together(
        ways.flip(one, seconds),
        ways.flip(one, lasts),
        ways.flip(two, depth - 3),
        ways.flip(after(three, two), depth - 4),
        here,
        mask,
        perm,
    )
    two = join(two, two_came)
    three = join(three, three_came)
    one_d, two_b, three_came, *one_other = together(
        ways.flip(one_b, lasts),
        ways.flip(two, seconds),
        ways.flip(three, depth - 3),
        swap_cores(one),
        swap_cores(one_b),
        swap_cores(one_c),
    )
    three = join(three, three_came)
    two_both = join(two, two_b)
    one_pieces = (one, one_b, one_c, one_d, *one_other, swap_cores(one_d))
    two_more, three_b = ways.flip(two_both, lasts), ways.flip(three, seconds)
    one_pieces = together(*one_pieces, two_both, three)[:8]
    if fast:
        vec, head_bias, side_bias, proj = unpack(core, one_pieces, *tables[1:], cols)
    else:
        vec, head_bias, side_bias, proj = unpack_plain(
            core, sides, one_pieces, blocks, small_sizes
        )
    side_bias = (side_bias[0:1], side_bias[1:2])

    qkv, lse, att, res_one, first, first_low, first_low_t, here_t, weights = attention_forward(
        here, perm, head_bias, mask, vec, one_pieces, cols
    )
    two_more, three_b = after((two_more, three_b), first_low)
    three_both = join(three, three_b)
    three_more = ways.flip(three_both, lasts)
    two_other = [swap_cores(part) for part in (two_both, two_more)]

    def quarters(both, more):
        return ((both, 0), (both, 1), (more, 0), (more, 1))

    two_own = quarters(two_both, two_more)
    hid_own, slope_own = up_forward(
        after(first_low, three_both, two_more), two_own, side_bias[0], False
    )
    two_other = quarters(*after(two_other, hid_own))
    three_both_other = swap_cores(three_both)
    cot_mine = lax.dynamic_index_in_dim(cotangent, core, 0, keepdims=False)
    cot_other = lax.dynamic_index_in_dim(cotangent, 1 - core, 0, keepdims=False)
    cot = in_order(cot_mine, after(swap_cores(after(cot_other, first_low)), hid_own))
    hid_other, slope_other = up_forward(after(first_low, cot), two_other, side_bias[1], True)
    three_more, three_both_other = after((three_more, three_both_other), hid_other)
    three_more_other = swap_cores(three_more)
    three_own = quarters(three_both, three_more)
    three_other = quarters(three_both_other, three_more_other)
    emb, g_ffn, g_ffn_t, g_res_two, proj_grad, sums_two = down_both(
        seq_len[None],
        (hid_own, hid_other),
        (three_both, three_more, three_both_other, three_more_other),
        first,
        vec,
        proj,
        cot,
    )

    def low(*values):
        return added(*values).astype(BF16)

    def spread(value):
        kept, sent = halves(value)
        return kept, sent.astype(BF16)

    dk_other, ds_other = down_grad(g_ffn_t, hid_other, True)
    ds_came, dk_came = swap_cores(ds_other), swap_cores(dk_other)
    dk, ds = down_grad(g_ffn_t, after(hid_own, ds_other), False)
    ds_came = after(ds_came, ds)
    d_high = low(halves(ds)[1], halves(ds_came)[1])
    d_low = low(halves(ds)[0], halves(ds_came)[0])
    d_came_high = ways.flip(d_high, lasts)
    uk_other, us_other, up_bias_other, part = up_grad(
        after(g_ffn, d_high, d_low),
        first_low_t,
        slope_other,
        three_other,
        two_other,
        g_res_two,
        True,
        (),
    )
    us_came, uk_came = swap_cores(us_other), swap_cores(uk_other)
    d_came_high, dk_came, d_low = after((d_came_high, dk_came, d_low), us_other)
    d_came_low = ways.flip(d_low, lasts)
    uk, us, up_bias, g_first = up_grad(
        after(g_ffn, us_other, d_came_high),
        first_low_t,
        slope_own,
        three_own,
        two_own,
        part,
        False,
        (up_bias_other,),
    )
    d_came_low, us_came, uk_came = after((d_came_low, us_came, uk_came), us)
    u_sent = low(us, us_came)
    u_came = ways.flip(u_sent, lasts)
    d_sent = low(halves(dk)[1], halves(dk_came)[1], d_came_high)
    d_held = added(halves(dk)[0], halves(dk_came)[0], d_came_low)
    d_came = ways.flip(d_sent, seconds)
    g_res_one, g_branch_t, g_att, sums = norm_back(
        after(g_first, u_sent, d_sent), res_one, vec, weights, sums_two, cols
    )
    pairs = list(range(cols // LANES))
    split = (len(pairs) + 1) // 2
    g_a, bias_a = attention_back(pairs[:split], g_att, att, qkv, lse, mask)
    beside = (g_branch_t, att)
    ak_other, as_other = project_other(here_t, g_a, beside)
    as_came, ak_came = swap_cores(as_other), swap_cores(ak_other)
    g_b, head_sums = attention_back(
        pairs[split:], after(g_att, as_other), att, qkv, lse, mask, (bias_a,)
    )
    as_came, ak_came = after((as_came, ak_came), g_b)
    a_keep, a_send = project_own(here_t, g_a, beside, (), ak_came, as_came)
    d_came, u_came = after((d_came, u_came), a_send)
    a_came = ways.flip(a_send, lasts)
    u_sent = low(halves(uk)[1], halves(uk_came)[1], halves(u_came)[1])
    u_held = added(halves(uk)[0], halves(uk_came)[0], halves(u_came)[0])
    u_came = ways.flip(u_sent, seconds)
    d_held, d_sent = spread(d_held + d_came.astype(F32))
    d_came = ways.flip(d_sent, depth - 3)
    bk_other, bs_other = project_other(here_t, after(g_b, a_send, u_sent, d_sent), ())
    bs_came, bk_came = swap_cores(bs_other), swap_cores(bk_other)
    if fast:
        small_own, small_other = pack_grads(
            *tables, after(sums, bs_other), up_bias, head_sums, proj_grad
        )
    else:
        small_own, small_other = pack_grads_plain(
            core, blocks, small_sizes, sums, up_bias, head_sums, proj_grad
        )
    small_came = swap_cores(small_other)
    bs_came, bk_came = after((bs_came, bk_came), small_other)
    b_keep, b_send = project_own(here_t, g_b, (), (small_own, small_came), bk_came, bs_came)
    d_came, u_came, a_came = after((d_came, u_came, a_came), b_send)
    b_came = ways.flip(b_send, lasts)
    a_sent = low(halves(a_keep)[1], halves(a_came)[1])
    a_held = added(halves(a_keep)[0], halves(a_came)[0])
    a_came = ways.flip(a_sent, seconds)
    u_held, u_sent = spread(after(u_held, a_sent) + u_came.astype(F32))
    u_came = ways.flip(u_sent, depth - 3)
    d_held, d_sent = spread(after(d_held, a_sent) + d_came.astype(F32))
    d_came = ways.flip(d_sent, depth - 4)
    b_came = after(b_came, u_sent, d_sent)
    b_sent = low(halves(b_keep)[1], halves(b_came)[1])
    b_held = added(halves(b_keep)[0], halves(b_came)[0])
    b_came = ways.flip(b_sent, seconds)
    g_here = token_back(
        (after(g_a, b_send, a_sent, u_sent, b_sent), g_b), g_res_one, perm, weights, cols
    )
    a_came, b_came, u_came, d_came, emb = after((a_came, b_came, u_came, d_came, emb), g_here)
    held = jnp.concatenate([a_held + a_came.astype(F32), b_held + b_came.astype(F32)], axis=1)
    for step in range(depth - 3, -1, -1):
        held, sent = spread(held)
        came = ways.flip(sent, step)
        if step == depth - 3:
            u_held, u_sent = spread(u_held + after(u_came, sent).astype(F32))
            u_came = ways.flip(u_sent, depth - 4)
        if step:
            held = held + came.astype(F32)
    d_held = d_held + after(d_came, u_sent).astype(F32)
    for step in range(depth - 5, -1, -1):
        d_held, sent = spread(d_held)
        d_held = d_held + ways.flip(sent, step).astype(F32)
        u_held, sent = spread(u_held + u_came.astype(F32))
        u_came = ways.flip(sent, step)
    down_shard, up_shard = d_held, u_held + u_came.astype(F32)
    a_wide, b_wide = split * LANES, (len(pairs) - split) * LANES
    if fast:
        qkv_shard, out_shard, emb_shard, gain_shard, bias_shard, up_bias_shard = finish(
            held, came, a_wide, cols, chunk, up_bias_vector.size, embedding_projection_weight.shape
        )
        out_shard, up_bias_shard = out_shard.T, up_bias_shard[0]
    else:
        shard = held + came.astype(F32)
        a_shard, b_shard = shard[:, : 3 * a_wide + cols], shard[:, 3 * a_wide + cols :]
        qkv_shard = jnp.stack(
            [
                jnp.concatenate(
                    [
                        a_shard[:, i * a_wide : (i + 1) * a_wide],
                        b_shard[:, i * b_wide : (i + 1) * b_wide],
                    ],
                    axis=1,
                )
                for i in range(3)
            ]
        )
        out_shard = a_shard[:, 3 * a_wide :].T
        tail = b_shard[:, 3 * b_wide :].reshape(-1)
        emb_shard = tail[:emb_size].reshape(embedding_projection_weight.shape)
        tail = tail[emb_size:]
        gain_shard = tail[: 2 * chunk].reshape(2, chunk)
        bias_shard = tail[2 * chunk : 8 * chunk].reshape(6, chunk)
        up_bias_shard = tail[8 * chunk : 8 * chunk + up_bias_vector.size]

    def give_back(value, places_of):
        own = half_of(value, core)
        other = swap_cores(half_of(value, 1 - core))
        blank = jnp.zeros((2,) + own.shape, value.dtype)
        blank = lax.dynamic_update_slice(blank, own[None], (places_of[0], 0, 0))
        return lax.dynamic_update_slice(blank, other[None], (places_of[1], 0, 0))

    embeddings = give_back(emb, (core, 1 - core))
    grad_tokens = give_back(g_here, (mine, theirs))
    return (
        embeddings,
        grad_tokens,
        qkv_shard,
        out_shard,
        up_shard,
        down_shard.T,
        emb_shard,
        gain_shard,
        bias_shard,
        up_bias_shard,
    )


def solution(mesh):
    return jax.shard_map(
        body,
        mesh=mesh,
        in_specs=(
            P("dp", "tensor", None),
            P("dp"),
            P("dp", None),
            P("dp", None),
            P(None, "dp", "tensor"),
            P("tensor", "dp"),
            P("dp", "tensor"),
            P("tensor", "dp"),
            P(("dp", "tensor"), None),
            P(None, ("dp", "tensor")),
            P(None, ("dp", "tensor")),
            P(("dp", "tensor")),
            P("dp", "tensor", None),
        ),
        out_specs=(
            P("dp", "tensor", None),
            P("dp", "tensor", None),
            P(None, "dp", "tensor"),
            P("tensor", "dp"),
            P("dp", "tensor"),
            P("tensor", "dp"),
            P(("dp", "tensor"), None),
            P(None, ("dp", "tensor")),
            P(None, ("dp", "tensor")),
            P(("dp", "tensor")),
        ),
        check_vma=False,
    )
```

```python
import functools

import jax
import jax.numpy as jnp
import numpy as np
from jax import lax
from jax.experimental import pallas as pl
from jax.experimental.pallas import tpu as pltpu
from jax.sharding import PartitionSpec as P

HD = 64
LANES = 128
STRIP = 128
F32 = jnp.float32
BF16 = jnp.bfloat16
VMEM_LIMIT = 18 * 1024 * 1024


def nn(left, right):
    return lax.dot_general(left, right, (((1,), (0,)), ((), ())), preferred_element_type=F32)


def nt(left, right):
    return lax.dot_general(left, right, (((1,), (1,)), ((), ())), preferred_element_type=F32)


def swap_cores(value):
    return lax.ppermute(value, "tensor", [(0, 1), (1, 0)])


def after(value, *others):
    return lax.optimization_barrier((value, others))[0]


def together(*values):
    return lax.optimization_barrier(values)


def strips(count, size, step):
    def run(i, carry):
        step(pl.ds(pl.multiple_of(i * size, size), size))
        return carry

    lax.fori_loop(0, count // size, run, 0)


def columns_of(width, step):
    block = 256 if width % 256 == 0 else width

    def run(i, carry):
        step(pl.ds(pl.multiple_of(i * block, block), block))
        return carry

    lax.fori_loop(0, width // block, run, 0)


def call(
    body, outs, args, grid=None, in_specs=None, out_specs=None, scratch=(), flops=0, grant=VMEM_LIMIT
):
    whole = pl.BlockSpec(memory_space=pltpu.VMEM)
    return pl.pallas_call(
        body,
        out_shape=outs,
        grid=grid or (),
        in_specs=in_specs or [whole] * len(args),
        out_specs=out_specs or jax.tree.map(lambda _: whole, outs),
        scratch_shapes=scratch,
        compiler_params=pltpu.CompilerParams(vmem_limit_bytes=grant),
        cost_estimate=pl.CostEstimate(flops=flops, bytes_accessed=1 << 20, transcendentals=0),
    )(*args)


def shaped(shape, dtype):
    return jax.ShapeDtypeStruct(shape, dtype)


ANY = pl.BlockSpec(memory_space=pl.ANY)
WHOLE = pl.BlockSpec(memory_space=pltpu.VMEM)


OTHER = (0, 2, 1, 3)


def load_weights(pieces, target, sems, first=0, last=None, at=(0,) * 8):
    quarter = target.shape[1] // 4
    columns = slice(first, last)
    copies = []
    for side in range(2):
        for place in range(4):
            source = place if side == 0 else 4 + OTHER[place]
            rows = pl.ds(at[source] * quarter, quarter)
            copies.append(
                pltpu.make_async_copy(
                    pieces[source].at[rows, columns],
                    target.at[side, pl.ds(place * quarter, quarter)],
                    sems.at[side, place],
                )
            )
    for copy in copies:
        copy.start()
    return copies


def attention_kernel(
    x_ref, perm_ref, bias_ref, mask_ref, vec_ref, *refs
):
    pieces, refs = refs[:8], refs[8:]
    qkv_ref, lse_ref, att_ref, res_ref, first_ref, low_ref, lowt_ref, xt_ref, w_ref = refs[:9]
    col_ref, rel_ref, sems = refs[9:]
    cols = qkv_ref.shape[2] // 3
    tokens = x_ref.shape[0]
    copies = load_weights(pieces, w_ref, sems, 0, 4 * cols)

    def reorder(span):
        rel_ref[:, span] = nn(x_ref[...], perm_ref[:, span]).astype(BF16)

    columns_of(x_ref.shape[1], reorder)
    xt_ref[...] = rel_ref[...].T
    col_ref[...] = jnp.broadcast_to(mask_ref[...], (LANES, tokens)).T
    for copy in copies:
        copy.wait()

    def project(i, carry):
        half, part = i // 3, i % 3
        span = pl.ds(pl.multiple_of(part * cols, cols), cols)
        made = nn(rel_ref[...], w_ref[half, :, span]) + bias_ref[pl.ds(half, 1), span]
        qkv_ref[half, :, span] = made.astype(BF16)
        return carry

    lax.fori_loop(0, 6, project, 0)
    lane = lax.broadcasted_iota(jnp.int32, (tokens, LANES), 1) < HD
    pairs = cols // LANES


    def pair(step, carry):
        half, i = step // pairs, step % pairs
        off = pl.multiple_of(i * LANES, LANES)
        query = qkv_ref[half, :, pl.ds(off, LANES)] * BF16(HD ** (-0.5))
        key = qkv_ref[half, :, pl.ds(pl.multiple_of(cols + off, LANES), LANES)]
        value = qkv_ref[half, :, pl.ds(pl.multiple_of(2 * cols + off, LANES), LANES)]
        value_t = value.T
        outs = []
        for head in range(2):
            kept = jnp.where(lane == (head == 0), key, jnp.zeros_like(key))
            scores = nt(kept, query)
            scores = scores + jnp.concatenate([col_ref[...]] * (tokens // LANES), axis=1)
            top = jnp.max(scores, axis=0, keepdims=True)
            shifted = jnp.exp(scores - top)
            total = jnp.sum(shifted, axis=0, keepdims=True)
            out = nn(value_t[head * HD : (head + 1) * HD], shifted.astype(BF16))
            outs.append(out / total)
            lse_ref[half, pl.ds(i * 2 + head, 1), :] = top + jnp.log(total)
        both = jnp.concatenate(outs, axis=0).T
        att_ref[half, :, pl.ds(off, LANES)] = both.astype(BF16)
        return carry

    lax.fori_loop(0, 2 * pairs, pair, 0)
    out = slice(3 * cols, 4 * cols)

    def branch(span):
        made = nt(att_ref[0], w_ref[0, span, out]) + nt(att_ref[1], w_ref[1, span, out])
        res_ref[:, span] = made

    columns_of(x_ref.shape[1], branch)

    def norm(rows):
        value = res_ref[rows, :] + vec_ref[4:5, :] + rel_ref[rows, :].astype(F32)
        res_ref[rows, :] = value
        average = jnp.mean(value, axis=-1, keepdims=True)
        centred = value - average
        inverse = lax.rsqrt(jnp.mean(centred * centred, axis=-1, keepdims=True) + 1e-12)
        first = centred * inverse * vec_ref[0:1, :] + vec_ref[5:6, :]
        first_ref[rows, :] = first
        low_ref[rows, :] = first.astype(BF16)

    strips(tokens, STRIP, norm)
    lowt_ref[...] = low_ref[...].T


def attention_forward(x, perm, head_bias, mask, vec, pieces, cols):
    tokens, width = x.shape
    heads = cols // HD
    outs = (
        shaped((2, tokens, 3 * cols), BF16),
        shaped((2, heads, tokens), F32),
        shaped((2, tokens, cols), BF16),
        shaped((tokens, width), F32),
        shaped((tokens, width), F32),
        shaped((tokens, width), BF16),
        shaped((width, tokens), BF16),
        shaped((width, tokens), BF16),
        shaped((2, width, 4 * cols), BF16),
    )
    return call(
        attention_kernel,
        outs,
        (x, perm, head_bias, mask, vec, *pieces),
        in_specs=[WHOLE] * 5 + [ANY] * 8,
        scratch=[
            pltpu.VMEM((tokens, LANES), F32),
            pltpu.VMEM((tokens, width), BF16),
            pltpu.SemaphoreType.DMA((2, 4)),
        ],
        flops=8 * tokens * width * width,
    )


ERF = (0.254829592, -0.284496736, 1.421413741, -1.453152027, 1.061405429)


def gelu_pair(value):
    size = jnp.abs(value)
    bell = jnp.exp(-0.5 * value * value)
    t = 1.0 / (1.0 + (0.3275911 * 0.5**0.5) * size)
    poly = ERF[4]
    for term in ERF[3::-1]:
        poly = poly * t + term
    tail = 0.5 * poly * t * bell
    phi = jnp.where(value >= 0, 1.0 - tail, tail)
    return value * phi, phi + value * bell * 0.3989422804014327


def join_rows(refs, target, swapped):
    quarter = target.shape[0] // 4
    for place in range(4):
        source = OTHER[place] if swapped else place
        target[place * quarter : (place + 1) * quarter, :] = refs[source][...]


def split_rows(value, keep_ref, send_ref, swapped):
    quarter = value.shape[0] // 4
    for place in range(4):
        source = OTHER[place] if swapped else place
        ref = (keep_ref, send_ref)[place // 2]
        rows = slice((place % 2) * quarter, (place % 2 + 1) * quarter)
        ref[rows, :] = value[source * quarter : (source + 1) * quarter, :]


def column_block(hidden):
    return 512 if hidden % 512 == 0 else hidden


def up_forward(low, pieces, bias, swapped):
    tokens, width = low.shape
    pieces, at = zip(*pieces)
    hidden = pieces[0].shape[1]
    block = column_block(hidden)

    def kernel(low_ref, a_ref, b_ref, c_ref, d_ref, bias_ref, hid_ref, slope_ref, acc_ref, w_ref):
        join_rows((a_ref, b_ref, c_ref, d_ref), w_ref, swapped)
        acc_ref[...] = nn(low_ref[...], w_ref[...])

        def act(rows):
            active, slope = gelu_pair(acc_ref[rows, :] + bias_ref[...])
            hid_ref[rows, :] = active.astype(BF16)
            slope_ref[rows, :] = slope.astype(BF16)

        strips(tokens, STRIP, act)

    outs = (shaped((tokens, hidden), BF16), shaped((tokens, hidden), BF16))
    chunk = pl.BlockSpec((tokens, block), lambda i: (0, i))
    parts = [pl.BlockSpec((width // 4, block), lambda i, row=row: (row, i)) for row in at]
    return call(
        kernel,
        outs,
        (low, *pieces, bias),
        grid=(hidden // block,),
        in_specs=[
            pl.BlockSpec((tokens, width), lambda i: (0, 0)),
            *parts,
            pl.BlockSpec((1, block), lambda i: (0, i)),
        ],
        out_specs=(chunk, chunk),
        scratch=[pltpu.VMEM((tokens, block), F32), pltpu.VMEM((width, block), BF16)],
        flops=2 * tokens * width * hidden,
    )


def down_kernel(
    len_ref, h0_ref, h1_ref, first_ref, vec_ref, proj_ref, cot_ref, *refs
):
    both_ref, more_ref, both_other, more_other, *refs = refs
    emb_ref, low_ref, lowt_ref, res_ref, pgrad_ref, sums_ref = refs[:6]
    ffn_ref, norm_ref, sec_ref, gp_ref, gs_ref, inv_ref, prj_ref, w_ref = refs[6:]
    tokens = first_ref.shape[0]
    length = len_ref[0]
    quarter = w_ref.shape[0] // 4
    for place, ref, part in ((0, both_other, 0), (1, more_other, 0), (2, both_other, 1), (3, more_other, 1)):
        w_ref[place * quarter : (place + 1) * quarter] = ref[part * quarter : (part + 1) * quarter]
    for ref, first in ((both_ref, 0), (more_ref, 2 * quarter)):
        span = slice(first, first + 2 * quarter)
        ffn_ref[:, span] = nt(h0_ref[...], ref[...]) + nt(h1_ref[...], w_ref[span])

    def norm(rows):
        value = first_ref[rows, :] + ffn_ref[rows, :] + vec_ref[6:7, :]
        average = jnp.mean(value, axis=-1, keepdims=True)
        centred = value - average
        inverse = lax.rsqrt(jnp.mean(centred * centred, axis=-1, keepdims=True) + 1e-12)
        normed = centred * inverse
        norm_ref[rows, :] = normed
        inv_ref[rows, :] = jnp.broadcast_to(inverse, (STRIP, LANES))
        sec_ref[rows, :] = (normed * vec_ref[1:2, :] + vec_ref[7:8, :]).astype(BF16)

    strips(tokens, STRIP, norm)
    prj_ref[...] = nn(sec_ref[...], proj_ref[...])

    def embed(rows):
        projected = prj_ref[rows, :]
        valid = rows.start + lax.broadcasted_iota(jnp.int32, projected.shape, 0) < length
        valid = valid.astype(F32)
        scale = lax.rsqrt(jnp.sum(projected * projected, axis=-1, keepdims=True) + 1e-06)
        unit = projected * scale
        emb_ref[rows, :] = unit * valid
        cot = cot_ref[rows, :] * valid
        back = scale * (cot - unit * jnp.sum(unit * cot, axis=-1, keepdims=True))
        gp_ref[rows, :] = back.astype(BF16)

    strips(tokens, STRIP, embed)
    pgrad_ref[...] = nn(sec_ref[...].T, gp_ref[...])
    gs_ref[...] = nt(gp_ref[...], proj_ref[...])
    sums_ref[...] = jnp.zeros_like(sums_ref)

    def back(rows):
        grad = gs_ref[rows, :]
        normed = norm_ref[rows, :]
        scaled = grad * vec_ref[1:2, :]
        inside = (
            scaled
            - jnp.mean(scaled, axis=-1, keepdims=True)
            - normed * jnp.mean(scaled * normed, axis=-1, keepdims=True)
        )
        value = inside * inv_ref[rows, 0:1]
        low = value.astype(BF16)
        res_ref[rows, :] = value
        low_ref[rows, :] = low
        fold = lambda v: jnp.sum(v.reshape(STRIP // 8, 8, v.shape[1]), axis=0)
        sums_ref[0:8, :] += fold(grad * normed)
        sums_ref[8:16, :] += fold(grad)
        sums_ref[16:24, :] += fold(low.astype(F32))

    strips(tokens, STRIP, back)
    lowt_ref[...] = low_ref[...].T


def down_both(length, hidden, pieces, first, vec, proj, cot):
    tokens, width = first.shape
    embed = proj.shape[1]
    outs = (
        shaped((tokens, embed), F32),
        shaped((tokens, width), BF16),
        shaped((width, tokens), BF16),
        shaped((tokens, width), F32),
        shaped((width, embed), F32),
        shaped((24, width), F32),
    )
    args = (length, *hidden, first, vec, proj, cot, *pieces)
    return call(
        down_kernel,
        outs,
        args,
        in_specs=[pl.BlockSpec(memory_space=pltpu.SMEM)] + [WHOLE] * 10,
        scratch=[
            pltpu.VMEM((tokens, width), F32),
            pltpu.VMEM((tokens, width), F32),
            pltpu.VMEM((tokens, width), BF16),
            pltpu.VMEM((tokens, embed), BF16),
            pltpu.VMEM((tokens, width), F32),
            pltpu.VMEM((tokens, LANES), F32),
            pltpu.VMEM((tokens, embed), F32),
            pltpu.VMEM((width, hidden[0].shape[1]), BF16),
        ],
        flops=2 * tokens * width * hidden[0].shape[1] * 2,
    )


def down_grad(g_low_t, hid, swapped):
    width, tokens = g_low_t.shape
    hidden = hid.shape[1]
    block = column_block(hidden)

    def kernel(gt_ref, hid_ref, keep_ref, send_ref):
        split_rows(nn(gt_ref[...], hid_ref[...]).astype(BF16), keep_ref, send_ref, swapped)

    piece = pl.BlockSpec((width // 2, block), lambda i: (0, i))
    out = shaped((width // 2, hidden), BF16)
    return call(
        kernel,
        (out, out),
        (g_low_t, hid),
        grid=(hidden // block,),
        in_specs=[
            pl.BlockSpec((width, tokens), lambda i: (0, 0)),
            pl.BlockSpec((tokens, block), lambda i: (0, i)),
        ],
        out_specs=(piece, piece),
        flops=2 * tokens * width * hidden,
    )


def up_grad(g_low, low_t, slope, down, up, start, swapped, biases):
    tokens, width = g_low.shape
    pieces, at = zip(*down, *up)
    hidden = slope.shape[1]
    block = column_block(hidden)

    def kernel(g_ref, lowt_ref, slope_ref, start_ref, *refs):
        wd_ref, wu_ref = refs[-2:]
        join_rows(refs[:4], wd_ref, swapped)
        join_rows(refs[4:8], wu_ref, swapped)
        more, refs = refs[8 : 8 + len(biases)], refs[8 + len(biases) :]
        keep_ref, send_ref, bias_ref, first_ref, gh_ref, gin_ref = refs[:-2]
        def matmul(span):
            gh_ref[:, span] = nn(g_ref[...], wd_ref[:, span])

        columns_of(block, matmul)
        bias_ref[...] = jnp.zeros_like(bias_ref)
        for ref in more:
            bias_ref[8:16, :] = ref[...]

        def act(rows):
            grad = (gh_ref[rows, :] * slope_ref[rows, :].astype(F32)).astype(BF16)
            gin_ref[rows, :] = grad
            wide = grad.astype(F32)
            bias_ref[0:8, :] += jnp.sum(wide.reshape(STRIP // 8, 8, wide.shape[1]), axis=0)

        strips(tokens, STRIP, act)
        split_rows(nn(lowt_ref[...], gin_ref[...]).astype(BF16), keep_ref, send_ref, swapped)
        @pl.when(pl.program_id(0) == 0)
        def _():
            first_ref[...] = start_ref[...]

        def add(span):
            first_ref[:, span] += nt(gin_ref[...], wu_ref[span, :])

        columns_of(width, add)

    row = pl.BlockSpec((tokens, width), lambda i: (0, 0))
    turned = pl.BlockSpec((width, tokens), lambda i: (0, 0))
    act = pl.BlockSpec((tokens, block), lambda i: (0, i))
    piece = pl.BlockSpec((width // 2, block), lambda i: (0, i))
    parts = [pl.BlockSpec((width // 4, block), lambda i, row=row: (row, i)) for row in at]
    thin = pl.BlockSpec((8, block), lambda i: (0, i))
    out = shaped((width // 2, hidden), BF16)
    return call(
        kernel,
        (out, out, shaped((8 * (1 + len(biases)), hidden), F32), shaped((tokens, width), F32)),
        (g_low, low_t, slope, start, *pieces, *biases),
        grid=(hidden // block,),
        in_specs=[row, turned, act, row] + parts + [thin] * len(biases),
        out_specs=(
            piece,
            piece,
            pl.BlockSpec((8 * (1 + len(biases)), block), lambda i: (0, i)),
            row,
        ),
        scratch=[
            pltpu.VMEM((tokens, block), F32),
            pltpu.VMEM((tokens, block), BF16),
            pltpu.VMEM((width, block), BF16),
            pltpu.VMEM((width, block), BF16),
        ],
        flops=6 * tokens * width * hidden,
    )


def norm_back(g_first, res, vec, weights, sums_two, cols):
    tokens, width = g_first.shape

    def kernel(
        gf_ref, res_ref, vec_ref, w_ref, two_ref, gres_ref, turn_ref, gatt_ref, sums_ref, low_ref
    ):
        sums_ref[0:24, :] = jnp.zeros((24, width), F32)
        sums_ref[24:48, :] = two_ref[...]

        def back(rows):
            value = res_ref[rows, :]
            average = jnp.mean(value, axis=-1, keepdims=True)
            centred = value - average
            inverse = lax.rsqrt(jnp.mean(centred * centred, axis=-1, keepdims=True) + 1e-12)
            normed = centred * inverse
            grad = gf_ref[rows, :]
            scaled = grad * vec_ref[0:1, :]
            inside = (
                scaled
                - jnp.mean(scaled, axis=-1, keepdims=True)
                - normed * jnp.mean(scaled * normed, axis=-1, keepdims=True)
            )
            out = inside * inverse
            low = out.astype(BF16)
            gres_ref[rows, :] = out
            low_ref[rows, :] = low
            fold = lambda v: jnp.sum(v.reshape(STRIP // 8, 8, v.shape[1]), axis=0)
            sums_ref[0:8, :] += fold(grad * normed)
            sums_ref[8:16, :] += fold(grad)
            sums_ref[16:24, :] += fold(low.astype(F32))

        strips(tokens, STRIP, back)
        turn_ref[...] = low_ref[...].T
        for half in range(2):
            gatt_ref[half] = nn(low_ref[...], w_ref[half, :, 3 * cols :]).astype(BF16)

    outs = (
        shaped((tokens, width), F32),
        shaped((width, tokens), BF16),
        shaped((2, tokens, cols), BF16),
        shaped((48, width), F32),
    )
    return call(
        kernel,
        outs,
        (g_first, res, vec, weights, sums_two),
        scratch=[pltpu.VMEM((tokens, width), BF16)],
        flops=4 * tokens * width * cols,
    )


def attention_back(pairs, g_att, att, qkv, lse, mask, earlier=()):
    tokens, cols = att.shape[1:]
    wide = len(pairs) * LANES
    scale = HD ** (-0.5)

    before = sum(part.shape[3] for part in earlier)

    def kernel(gatt_ref, att_ref, qkv_ref, lse_ref, mask_ref, *refs):
        gqkv_ref, sums_ref, col_ref = refs[len(earlier) :]
        for ref in refs[: len(earlier)]:
            sums_ref[:, :, :, 0:before] = ref[...]
        col_ref[...] = jnp.broadcast_to(mask_ref[...], (LANES, tokens)).T
        lane = lax.broadcasted_iota(jnp.int32, (tokens, LANES), 1) < HD

        def pair(step, carry):
            half, place = step // len(pairs), step % len(pairs)
            i = pairs[0] + place
            off = pl.multiple_of(i * LANES, LANES)
            off_k = pl.multiple_of(cols + off, LANES)
            off_v = pl.multiple_of(2 * cols + off, LANES)
            query = qkv_ref[half, :, pl.ds(off, LANES)] * BF16(scale)
            key = qkv_ref[half, :, pl.ds(off_k, LANES)]
            value = qkv_ref[half, :, pl.ds(off_v, LANES)]
            grad = gatt_ref[half, :, pl.ds(off, LANES)]
            out = att_ref[half, :, pl.ds(off, LANES)]
            key_t = (key * BF16(scale)).T
            delta = (grad.astype(F32) * out.astype(F32)).T
            g_query, g_key, g_value = [], [], []
            for head in range(2):
                pick = lane == (head == 0)
                span = slice(head * HD, (head + 1) * HD)
                zero = jnp.zeros_like(key)
                scores = nt(jnp.where(pick, key, zero), query)
                scores = scores + jnp.concatenate([col_ref[...]] * (tokens // LANES), axis=1)
                probs = jnp.exp(scores - lse_ref[half, pl.ds(i * 2 + head, 1), :])
                g_probs = nt(jnp.where(pick, value, zero), grad)
                row_delta = jnp.sum(delta[span], axis=0, keepdims=True)
                g_scores = (probs * (g_probs - row_delta)).astype(BF16)
                g_value.append(nn(probs.astype(BF16), grad))
                g_key.append(nn(g_scores, query))
                g_query.append(nn(key_t[span], g_scores))
            g_q = jnp.concatenate(g_query, axis=0).T.astype(BF16)
            g_v = jnp.where(lane, *g_value).astype(BF16)
            to = pl.multiple_of(place * LANES, LANES)
            gqkv_ref[half, :, pl.ds(to, LANES)] = g_q
            to_k = pl.ds(pl.multiple_of(wide + to, LANES), LANES)
            gqkv_ref[half, :, to_k] = jnp.where(lane, *g_key).astype(BF16)
            gqkv_ref[half, :, pl.ds(pl.multiple_of(2 * wide + to, LANES), LANES)] = g_v
            for row, grads in ((0, g_q), (1, g_v)):
                total = jnp.sum(grads.astype(F32).reshape(-1, 8, LANES), axis=0)
                place_to = pl.ds(pl.multiple_of(before + to, LANES), LANES)
                sums_ref[half, row, :, place_to] = total
            return carry

        lax.fori_loop(0, 2 * len(pairs), pair, 0)

    return call(
        kernel,
        (shaped((2, tokens, 3 * wide), BF16), shaped((2, 2, 8, before + wide), F32)),
        (g_att, att, qkv, lse, mask, *earlier),
        scratch=[pltpu.VMEM((tokens, LANES), F32)],
        flops=20 * tokens * tokens * wide * 2,
    )


def project_other(x_t, g_qkv, beside):
    width, tokens = x_t.shape
    columns = g_qkv.shape[2]
    extra = beside[1].shape[2] if beside else 0

    def kernel(xt_ref, g_ref, *refs):
        keep_ref, send_ref = refs[len(beside) :]
        span = slice(0, columns)
        made = nn(xt_ref[...], g_ref[1]).astype(BF16)
        split_rows(made, keep_ref.at[:, span], send_ref.at[:, span], True)
        if beside:
            span = slice(columns, columns + extra)
            made = nn(refs[0][...], refs[1][1]).astype(BF16)
            split_rows(made, keep_ref.at[:, span], send_ref.at[:, span], True)

    out = shaped((width // 2, columns + extra), BF16)
    return call(
        kernel,
        (out, out),
        (x_t, g_qkv, *beside),
        flops=2 * tokens * width * (columns + extra),
    )


def project_own(x_t, g_qkv, beside, small, keep_came, send_came):
    width, tokens = x_t.shape
    columns = g_qkv.shape[2]
    extra = beside[1].shape[2] if beside else 0
    tail = small[0].shape[1] if small else 0
    middle = width // 2
    count = len(beside) + len(small)

    def kernel(xt_ref, g_ref, kc_ref, sc_ref, *refs):
        keep_ref, send_ref = refs[count:]
        for out, came, first in ((keep_ref, kc_ref, 0), (send_ref, sc_ref, middle)):
            rows = slice(first, first + middle)
            span = slice(0, columns)
            made = nn(xt_ref[rows, :], g_ref[0])
            out[:, span] = (made + came[:, span].astype(F32)).astype(BF16)
            if beside:
                span = slice(columns, columns + extra)
                made = nn(refs[0][rows, :], refs[1][0])
                out[:, span] = (made + came[:, span].astype(F32)).astype(BF16)
            if small:
                total = refs[count - 2][rows, :].astype(F32) + refs[count - 1][rows, :].astype(F32)
                out[:, columns + extra :] = total.astype(BF16)

    out = shaped((middle, columns + extra + tail), BF16)
    return call(
        kernel,
        (out, out),
        (x_t, g_qkv, keep_came, send_came, *beside, *small),
        flops=2 * tokens * width * (columns + extra),
    )


def token_back(g_parts, start, perm, weights, cols):
    tokens, width = start.shape
    widths = [part.shape[2] // 3 for part in g_parts]

    def kernel(a_ref, b_ref, start_ref, perm_ref, w_ref, out_ref, g_ref, high_ref, rest_ref):
        for half in range(2):
            for kind in range(3):
                to = kind * cols
                for ref, wide in zip((a_ref, b_ref), widths):
                    taken = ref[half, :, kind * wide : (kind + 1) * wide]
                    g_ref[half, :, to : to + wide] = taken
                    to += wide
        used = slice(0, 3 * cols)

        def matmul(span):
            made = nt(g_ref[0], w_ref[0, span, used]) + nt(g_ref[1], w_ref[1, span, used])
            made = start_ref[:, span] + made
            high = made.astype(BF16)
            high_ref[:, span] = high
            rest_ref[:, span] = (made - high.astype(F32)).astype(BF16)

        columns_of(width, matmul)

        def reorder(span):
            turn = perm_ref[span, :]
            out_ref[:, span] = nt(high_ref[...], turn) + nt(rest_ref[...], turn)

        columns_of(width, reorder)

    return call(
        kernel,
        shaped((tokens, width), F32),
        (*g_parts, start, perm, weights),
        scratch=[
            pltpu.VMEM((2, tokens, 3 * cols), BF16),
            pltpu.VMEM((tokens, width), BF16),
            pltpu.VMEM((tokens, width), BF16),
        ],
        flops=16 * tokens * width * cols,
    )


class Exchange:
    def __init__(self, size):
        self.size = size
        self.depth = size.bit_length() - 1
        self.rank = lax.axis_index("dp")
        self.core = lax.axis_index("tensor")
        outer = list(range(self.depth - 1, 1, -1))
        self.bits = (outer + [1, 0], outer + [0, 1])

    def flip(self, value, *steps):
        pairs = []
        for i in range(self.size):
            for core in range(2):
                to = i
                for step in steps:
                    to ^= 1 << self.bits[core][step]
                pairs.append((i * 2 + core, to * 2 + core))
        return lax.ppermute(value, ("dp", "tensor"), pairs)

    def last_outer(self):
        low, high = self.depth - 4, self.depth - 3
        return (low,), (high,), (low, high)

    def flip_three(self, values):
        return [self.flip(value, *steps) for value, steps in zip(values, self.last_outer())]

    def blocks(self):
        tables = []
        for bits in self.bits:
            tables.append(
                [
                    sum(((j >> step) & 1) << bit for step, bit in enumerate(bits))
                    for j in range(self.size)
                ]
            )
        table = np.array(tables, np.int32)
        return jnp.where(self.core == 0, table[0], table[1]) ^ self.rank


def join(*parts):
    return jnp.concatenate(parts, axis=0)


def added(*values):
    total = values[0].astype(F32)
    for value in values[1:]:
        total = total + value.astype(F32)
    return total


def halves(value):
    middle = value.shape[0] // 2
    return value[:middle], value[middle:]


def three_parts(value):
    high = lax.reduce_precision(value, 8, 7)
    rest = value - high
    middle = lax.reduce_precision(rest, 8, 7)
    return (high.astype(BF16), middle.astype(BF16), (rest - middle).astype(BF16))


SMALL = 48
UP = 32


def pack(qkv_w, out_w, emb_w, gains, biases, up_bias):
    rows, cols = out_w.shape
    chunk = gains.shape[1]
    args = (qkv_w, out_w, emb_w, gains, biases, up_bias[None])

    def kernel(*refs):
        one_ref, refs, vec_ref, sems = refs[6], (*refs[:6], *refs[7:13]), refs[13], refs[14]
        copies = []
        for place in range(6):
            copies.append(pltpu.make_async_copy(refs[place], refs[6 + place], sems.at[place]))
        for copy in copies:
            copy.start()
        for copy in copies:
            copy.wait()
        q_ref, o_ref, e_ref, g_ref, b_ref, u_ref = refs[6:]
        for part in range(3):
            one_ref[:, part * cols : (part + 1) * cols] = q_ref[part]
        one_ref[:, 3 * cols : 4 * cols] = o_ref[...]
        vec_ref[...] = jnp.zeros_like(vec_ref)
        vec_ref[0:2, 0:chunk] = g_ref[...]
        vec_ref[2:8, 0:chunk] = b_ref[...]
        vec_ref[0:1, UP : UP + u_ref.shape[1]] = u_ref[...]
        value = vec_ref[...]
        high = value.astype(BF16).astype(F32)
        middle = (value - high).astype(BF16).astype(F32)
        block = [e_ref[...].astype(F32), high, middle, value - high - middle]
        one_ref[:, 4 * cols :] = jnp.concatenate(block, axis=0).astype(BF16)

    return call(
        kernel,
        shaped((rows, 4 * cols + LANES), BF16),
        args,
        in_specs=[pl.BlockSpec(memory_space=pltpu.HBM)] * 6,
        scratch=[pltpu.VMEM(arg.shape, arg.dtype) for arg in args]
        + [pltpu.VMEM((8, LANES), F32), pltpu.SemaphoreType.DMA((6,))],
        grant=60 * 1024 * 1024,
    )


def spreads(sides, width, hidden, chunk, up_chunk):
    lane = jnp.arange(LANES, dtype=jnp.int32)[:, None]
    column = jnp.arange(width, dtype=jnp.int32)[None]
    up_column = jnp.arange(hidden, dtype=jnp.int32)[None]
    thin, broad = [], []
    for side in sides:
        thin.append((lane < chunk) & (column % (2 * chunk) == side * chunk + lane))
        broad.append((lane >= UP) & (up_column % (2 * up_chunk) == side * up_chunk + lane - UP))
    return jnp.stack(thin).astype(BF16), jnp.stack(broad).astype(BF16)


def unpack(core, pieces, thin, broad, rel, absolute, up_rel, cols):
    width, hidden = thin.shape[2], broad.shape[2]
    count = width // SMALL

    def kernel(core_ref, thin_ref, broad_ref, rel_ref, abs_ref, up_ref, *refs):
        vec_ref, head_ref, side_ref, proj_ref, e_ref, sems = refs[8:]
        copies = load_weights(refs[:8], e_ref, sems, 4 * cols, 4 * cols + LANES)
        for copy in copies:
            copy.wait()
        first = core_ref[0] == 0
        blocks = [e_ref[side].astype(F32).reshape(count, SMALL, LANES) for side in range(2)]
        tops = [block[:, : SMALL // 2] for block in blocks]
        halves = [jnp.where(first, tops[0], tops[1]), jnp.where(first, tops[1], tops[0])]
        proj_ref[...] = jnp.concatenate(halves, axis=1).reshape(width, LANES).astype(BF16)
        flat = lax.broadcasted_iota(jnp.int32, (count, count * 8), 1)
        pick = flat == 8 * lax.broadcasted_iota(jnp.int32, (count, count * 8), 0)
        pick = pick.astype(F32).astype(BF16)
        vec = jnp.zeros((8, width), F32)
        plain = jnp.zeros((8, width), F32)
        wide = jnp.zeros((1, hidden), F32)
        index = lax.broadcasted_iota(jnp.int32, (count, hidden), 0)
        for side in range(2):
            placed, up_placed = None, None
            for part in (2, 1, 0):
                start = SMALL // 2 + 8 * part
                rows = blocks[side][:, start : start + 8].reshape(count * 8, LANES).astype(BF16)
                spread = nn(rows, thin_ref[side])
                up_spread = nn(nn(pick, rows).astype(BF16), broad_ref[side])
                placed = spread if placed is None else placed + spread
                up_placed = up_spread if up_placed is None else up_placed + up_spread
            for j in range(count):
                row = placed[8 * j : 8 * j + 8]
                vec = vec + jnp.where(rel_ref[...] == j, row, 0.0)
                plain = plain + jnp.where(abs_ref[...] == j, row, 0.0)
            chosen = jnp.where(up_ref[...] == index, up_placed, 0.0)
            wide = wide + jnp.sum(chosen, axis=0, keepdims=True)
        vec_ref[...] = vec
        for side in range(2):
            low_half = first if side == 0 else jnp.logical_not(first)
            part = jnp.where(low_half, plain[:, :cols], plain[:, cols:])
            head_ref[side : side + 1, :cols] = part[2:3]
            head_ref[side : side + 1, cols : 2 * cols] = jnp.zeros((1, cols), F32)
            head_ref[side : side + 1, 2 * cols :] = part[3:4]
            middle = hidden // 2
            side_ref[side : side + 1, :] = jnp.where(low_half, wide[:, :middle], wide[:, middle:])

    outs = (
        shaped((8, width), F32),
        shaped((2, 3 * cols), F32),
        shaped((2, hidden // 2), F32),
        shaped((width, LANES), BF16),
    )
    return call(
        kernel,
        outs,
        (core[None], thin, broad, rel, absolute, up_rel, *pieces),
        in_specs=[pl.BlockSpec(memory_space=pltpu.SMEM)] + [WHOLE] * 5 + [ANY] * 8,
        scratch=[pltpu.VMEM((2, width, LANES), BF16), pltpu.SemaphoreType.DMA((2, 4))],
    )


def pack_grads(
    core, thin, broad, rel, absolute, up_rel, sums, up_sums, head_sums, proj_grad,
):
    width, hidden = thin.shape[2], broad.shape[2]
    count = width // SMALL

    def kernel(
        core_ref, thin_ref, broad_ref, rel_ref, abs_ref, up_ref, sums_ref, ups_ref, heads_ref,
        pg_ref, own_ref, other_ref,
    ):
        first = core_ref[0] == 0
        fold = lambda v: jnp.sum(v, axis=0, keepdims=True)

        def ordered(own, other):
            low, high = jnp.where(first, own, other), jnp.where(first, other, own)
            return jnp.concatenate([low, high], axis=1)

        def heads(half, kind):
            return fold(heads_ref[half, kind])

        rows = [
            fold(sums_ref[0:8]),
            fold(sums_ref[24:32]),
            ordered(heads(0, 0), heads(1, 0)),
            ordered(heads(0, 1), heads(1, 1)),
            fold(sums_ref[16:24]),
            fold(sums_ref[8:16]),
            fold(sums_ref[40:48]),
            fold(sums_ref[32:40]),
        ]
        grads = jnp.concatenate(rows, axis=0)
        row = lax.broadcasted_iota(jnp.int32, (8, width), 0)
        block = jnp.where((row == 2) | (row == 3), abs_ref[...], rel_ref[...])
        spread = [jnp.where(block == j, grads, 0.0) for j in range(count)]
        spread = jnp.concatenate(spread, axis=0)
        high = spread.astype(BF16)
        rest = (spread - high.astype(F32)).astype(BF16)
        up = ordered(fold(ups_ref[0:8]), fold(ups_ref[8:16]))
        index = lax.broadcasted_iota(jnp.int32, (count, hidden), 0)
        up = jnp.where(up_ref[...] == index, up, 0.0)
        up_high = up.astype(BF16)
        up_rest = (up - up_high.astype(F32)).astype(BF16)
        flat = lax.broadcasted_iota(jnp.int32, (count * 8, count), 0)
        put = flat == 8 * lax.broadcasted_iota(jnp.int32, (count * 8, count), 1)
        put = put.astype(F32).astype(BF16)
        tops = pg_ref[...].reshape(count, SMALL, LANES)
        for side, out_ref in enumerate((own_ref, other_ref)):
            low_half = first if side == 0 else jnp.logical_not(first)
            top = jnp.where(low_half, tops[:, : SMALL // 2], tops[:, SMALL // 2 :])
            thin_part = nt(high, thin_ref[side]) + nt(rest, thin_ref[side])
            up_part = nt(up_high, broad_ref[side]) + nt(up_rest, broad_ref[side])
            vec = (thin_part + nn(put, up_part.astype(BF16))).reshape(count, 8, LANES)
            blank = jnp.zeros((count, SMALL // 2 - 8, LANES), F32)
            made = jnp.concatenate([top, vec, blank], axis=1).reshape(width, LANES).astype(BF16)
            quarter = width // 4
            for place in range(4):
                source = OTHER[place] if side == 1 else place
                out_ref[place * quarter : (place + 1) * quarter, :] = made[
                    source * quarter : (source + 1) * quarter
                ]

    out = shaped((width, LANES), BF16)
    return call(
        kernel,
        (out, out),
        (
            core[None], thin, broad, rel, absolute, up_rel, sums, up_sums, head_sums, proj_grad,
        ),
        in_specs=[pl.BlockSpec(memory_space=pltpu.SMEM)] + [WHOLE] * 9,
    )


def finish(kept, came, a_wide, cols, chunk, up_chunk, emb_shape):
    rows = kept.shape[0]
    b_wide = cols - a_wide
    beside = 3 * a_wide
    second = beside + cols

    def kernel(kept_ref, *refs):
        qkv_ref, out_ref, emb_ref, gain_ref, bias_ref, up_ref, sum_ref = refs[len(came) :]
        total = kept_ref[...]
        for ref in refs[: len(came)]:
            total = total + ref[...].astype(F32)
        sum_ref[...] = total
        for part in range(3):
            qkv_ref[part, :, :a_wide] = sum_ref[:, part * a_wide : (part + 1) * a_wide]
            start = second + part * b_wide
            qkv_ref[part, :, a_wide:] = sum_ref[:, start : start + b_wide]
        out_ref[...] = sum_ref[:, beside:second]
        first = second + 3 * b_wide
        half = SMALL // 2
        emb_ref[...] = sum_ref[0:half, first:]
        gain_ref[...] = sum_ref[half : half + 2, first : first + chunk]
        bias_ref[...] = sum_ref[half + 2 : half + 8, first : first + chunk]
        up_ref[...] = sum_ref[half : half + 1, first + UP : first + UP + up_chunk]

    outs = (
        shaped((3, rows, cols), F32),
        shaped((rows, cols), F32),
        shaped(emb_shape, F32),
        shaped((2, chunk), F32),
        shaped((6, chunk), F32),
        shaped((1, up_chunk), F32),
    )
    return call(kernel, outs, (kept, *came), scratch=[pltpu.VMEM(kept.shape, F32)])


def pack_plain(qkv_w, out_w, emb_w, gains, biases, up_bias):
    rows = out_w.shape[0]
    vector = jnp.concatenate([gains.reshape(-1), biases.reshape(-1), up_bias])
    pad_to = -(-vector.size // LANES) * LANES
    padded = jnp.pad(vector, (0, pad_to - vector.size))
    flat = jnp.concatenate([emb_w.reshape(-1), *three_parts(padded)])
    extra = -(-flat.size // (rows * LANES)) * LANES
    flat = jnp.pad(flat, (0, rows * extra - flat.size)).reshape(rows, extra)
    one = jnp.concatenate([qkv_w[0], qkv_w[1], qkv_w[2], out_w, flat], axis=1)
    sizes = (rows, extra, emb_w.size, gains.shape[1], up_bias.size, pad_to)
    return one, sizes


def unpack_plain(core, sides, pieces, blocks, sizes):
    rows, extra, emb_size, chunk, up_chunk, pad_to = sizes
    size = blocks.shape[0]
    width = size * rows
    cols = width // 2
    ff_local = size * up_chunk
    pieces = [part[:, 4 * cols :] for part in pieces]
    own = jnp.concatenate(pieces[:4])
    other = jnp.concatenate([pieces[4 + place] for place in OTHER])
    small = [part.reshape(size, rows * extra) for part in (own, other)]
    small = jnp.where(core == 0, jnp.stack(small, 1), jnp.stack(small[::-1], 1))
    proj = small[:, :, :emb_size].reshape(width, -1)
    thirds = small[:, :, emb_size : emb_size + 3 * pad_to].astype(F32)
    thirds = thirds.reshape(size, 2, 3, pad_to)
    vectors = thirds[:, :, 0] + (thirds[:, :, 1] + thirds[:, :, 2])
    plain = vectors[jnp.argsort(blocks)].reshape(size * 2, pad_to)
    vectors = vectors.reshape(size * 2, pad_to)
    vec = jnp.moveaxis(vectors[:, : 8 * chunk].reshape(-1, 8, chunk), 1, 0).reshape(8, width)
    query_bias = plain[:, 2 * chunk : 3 * chunk].reshape(-1)
    value_bias = plain[:, 3 * chunk : 4 * chunk].reshape(-1)
    up_bias = plain[:, 8 * chunk : 8 * chunk + up_chunk].reshape(-1)
    head_bias, side_bias = [], []
    for side in sides:
        query_part = lax.dynamic_slice_in_dim(query_bias, side * cols, cols)
        value_part = lax.dynamic_slice_in_dim(value_bias, side * cols, cols)
        head_bias.append(jnp.concatenate([query_part, jnp.zeros_like(query_part), value_part]))
        side_bias.append(lax.dynamic_slice_in_dim(up_bias, side * ff_local, ff_local))
    return vec, jnp.stack(head_bias), jnp.stack(side_bias), proj


def pack_grads_plain(
    core, blocks, sizes, sums, up_sums, head_sums, proj_grad
):
    rows, extra, emb_size, chunk, up_chunk, pad_to = sizes
    size = blocks.shape[0]

    def fold(value):
        return jnp.sum(value.reshape(-1, 8, value.shape[-1]), axis=1)

    def absolute(own, other):
        return jnp.where(
            core == 0, jnp.concatenate([own, other]), jnp.concatenate([other, own])
        )

    def relative(value):
        return value.reshape(size, 2, -1)[blocks]

    gain_one, shift_one, out_bias, gain_two, shift_two, ffn_bias = (
        row.reshape(size, 2, chunk) for row in fold(sums)
    )
    own, other = jnp.sum(head_sums, axis=2)
    small = jnp.concatenate(
        [
            proj_grad.reshape(size, 2, emb_size),
            gain_one,
            gain_two,
            relative(absolute(own[0], other[0])),
            relative(absolute(own[1], other[1])),
            out_bias,
            shift_one,
            ffn_bias,
            shift_two,
            relative(absolute(*fold(up_sums))),
        ],
        axis=2,
    ).astype(BF16)
    small = jnp.pad(small, ((0, 0), (0, 0), (0, rows * extra - small.shape[2])))
    small = jnp.where(core == 0, small, small[:, ::-1])
    own, other = jnp.moveaxis(small, 1, 0).reshape(2, size * rows, extra)
    first, second, third, fourth = jnp.split(other, 4)
    return own, jnp.concatenate([first, third, second, fourth])


def body(
    tokens,
    lengths,
    key_mask,
    order,
    query_key_value_weight,
    output_projection_weight,
    up_projection_weight,
    down_projection_weight,
    embedding_projection_weight,
    gains,
    biases,
    up_bias_vector,
    cotangent,
):
    size = lax.axis_size("dp")
    core = lax.axis_index("tensor")
    ways = Exchange(size)
    depth = ways.depth
    half_len = tokens.shape[1]
    full_len = key_mask.shape[1]
    width = tokens.shape[2]
    cols = output_projection_weight.shape[0]
    rows = output_projection_weight.shape[1]
    ff_local = up_projection_weight.shape[1]
    chunk = gains.shape[1]
    emb_size = embedding_projection_weight.size
    sides = (core, 1 - core)

    fast = rows == SMALL and emb_size == SMALL // 2 * LANES and up_bias_vector.size <= LANES - UP
    small_args = (
        query_key_value_weight,
        output_projection_weight.T,
        embedding_projection_weight,
        gains,
        biases,
        up_bias_vector,
    )
    if fast:
        one = pack(*small_args)
    else:
        one, small_sizes = pack_plain(*small_args)

    wide = 4 * cols
    seconds, lasts = depth - 2, depth - 1
    for step in range(depth - 4):
        one = join(one, ways.flip(one, step))
    tokens, order, lengths, key_mask = after((tokens, order, lengths, key_mask), one)
    mine = order[0, core]
    theirs = order[0, 1 - core]
    my_half = lax.dynamic_index_in_dim(tokens, mine, 0, keepdims=False)
    their_half = lax.dynamic_index_in_dim(tokens, theirs, 0, keepdims=False)
    blocks = ways.blocks()
    one_came = ways.flip_three([one] * 3)
    if fast:
        thin, broad = spreads(sides, width, 2 * ff_local, chunk, up_bias_vector.size)
        places_of = jnp.argsort(blocks)
        rel = (jnp.arange(width, dtype=jnp.int32) // rows)[None]
        absolute = jnp.repeat(places_of, rows)[None].astype(jnp.int32)
        up_rel = jnp.repeat(places_of, 2 * up_bias_vector.size)[None].astype(jnp.int32)
        *one_came, thin, broad, rel, absolute, up_rel = together(
            *one_came, thin, broad, rel, absolute, up_rel
        )
        tables = (core, thin, broad, rel, absolute, up_rel)

    def in_order(own, other):
        return jnp.where(
            core == 0, jnp.concatenate([own, other]), jnp.concatenate([other, own])
        )

    def half_of(value, which):
        return lax.dynamic_slice_in_dim(value, which * half_len, half_len)

    seq_len = lengths[mine]
    marks = lax.dynamic_index_in_dim(key_mask, mine, 0, keepdims=False)
    places = jnp.arange(full_len, dtype=jnp.int32)
    key_ok = (places < seq_len) & ((marks == 1) | (places == 0))
    mask = jnp.where(key_ok, 0.0, -1e30).astype(F32)[None, :]
    where = (blocks[:, None] * rows + jnp.arange(rows, dtype=jnp.int32)[None]).reshape(-1)
    perm = (jnp.arange(width, dtype=jnp.int32)[:, None] == where[None]).astype(BF16)
    two, three = after((up_projection_weight, down_projection_weight.T), order)
    for step in range(depth - 4):
        two = join(two, ways.flip(two, step))
        three = join(three, ways.flip(three, step))
    one = join(one, *one_came)
    here = in_order(my_half, swap_cores(after(their_half, one)))
    two_came = ways.flip_three([after(two, one)] * 3)
    one_b, one_c, here, mask, perm, *two_came = together(
        ways.flip(one, seconds), ways.flip(one, lasts), here, mask, perm, *two_came
    )
    two = join(two, *two_came)
    one_other = together(swap_cores(one), swap_cores(one_b), swap_cores(one_c))
    three_came = ways.flip_three([after(three, two, *one_other)] * 3)
    one_d, two_b, *three_came = together(
        ways.flip(one_b, lasts), ways.flip(two, seconds), *three_came
    )
    three = join(three, *three_came)
    two_both = join(two, two_b)
    one_pieces = (one, one_b, one_c, one_d, *one_other, swap_cores(one_d))
    two_more, three_b = ways.flip(two_both, lasts), ways.flip(three, seconds)
    one_pieces = together(*one_pieces, two_both, three)[:8]
    if fast:
        vec, head_bias, side_bias, proj = unpack(core, one_pieces, *tables[1:], cols)
    else:
        vec, head_bias, side_bias, proj = unpack_plain(
            core, sides, one_pieces, blocks, small_sizes
        )
    side_bias = (side_bias[0:1], side_bias[1:2])

    qkv, lse, att, res_one, first, first_low, first_low_t, here_t, weights = attention_forward(
        here, perm, head_bias, mask, vec, one_pieces, cols
    )
    two_more, three_b = after((two_more, three_b), first_low)
    three_both = join(three, three_b)
    three_more = ways.flip(three_both, lasts)
    two_other = [swap_cores(part) for part in (two_both, two_more)]

    def quarters(both, more):
        return ((both, 0), (both, 1), (more, 0), (more, 1))

    two_own = quarters(two_both, two_more)
    hid_own, slope_own = up_forward(
        after(first_low, three_both, two_more), two_own, side_bias[0], False
    )
    two_other = quarters(*after(two_other, hid_own))
    three_both_other = swap_cores(three_both)
    cot_mine = lax.dynamic_index_in_dim(cotangent, core, 0, keepdims=False)
    cot_other = lax.dynamic_index_in_dim(cotangent, 1 - core, 0, keepdims=False)
    cot = in_order(cot_mine, after(swap_cores(after(cot_other, first_low)), hid_own))
    hid_other, slope_other = up_forward(after(first_low, cot), two_other, side_bias[1], True)
    three_more, three_both_other = after((three_more, three_both_other), hid_other)
    three_more_other = swap_cores(three_more)
    three_own = quarters(three_both, three_more)
    three_other = quarters(three_both_other, three_more_other)
    emb, g_ffn, g_ffn_t, g_res_two, proj_grad, sums_two = down_both(
        seq_len[None],
        (hid_own, hid_other),
        (three_both, three_more, three_both_other, three_more_other),
        first,
        vec,
        proj,
        cot,
    )

    def low(*values):
        return added(*values).astype(BF16)

    def spread(value):
        kept, sent = halves(value)
        return kept, sent.astype(BF16)

    def quarter_out(value):
        kept, *sent = jnp.split(value, 4)
        return kept, [part.astype(BF16) for part in sent]

    dk_other, ds_other = down_grad(g_ffn_t, hid_other, True)
    ds_came, dk_came = swap_cores(ds_other), swap_cores(dk_other)
    dk, ds = down_grad(g_ffn_t, after(hid_own, ds_other), False)
    ds_came = after(ds_came, ds)
    d_high = low(halves(ds)[1], halves(ds_came)[1])
    d_low = low(halves(ds)[0], halves(ds_came)[0])
    d_came_high = ways.flip(d_high, lasts)
    uk_other, us_other, up_bias_other, part = up_grad(
        after(g_ffn, d_high, d_low),
        first_low_t,
        slope_other,
        three_other,
        two_other,
        g_res_two,
        True,
        (),
    )
    us_came, uk_came = swap_cores(us_other), swap_cores(uk_other)
    d_came_high, dk_came, d_low = after((d_came_high, dk_came, d_low), us_other)
    d_came_low = ways.flip(d_low, lasts)
    uk, us, up_bias, g_first = up_grad(
        after(g_ffn, us_other, d_came_high),
        first_low_t,
        slope_own,
        three_own,
        two_own,
        part,
        False,
        (up_bias_other,),
    )
    d_came_low, us_came, uk_came = after((d_came_low, us_came, uk_came), us)
    u_sent = low(us, us_came)
    u_came = ways.flip(u_sent, lasts)
    d_sent = low(halves(dk)[1], halves(dk_came)[1], d_came_high)
    d_held = added(halves(dk)[0], halves(dk_came)[0], d_came_low)
    d_came = ways.flip(d_sent, seconds)
    g_res_one, g_branch_t, g_att, sums = norm_back(
        after(g_first, u_sent, d_sent), res_one, vec, weights, sums_two, cols
    )
    pairs = list(range(cols // LANES))
    split = (len(pairs) + 1) // 2
    g_a, bias_a = attention_back(pairs[:split], g_att, att, qkv, lse, mask)
    beside = (g_branch_t, att)
    ak_other, as_other = project_other(here_t, g_a, beside)
    as_came, ak_came = swap_cores(as_other), swap_cores(ak_other)
    g_b, head_sums = attention_back(
        pairs[split:], after(g_att, as_other), att, qkv, lse, mask, (bias_a,)
    )
    as_came, ak_came = after((as_came, ak_came), g_b)
    a_keep, a_send = project_own(here_t, g_a, beside, (), ak_came, as_came)
    d_came, u_came = after((d_came, u_came), a_send)
    a_came = ways.flip(a_send, lasts)
    u_sent = low(halves(uk)[1], halves(uk_came)[1], halves(u_came)[1])
    u_held = added(halves(uk)[0], halves(uk_came)[0], halves(u_came)[0])
    u_came = ways.flip(u_sent, seconds)
    d_held, d_sent = quarter_out(d_held + d_came.astype(F32))
    d_came = ways.flip_three(d_sent)
    bk_other, bs_other = project_other(here_t, after(g_b, a_send, u_sent, d_sent), ())
    bs_came, bk_came = swap_cores(bs_other), swap_cores(bk_other)
    if fast:
        small_own, small_other = pack_grads(
            *tables, after(sums, bs_other), up_bias, head_sums, proj_grad
        )
    else:
        small_own, small_other = pack_grads_plain(
            core, blocks, small_sizes, sums, up_bias, head_sums, proj_grad
        )
    small_came = swap_cores(small_other)
    bs_came, bk_came = after((bs_came, bk_came), small_other)
    b_keep, b_send = project_own(here_t, g_b, (), (small_own, small_came), bk_came, bs_came)
    u_came, a_came = after((u_came, a_came), b_send)
    b_came = ways.flip(b_send, lasts)
    a_sent = low(halves(a_keep)[1], halves(a_came)[1])
    a_held = added(halves(a_keep)[0], halves(a_came)[0])
    a_came = ways.flip(a_sent, seconds)
    u_held, u_sent = quarter_out(after(u_held, a_sent) + u_came.astype(F32))
    u_came = ways.flip_three(u_sent)
    b_came = after(b_came, *u_sent)
    b_sent = low(halves(b_keep)[1], halves(b_came)[1])
    b_held = added(halves(b_keep)[0], halves(b_came)[0])
    b_came = ways.flip(b_sent, seconds)
    g_here = token_back(
        (after(g_a, b_send, a_sent, b_sent, *u_sent, *d_came), g_b), g_res_one, perm, weights, cols
    )
    a_came, b_came, u_came, emb = after((a_came, b_came, u_came, emb), g_here)
    held = jnp.concatenate([a_held + a_came.astype(F32), b_held + b_came.astype(F32)], axis=1)
    held, sent = quarter_out(held)
    came = ways.flip_three(sent)
    d_came, u_came, u_held = after((d_came, u_came, u_held), *sent)
    d_held, u_held = added(d_held, *d_came), added(u_held, *u_came)
    for step in range(depth - 5, -1, -1):
        held, sent = spread(added(held, *came))
        came = [ways.flip(sent, step)]
        d_held, sent = spread(d_held)
        d_held = d_held + ways.flip(sent, step).astype(F32)
        u_held, sent = spread(u_held)
        u_held = u_held + ways.flip(sent, step).astype(F32)
    down_shard, up_shard = d_held, u_held
    a_wide, b_wide = split * LANES, (len(pairs) - split) * LANES
    if fast:
        qkv_shard, out_shard, emb_shard, gain_shard, bias_shard, up_bias_shard = finish(
            held, came, a_wide, cols, chunk, up_bias_vector.size, embedding_projection_weight.shape
        )
        out_shard, up_bias_shard = out_shard.T, up_bias_shard[0]
    else:
        shard = added(held, *came)
        a_shard, b_shard = shard[:, : 3 * a_wide + cols], shard[:, 3 * a_wide + cols :]
        qkv_shard = jnp.stack(
            [
                jnp.concatenate(
                    [
                        a_shard[:, i * a_wide : (i + 1) * a_wide],
                        b_shard[:, i * b_wide : (i + 1) * b_wide],
                    ],
                    axis=1,
                )
                for i in range(3)
            ]
        )
        out_shard = a_shard[:, 3 * a_wide :].T
        tail = b_shard[:, 3 * b_wide :].reshape(-1)
        emb_shard = tail[:emb_size].reshape(embedding_projection_weight.shape)
        tail = tail[emb_size:]
        gain_shard = tail[: 2 * chunk].reshape(2, chunk)
        bias_shard = tail[2 * chunk : 8 * chunk].reshape(6, chunk)
        up_bias_shard = tail[8 * chunk : 8 * chunk + up_bias_vector.size]

    def give_back(value, places_of):
        own = half_of(value, core)
        other = swap_cores(half_of(value, 1 - core))
        blank = jnp.zeros((2,) + own.shape, value.dtype)
        blank = lax.dynamic_update_slice(blank, own[None], (places_of[0], 0, 0))
        return lax.dynamic_update_slice(blank, other[None], (places_of[1], 0, 0))

    embeddings = give_back(emb, (core, 1 - core))
    grad_tokens = give_back(g_here, (mine, theirs))
    return (
        embeddings,
        grad_tokens,
        qkv_shard,
        out_shard,
        up_shard,
        down_shard.T,
        emb_shard,
        gain_shard,
        bias_shard,
        up_bias_shard,
    )


def solution(mesh):
    return jax.shard_map(
        body,
        mesh=mesh,
        in_specs=(
            P("dp", "tensor", None),
            P("dp"),
            P("dp", None),
            P("dp", None),
            P(None, "dp", "tensor"),
            P("tensor", "dp"),
            P("dp", "tensor"),
            P("tensor", "dp"),
            P(("dp", "tensor"), None),
            P(None, ("dp", "tensor")),
            P(None, ("dp", "tensor")),
            P(("dp", "tensor")),
            P("dp", "tensor", None),
        ),
        out_specs=(
            P("dp", "tensor", None),
            P("dp", "tensor", None),
            P(None, "dp", "tensor"),
            P("tensor", "dp"),
            P("dp", "tensor"),
            P("tensor", "dp"),
            P(("dp", "tensor"), None),
            P(None, ("dp", "tensor")),
            P(None, ("dp", "tensor")),
            P(("dp", "tensor")),
        ),
        check_vma=False,
    )
```

```python
import functools

import jax
import jax.numpy as jnp
import numpy as np
from jax import lax
from jax.experimental import pallas as pl
from jax.experimental.pallas import tpu as pltpu
from jax.sharding import PartitionSpec as P

HD = 64
LANES = 128
STRIP = 128
F32 = jnp.float32
BF16 = jnp.bfloat16
VMEM_LIMIT = 15 * 1024 * 1024


def nn(left, right):
    return lax.dot_general(left, right, (((1,), (0,)), ((), ())), preferred_element_type=F32)


def nt(left, right):
    return lax.dot_general(left, right, (((1,), (1,)), ((), ())), preferred_element_type=F32)


def swap_cores(value):
    return lax.ppermute(value, "tensor", [(0, 1), (1, 0)])


def after(value, *others):
    return lax.optimization_barrier((value, others))[0]


def together(*values):
    return lax.optimization_barrier(values)


def strips(count, size, step):
    def run(i, carry):
        step(pl.ds(pl.multiple_of(i * size, size), size))
        return carry

    lax.fori_loop(0, count // size, run, 0)


def columns_of(width, step):
    block = 256 if width % 256 == 0 else width

    def run(i, carry):
        step(pl.ds(pl.multiple_of(i * block, block), block))
        return carry

    lax.fori_loop(0, width // block, run, 0)


def call(
    body, outs, args, grid=None, in_specs=None, out_specs=None, scratch=(), flops=0, grant=VMEM_LIMIT
):
    whole = pl.BlockSpec(memory_space=pltpu.VMEM)
    return pl.pallas_call(
        body,
        out_shape=outs,
        grid=grid or (),
        in_specs=in_specs or [whole] * len(args),
        out_specs=out_specs or jax.tree.map(lambda _: whole, outs),
        scratch_shapes=scratch,
        compiler_params=pltpu.CompilerParams(vmem_limit_bytes=grant),
        cost_estimate=pl.CostEstimate(flops=flops, bytes_accessed=1 << 20, transcendentals=0),
    )(*args)


def shaped(shape, dtype):
    return jax.ShapeDtypeStruct(shape, dtype)


ANY = pl.BlockSpec(memory_space=pl.ANY)
WHOLE = pl.BlockSpec(memory_space=pltpu.VMEM)


OTHER = (0, 2, 1, 3)


def load_weights(pieces, target, sems, first=0, last=None, at=(0,) * 8):
    quarter = target.shape[1] // 4
    columns = slice(first, last)
    copies = []
    for side in range(2):
        for place in range(4):
            source = place if side == 0 else 4 + OTHER[place]
            rows = pl.ds(at[source] * quarter, quarter)
            copies.append(
                pltpu.make_async_copy(
                    pieces[source].at[rows, columns],
                    target.at[side, pl.ds(place * quarter, quarter)],
                    sems.at[side, place],
                )
            )
    for copy in copies:
        copy.start()
    return copies


def attention_kernel(
    x_ref, perm_ref, bias_ref, mask_ref, vec_ref, *refs
):
    pieces, refs = refs[:8], refs[8:]
    qkv_ref, lse_ref, att_ref, res_ref, first_ref, low_ref, lowt_ref, xt_ref, w_ref = refs[:9]
    col_ref, rel_ref, sems = refs[9:]
    cols = qkv_ref.shape[2] // 3
    tokens = x_ref.shape[0]
    copies = load_weights(pieces, w_ref, sems, 0, 4 * cols)

    def reorder(span):
        rel_ref[:, span] = nn(x_ref[...], perm_ref[:, span]).astype(BF16)

    columns_of(x_ref.shape[1], reorder)
    xt_ref[...] = rel_ref[...].T
    col_ref[...] = jnp.broadcast_to(mask_ref[...], (LANES, tokens)).T
    for copy in copies:
        copy.wait()

    def project(i, carry):
        half, part = i // 3, i % 3
        span = pl.ds(pl.multiple_of(part * cols, cols), cols)
        made = nn(rel_ref[...], w_ref[half, :, span]) + bias_ref[pl.ds(half, 1), span]
        qkv_ref[half, :, span] = made.astype(BF16)
        return carry

    lax.fori_loop(0, 6, project, 0)
    lane = lax.broadcasted_iota(jnp.int32, (tokens, LANES), 1) < HD
    pairs = cols // LANES


    def pair(step, carry):
        half, i = step // pairs, step % pairs
        off = pl.multiple_of(i * LANES, LANES)
        query = qkv_ref[half, :, pl.ds(off, LANES)] * BF16(HD ** (-0.5))
        key = qkv_ref[half, :, pl.ds(pl.multiple_of(cols + off, LANES), LANES)]
        value = qkv_ref[half, :, pl.ds(pl.multiple_of(2 * cols + off, LANES), LANES)]
        value_t = value.T
        outs = []
        for head in range(2):
            kept = jnp.where(lane == (head == 0), key, jnp.zeros_like(key))
            scores = nt(kept, query)
            scores = scores + jnp.concatenate([col_ref[...]] * (tokens // LANES), axis=1)
            top = jnp.max(scores, axis=0, keepdims=True)
            shifted = jnp.exp(scores - top)
            total = jnp.sum(shifted, axis=0, keepdims=True)
            out = nn(value_t[head * HD : (head + 1) * HD], shifted.astype(BF16))
            outs.append(out / total)
            lse_ref[half, pl.ds(i * 2 + head, 1), :] = top + jnp.log(total)
        both = jnp.concatenate(outs, axis=0).T
        att_ref[half, :, pl.ds(off, LANES)] = both.astype(BF16)
        return carry

    lax.fori_loop(0, 2 * pairs, pair, 0)
    out = slice(3 * cols, 4 * cols)

    def branch(span):
        made = nt(att_ref[0], w_ref[0, span, out]) + nt(att_ref[1], w_ref[1, span, out])
        res_ref[:, span] = made

    columns_of(x_ref.shape[1], branch)

    def norm(rows):
        value = res_ref[rows, :] + vec_ref[4:5, :] + rel_ref[rows, :].astype(F32)
        res_ref[rows, :] = value
        average = jnp.mean(value, axis=-1, keepdims=True)
        centred = value - average
        inverse = lax.rsqrt(jnp.mean(centred * centred, axis=-1, keepdims=True) + 1e-12)
        first = centred * inverse * vec_ref[0:1, :] + vec_ref[5:6, :]
        first_ref[rows, :] = first
        low_ref[rows, :] = first.astype(BF16)

    strips(tokens, STRIP, norm)
    lowt_ref[...] = low_ref[...].T


def attention_forward(x, perm, head_bias, mask, vec, pieces, cols):
    tokens, width = x.shape
    heads = cols // HD
    outs = (
        shaped((2, tokens, 3 * cols), BF16),
        shaped((2, heads, tokens), F32),
        shaped((2, tokens, cols), BF16),
        shaped((tokens, width), F32),
        shaped((tokens, width), F32),
        shaped((tokens, width), BF16),
        shaped((width, tokens), BF16),
        shaped((width, tokens), BF16),
        shaped((2, width, 4 * cols), BF16),
    )
    return call(
        attention_kernel,
        outs,
        (x, perm, head_bias, mask, vec, *pieces),
        in_specs=[WHOLE] * 5 + [ANY] * 8,
        scratch=[
            pltpu.VMEM((tokens, LANES), F32),
            pltpu.VMEM((tokens, width), BF16),
            pltpu.SemaphoreType.DMA((2, 4)),
        ],
        flops=8 * tokens * width * width,
    )


ERF = (0.254829592, -0.284496736, 1.421413741, -1.453152027, 1.061405429)


def gelu_pair(value):
    size = jnp.abs(value)
    bell = jnp.exp(-0.5 * value * value)
    t = 1.0 / (1.0 + (0.3275911 * 0.5**0.5) * size)
    poly = ERF[4]
    for term in ERF[3::-1]:
        poly = poly * t + term
    tail = 0.5 * poly * t * bell
    phi = jnp.where(value >= 0, 1.0 - tail, tail)
    return value * phi, phi + value * bell * 0.3989422804014327


def join_rows(refs, target, swapped):
    quarter = target.shape[0] // 4
    for place in range(4):
        source = OTHER[place] if swapped else place
        target[place * quarter : (place + 1) * quarter, :] = refs[source][...]


def split_rows(value, keep_ref, send_ref, swapped):
    quarter = value.shape[0] // 4
    for place in range(4):
        source = OTHER[place] if swapped else place
        ref = (keep_ref, send_ref)[place // 2]
        rows = slice((place % 2) * quarter, (place % 2 + 1) * quarter)
        ref[rows, :] = value[source * quarter : (source + 1) * quarter, :]


def column_block(hidden):
    return 512 if hidden % 512 == 0 else hidden


def up_forward(low, pieces, bias, swapped):
    tokens, width = low.shape
    pieces, at = zip(*pieces)
    hidden = pieces[0].shape[1]
    block = column_block(hidden)

    def kernel(low_ref, a_ref, b_ref, c_ref, d_ref, bias_ref, hid_ref, slope_ref, acc_ref, w_ref):
        join_rows((a_ref, b_ref, c_ref, d_ref), w_ref, swapped)
        acc_ref[...] = nn(low_ref[...], w_ref[...])

        def act(rows):
            active, slope = gelu_pair(acc_ref[rows, :] + bias_ref[...])
            hid_ref[rows, :] = active.astype(BF16)
            slope_ref[rows, :] = slope.astype(BF16)

        strips(tokens, STRIP, act)

    outs = (shaped((tokens, hidden), BF16), shaped((tokens, hidden), BF16))
    chunk = pl.BlockSpec((tokens, block), lambda i: (0, i))
    parts = [pl.BlockSpec((width // 4, block), lambda i, row=row: (row, i)) for row in at]
    return call(
        kernel,
        outs,
        (low, *pieces, bias),
        grid=(hidden // block,),
        in_specs=[
            pl.BlockSpec((tokens, width), lambda i: (0, 0)),
            *parts,
            pl.BlockSpec((1, block), lambda i: (0, i)),
        ],
        out_specs=(chunk, chunk),
        scratch=[pltpu.VMEM((tokens, block), F32), pltpu.VMEM((width, block), BF16)],
        flops=2 * tokens * width * hidden,
    )


def down_kernel(
    len_ref, h0_ref, h1_ref, first_ref, vec_ref, proj_ref, cot_ref, *refs
):
    both_ref, more_ref, both_other, more_other, *refs = refs
    emb_ref, low_ref, lowt_ref, res_ref, pgrad_ref, sums_ref = refs[:6]
    ffn_ref, norm_ref, sec_ref, gp_ref, gs_ref, inv_ref, prj_ref, w_ref = refs[6:]
    tokens = first_ref.shape[0]
    length = len_ref[0]
    quarter = w_ref.shape[0] // 4
    for place, ref, part in ((0, both_other, 0), (1, more_other, 0), (2, both_other, 1), (3, more_other, 1)):
        w_ref[place * quarter : (place + 1) * quarter] = ref[part * quarter : (part + 1) * quarter]
    for ref, first in ((both_ref, 0), (more_ref, 2 * quarter)):
        span = slice(first, first + 2 * quarter)
        ffn_ref[:, span] = nt(h0_ref[...], ref[...]) + nt(h1_ref[...], w_ref[span])

    def norm(rows):
        value = first_ref[rows, :] + ffn_ref[rows, :] + vec_ref[6:7, :]
        average = jnp.mean(value, axis=-1, keepdims=True)
        centred = value - average
        inverse = lax.rsqrt(jnp.mean(centred * centred, axis=-1, keepdims=True) + 1e-12)
        normed = centred * inverse
        norm_ref[rows, :] = normed
        inv_ref[rows, :] = jnp.broadcast_to(inverse, (STRIP, LANES))
        sec_ref[rows, :] = (normed * vec_ref[1:2, :] + vec_ref[7:8, :]).astype(BF16)

    strips(tokens, STRIP, norm)
    prj_ref[...] = nn(sec_ref[...], proj_ref[...])

    def embed(rows):
        projected = prj_ref[rows, :]
        valid = rows.start + lax.broadcasted_iota(jnp.int32, projected.shape, 0) < length
        valid = valid.astype(F32)
        scale = lax.rsqrt(jnp.sum(projected * projected, axis=-1, keepdims=True) + 1e-06)
        unit = projected * scale
        emb_ref[rows, :] = unit * valid
        cot = cot_ref[rows, :] * valid
        back = scale * (cot - unit * jnp.sum(unit * cot, axis=-1, keepdims=True))
        gp_ref[rows, :] = back.astype(BF16)

    strips(tokens, STRIP, embed)
    pgrad_ref[...] = nn(sec_ref[...].T, gp_ref[...])
    gs_ref[...] = nt(gp_ref[...], proj_ref[...])
    sums_ref[...] = jnp.zeros_like(sums_ref)

    def back(rows):
        grad = gs_ref[rows, :]
        normed = norm_ref[rows, :]
        scaled = grad * vec_ref[1:2, :]
        inside = (
            scaled
            - jnp.mean(scaled, axis=-1, keepdims=True)
            - normed * jnp.mean(scaled * normed, axis=-1, keepdims=True)
        )
        value = inside * inv_ref[rows, 0:1]
        low = value.astype(BF16)
        res_ref[rows, :] = value
        low_ref[rows, :] = low
        fold = lambda v: jnp.sum(v.reshape(STRIP // 8, 8, v.shape[1]), axis=0)
        sums_ref[0:8, :] += fold(grad * normed)
        sums_ref[8:16, :] += fold(grad)
        sums_ref[16:24, :] += fold(low.astype(F32))

    strips(tokens, STRIP, back)
    lowt_ref[...] = low_ref[...].T


def down_both(length, hidden, pieces, first, vec, proj, cot):
    tokens, width = first.shape
    embed = proj.shape[1]
    outs = (
        shaped((tokens, embed), F32),
        shaped((tokens, width), BF16),
        shaped((width, tokens), BF16),
        shaped((tokens, width), F32),
        shaped((width, embed), F32),
        shaped((24, width), F32),
    )
    args = (length, *hidden, first, vec, proj, cot, *pieces)
    return call(
        down_kernel,
        outs,
        args,
        in_specs=[pl.BlockSpec(memory_space=pltpu.SMEM)] + [WHOLE] * 10,
        scratch=[
            pltpu.VMEM((tokens, width), F32),
            pltpu.VMEM((tokens, width), F32),
            pltpu.VMEM((tokens, width), BF16),
            pltpu.VMEM((tokens, embed), BF16),
            pltpu.VMEM((tokens, width), F32),
            pltpu.VMEM((tokens, LANES), F32),
            pltpu.VMEM((tokens, embed), F32),
            pltpu.VMEM((width, hidden[0].shape[1]), BF16),
        ],
        flops=2 * tokens * width * hidden[0].shape[1] * 2,
    )


def down_grad(g_low_t, hid, swapped):
    width, tokens = g_low_t.shape
    hidden = hid.shape[1]
    block = column_block(hidden)

    def kernel(gt_ref, hid_ref, keep_ref, send_ref):
        split_rows(nn(gt_ref[...], hid_ref[...]).astype(BF16), keep_ref, send_ref, swapped)

    piece = pl.BlockSpec((width // 2, block), lambda i: (0, i))
    out = shaped((width // 2, hidden), BF16)
    return call(
        kernel,
        (out, out),
        (g_low_t, hid),
        grid=(hidden // block,),
        in_specs=[
            pl.BlockSpec((width, tokens), lambda i: (0, 0)),
            pl.BlockSpec((tokens, block), lambda i: (0, i)),
        ],
        out_specs=(piece, piece),
        flops=2 * tokens * width * hidden,
    )


def up_grad(g_low, low_t, slope, down, up, start, swapped, biases):
    tokens, width = g_low.shape
    hidden = slope.shape[1]
    block = column_block(hidden)
    quarter = width // 4
    count = 8 * (1 + len(biases))

    def kernel(g_ref, lowt_ref, slope_ref, start_ref, db_ref, dm_ref, ub_ref, um_ref, *refs):
        more, refs = refs[: len(biases)], refs[len(biases) :]
        keep_ref, send_ref, bias_ref, first_ref, gh_ref, gin_ref, wd_ref, wu_ref = refs
        first_ref[...] = start_ref[...]
        bias_ref[...] = jnp.zeros_like(bias_ref)
        for ref in more:
            bias_ref[8:16, :] = ref[...]

        def chunk(i, carry):
            here = pl.ds(pl.multiple_of(i * block, block), block)
            for target, both_ref, more_ref in ((wd_ref, db_ref, dm_ref), (wu_ref, ub_ref, um_ref)):
                for place in range(4):
                    source = OTHER[place] if swapped else place
                    ref = (both_ref, more_ref)[source // 2]
                    rows = slice((source % 2) * quarter, (source % 2 + 1) * quarter)
                    target[place * quarter : (place + 1) * quarter, :] = ref[rows, here]

            def matmul(span):
                gh_ref[:, span] = nn(g_ref[...], wd_ref[:, span])

            columns_of(block, matmul)

            def act(rows):
                grad = (gh_ref[rows, :] * slope_ref[rows, here].astype(F32)).astype(BF16)
                gin_ref[rows, :] = grad
                wide = grad.astype(F32)
                total = jnp.sum(wide.reshape(STRIP // 8, 8, wide.shape[1]), axis=0)
                bias_ref[0:8, here] += total

            strips(tokens, STRIP, act)
            made = nn(lowt_ref[...], gin_ref[...]).astype(BF16)
            split_rows(made, keep_ref.at[:, here], send_ref.at[:, here], swapped)

            def add(span):
                first_ref[:, span] += nt(gin_ref[...], wu_ref[span, :])

            columns_of(width, add)
            return carry

        lax.fori_loop(0, hidden // block, chunk, 0)

    out = shaped((width // 2, hidden), BF16)
    return call(
        kernel,
        (out, out, shaped((count, hidden), F32), shaped((tokens, width), F32)),
        (g_low, low_t, slope, start, *down, *up, *biases),
        scratch=[
            pltpu.VMEM((tokens, block), F32),
            pltpu.VMEM((tokens, block), BF16),
            pltpu.VMEM((width, block), BF16),
            pltpu.VMEM((width, block), BF16),
        ],
        flops=6 * tokens * width * hidden,
    )


def norm_back(g_first, res, vec, weights, sums_two, cols):
    tokens, width = g_first.shape

    def kernel(
        gf_ref, res_ref, vec_ref, w_ref, two_ref, gres_ref, turn_ref, gatt_ref, sums_ref, low_ref
    ):
        sums_ref[0:24, :] = jnp.zeros((24, width), F32)
        sums_ref[24:48, :] = two_ref[...]

        def back(rows):
            value = res_ref[rows, :]
            average = jnp.mean(value, axis=-1, keepdims=True)
            centred = value - average
            inverse = lax.rsqrt(jnp.mean(centred * centred, axis=-1, keepdims=True) + 1e-12)
            normed = centred * inverse
            grad = gf_ref[rows, :]
            scaled = grad * vec_ref[0:1, :]
            inside = (
                scaled
                - jnp.mean(scaled, axis=-1, keepdims=True)
                - normed * jnp.mean(scaled * normed, axis=-1, keepdims=True)
            )
            out = inside * inverse
            low = out.astype(BF16)
            gres_ref[rows, :] = out
            low_ref[rows, :] = low
            fold = lambda v: jnp.sum(v.reshape(STRIP // 8, 8, v.shape[1]), axis=0)
            sums_ref[0:8, :] += fold(grad * normed)
            sums_ref[8:16, :] += fold(grad)
            sums_ref[16:24, :] += fold(low.astype(F32))

        strips(tokens, STRIP, back)
        turn_ref[...] = low_ref[...].T
        for half in range(2):
            gatt_ref[half] = nn(low_ref[...], w_ref[half, :, 3 * cols :]).astype(BF16)

    outs = (
        shaped((tokens, width), F32),
        shaped((width, tokens), BF16),
        shaped((2, tokens, cols), BF16),
        shaped((48, width), F32),
    )
    return call(
        kernel,
        outs,
        (g_first, res, vec, weights, sums_two),
        scratch=[pltpu.VMEM((tokens, width), BF16)],
        flops=4 * tokens * width * cols,
    )


def attention_back(pairs, g_att, att, qkv, lse, mask, earlier=()):
    tokens, cols = att.shape[1:]
    wide = len(pairs) * LANES
    scale = HD ** (-0.5)

    before = sum(part.shape[3] for part in earlier)

    def kernel(gatt_ref, att_ref, qkv_ref, lse_ref, mask_ref, *refs):
        gqkv_ref, sums_ref, col_ref = refs[len(earlier) :]
        for ref in refs[: len(earlier)]:
            sums_ref[:, :, :, 0:before] = ref[...]
        col_ref[...] = jnp.broadcast_to(mask_ref[...], (LANES, tokens)).T
        lane = lax.broadcasted_iota(jnp.int32, (tokens, LANES), 1) < HD

        def pair(step, carry):
            half, place = step // len(pairs), step % len(pairs)
            i = pairs[0] + place
            off = pl.multiple_of(i * LANES, LANES)
            off_k = pl.multiple_of(cols + off, LANES)
            off_v = pl.multiple_of(2 * cols + off, LANES)
            query = qkv_ref[half, :, pl.ds(off, LANES)] * BF16(scale)
            key = qkv_ref[half, :, pl.ds(off_k, LANES)]
            value = qkv_ref[half, :, pl.ds(off_v, LANES)]
            grad = gatt_ref[half, :, pl.ds(off, LANES)]
            out = att_ref[half, :, pl.ds(off, LANES)]
            key_t = (key * BF16(scale)).T
            delta = (grad.astype(F32) * out.astype(F32)).T
            g_query, g_key, g_value = [], [], []
            for head in range(2):
                pick = lane == (head == 0)
                span = slice(head * HD, (head + 1) * HD)
                zero = jnp.zeros_like(key)
                scores = nt(jnp.where(pick, key, zero), query)
                scores = scores + jnp.concatenate([col_ref[...]] * (tokens // LANES), axis=1)
                probs = jnp.exp(scores - lse_ref[half, pl.ds(i * 2 + head, 1), :])
                g_probs = nt(jnp.where(pick, value, zero), grad)
                row_delta = jnp.sum(delta[span], axis=0, keepdims=True)
                g_scores = (probs * (g_probs - row_delta)).astype(BF16)
                g_value.append(nn(probs.astype(BF16), grad))
                g_key.append(nn(g_scores, query))
                g_query.append(nn(key_t[span], g_scores))
            g_q = jnp.concatenate(g_query, axis=0).T.astype(BF16)
            g_v = jnp.where(lane, *g_value).astype(BF16)
            to = pl.multiple_of(place * LANES, LANES)
            gqkv_ref[half, :, pl.ds(to, LANES)] = g_q
            to_k = pl.ds(pl.multiple_of(wide + to, LANES), LANES)
            gqkv_ref[half, :, to_k] = jnp.where(lane, *g_key).astype(BF16)
            gqkv_ref[half, :, pl.ds(pl.multiple_of(2 * wide + to, LANES), LANES)] = g_v
            for row, grads in ((0, g_q), (1, g_v)):
                total = jnp.sum(grads.astype(F32).reshape(-1, 8, LANES), axis=0)
                place_to = pl.ds(pl.multiple_of(before + to, LANES), LANES)
                sums_ref[half, row, :, place_to] = total
            return carry

        lax.fori_loop(0, 2 * len(pairs), pair, 0)

    return call(
        kernel,
        (shaped((2, tokens, 3 * wide), BF16), shaped((2, 2, 8, before + wide), F32)),
        (g_att, att, qkv, lse, mask, *earlier),
        scratch=[pltpu.VMEM((tokens, LANES), F32)],
        flops=20 * tokens * tokens * wide * 2,
    )


def project_other(x_t, g_qkv, beside):
    width, tokens = x_t.shape
    columns = g_qkv.shape[2]
    extra = beside[1].shape[2] if beside else 0

    def kernel(xt_ref, g_ref, *refs):
        keep_ref, send_ref = refs[len(beside) :]
        span = slice(0, columns)
        made = nn(xt_ref[...], g_ref[1]).astype(BF16)
        split_rows(made, keep_ref.at[:, span], send_ref.at[:, span], True)
        if beside:
            span = slice(columns, columns + extra)
            made = nn(refs[0][...], refs[1][1]).astype(BF16)
            split_rows(made, keep_ref.at[:, span], send_ref.at[:, span], True)

    out = shaped((width // 2, columns + extra), BF16)
    return call(
        kernel,
        (out, out),
        (x_t, g_qkv, *beside),
        flops=2 * tokens * width * (columns + extra),
    )


def project_own(x_t, g_qkv, beside, small, keep_came, send_came):
    width, tokens = x_t.shape
    columns = g_qkv.shape[2]
    extra = beside[1].shape[2] if beside else 0
    tail = small[0].shape[1] if small else 0
    middle = width // 2
    count = len(beside) + len(small)

    def kernel(xt_ref, g_ref, kc_ref, sc_ref, *refs):
        keep_ref, send_ref = refs[count:]
        for out, came, first in ((keep_ref, kc_ref, 0), (send_ref, sc_ref, middle)):
            rows = slice(first, first + middle)
            span = slice(0, columns)
            made = nn(xt_ref[rows, :], g_ref[0])
            out[:, span] = (made + came[:, span].astype(F32)).astype(BF16)
            if beside:
                span = slice(columns, columns + extra)
                made = nn(refs[0][rows, :], refs[1][0])
                out[:, span] = (made + came[:, span].astype(F32)).astype(BF16)
            if small:
                total = refs[count - 2][rows, :].astype(F32) + refs[count - 1][rows, :].astype(F32)
                out[:, columns + extra :] = total.astype(BF16)

    out = shaped((middle, columns + extra + tail), BF16)
    return call(
        kernel,
        (out, out),
        (x_t, g_qkv, keep_came, send_came, *beside, *small),
        flops=2 * tokens * width * (columns + extra),
    )


def token_back(g_parts, start, perm, weights, cols):
    tokens, width = start.shape
    widths = [part.shape[2] // 3 for part in g_parts]

    def kernel(a_ref, b_ref, start_ref, perm_ref, w_ref, out_ref, g_ref, high_ref, rest_ref):
        for half in range(2):
            for kind in range(3):
                to = kind * cols
                for ref, wide in zip((a_ref, b_ref), widths):
                    taken = ref[half, :, kind * wide : (kind + 1) * wide]
                    g_ref[half, :, to : to + wide] = taken
                    to += wide
        used = slice(0, 3 * cols)

        def matmul(span):
            made = nt(g_ref[0], w_ref[0, span, used]) + nt(g_ref[1], w_ref[1, span, used])
            made = start_ref[:, span] + made
            high = made.astype(BF16)
            high_ref[:, span] = high
            rest_ref[:, span] = (made - high.astype(F32)).astype(BF16)

        columns_of(width, matmul)

        def reorder(span):
            turn = perm_ref[span, :]
            out_ref[:, span] = nt(high_ref[...], turn) + nt(rest_ref[...], turn)

        columns_of(width, reorder)

    return call(
        kernel,
        shaped((tokens, width), F32),
        (*g_parts, start, perm, weights),
        scratch=[
            pltpu.VMEM((2, tokens, 3 * cols), BF16),
            pltpu.VMEM((tokens, width), BF16),
            pltpu.VMEM((tokens, width), BF16),
        ],
        flops=16 * tokens * width * cols,
    )


class Exchange:
    def __init__(self, size):
        self.size = size
        self.depth = size.bit_length() - 1
        self.rank = lax.axis_index("dp")
        self.core = lax.axis_index("tensor")
        outer = list(range(self.depth - 1, 1, -1))
        self.bits = (outer + [1, 0], outer + [0, 1])

    def flip(self, value, *steps):
        pairs = []
        for i in range(self.size):
            for core in range(2):
                to = i
                for step in steps:
                    to ^= 1 << self.bits[core][step]
                pairs.append((i * 2 + core, to * 2 + core))
        return lax.ppermute(value, ("dp", "tensor"), pairs)

    def last_outer(self):
        low, high = self.depth - 4, self.depth - 3
        return (low,), (high,), (low, high)

    def flip_three(self, values):
        return [self.flip(value, *steps) for value, steps in zip(values, self.last_outer())]

    def blocks(self):
        tables = []
        for bits in self.bits:
            tables.append(
                [
                    sum(((j >> step) & 1) << bit for step, bit in enumerate(bits))
                    for j in range(self.size)
                ]
            )
        table = np.array(tables, np.int32)
        return jnp.where(self.core == 0, table[0], table[1]) ^ self.rank


def join(*parts):
    return jnp.concatenate(parts, axis=0)


def added(*values):
    total = values[0].astype(F32)
    for value in values[1:]:
        total = total + value.astype(F32)
    return total


def halves(value):
    middle = value.shape[0] // 2
    return value[:middle], value[middle:]


def three_parts(value):
    high = lax.reduce_precision(value, 8, 7)
    rest = value - high
    middle = lax.reduce_precision(rest, 8, 7)
    return (high.astype(BF16), middle.astype(BF16), (rest - middle).astype(BF16))


SMALL = 48
UP = 32


def pack(qkv_w, out_w, emb_w, gains, biases, up_bias):
    rows, cols = out_w.shape
    chunk = gains.shape[1]
    args = (qkv_w, out_w, emb_w, gains, biases, up_bias[None])

    def kernel(*refs):
        one_ref, refs, vec_ref, sems = refs[6], (*refs[:6], *refs[7:13]), refs[13], refs[14]
        copies = []
        for place in range(6):
            copies.append(pltpu.make_async_copy(refs[place], refs[6 + place], sems.at[place]))
        for copy in copies:
            copy.start()
        for copy in copies:
            copy.wait()
        q_ref, o_ref, e_ref, g_ref, b_ref, u_ref = refs[6:]
        for part in range(3):
            one_ref[:, part * cols : (part + 1) * cols] = q_ref[part]
        one_ref[:, 3 * cols : 4 * cols] = o_ref[...]
        vec_ref[...] = jnp.zeros_like(vec_ref)
        vec_ref[0:2, 0:chunk] = g_ref[...]
        vec_ref[2:8, 0:chunk] = b_ref[...]
        vec_ref[0:1, UP : UP + u_ref.shape[1]] = u_ref[...]
        value = vec_ref[...]
        high = value.astype(BF16).astype(F32)
        middle = (value - high).astype(BF16).astype(F32)
        block = [e_ref[...].astype(F32), high, middle, value - high - middle]
        one_ref[:, 4 * cols :] = jnp.concatenate(block, axis=0).astype(BF16)

    return call(
        kernel,
        shaped((rows, 4 * cols + LANES), BF16),
        args,
        in_specs=[pl.BlockSpec(memory_space=pltpu.HBM)] * 6,
        scratch=[pltpu.VMEM(arg.shape, arg.dtype) for arg in args]
        + [pltpu.VMEM((8, LANES), F32), pltpu.SemaphoreType.DMA((6,))],
        grant=60 * 1024 * 1024,
    )


def spreads(sides, width, hidden, chunk, up_chunk):
    lane = jnp.arange(LANES, dtype=jnp.int32)[:, None]
    column = jnp.arange(width, dtype=jnp.int32)[None]
    up_column = jnp.arange(hidden, dtype=jnp.int32)[None]
    thin, broad = [], []
    for side in sides:
        thin.append((lane < chunk) & (column % (2 * chunk) == side * chunk + lane))
        broad.append((lane >= UP) & (up_column % (2 * up_chunk) == side * up_chunk + lane - UP))
    return jnp.stack(thin).astype(BF16), jnp.stack(broad).astype(BF16)


def unpack(core, pieces, thin, broad, rel, absolute, up_rel, cols):
    width, hidden = thin.shape[2], broad.shape[2]
    count = width // SMALL

    def kernel(core_ref, thin_ref, broad_ref, rel_ref, abs_ref, up_ref, *refs):
        vec_ref, head_ref, side_ref, proj_ref, e_ref, sems = refs[8:]
        copies = load_weights(refs[:8], e_ref, sems, 4 * cols, 4 * cols + LANES)
        for copy in copies:
            copy.wait()
        first = core_ref[0] == 0
        blocks = [e_ref[side].astype(F32).reshape(count, SMALL, LANES) for side in range(2)]
        tops = [block[:, : SMALL // 2] for block in blocks]
        halves = [jnp.where(first, tops[0], tops[1]), jnp.where(first, tops[1], tops[0])]
        proj_ref[...] = jnp.concatenate(halves, axis=1).reshape(width, LANES).astype(BF16)
        flat = lax.broadcasted_iota(jnp.int32, (count, count * 8), 1)
        pick = flat == 8 * lax.broadcasted_iota(jnp.int32, (count, count * 8), 0)
        pick = pick.astype(F32).astype(BF16)
        vec = jnp.zeros((8, width), F32)
        plain = jnp.zeros((8, width), F32)
        wide = jnp.zeros((1, hidden), F32)
        index = lax.broadcasted_iota(jnp.int32, (count, hidden), 0)
        for side in range(2):
            placed, up_placed = None, None
            for part in (2, 1, 0):
                start = SMALL // 2 + 8 * part
                rows = blocks[side][:, start : start + 8].reshape(count * 8, LANES).astype(BF16)
                spread = nn(rows, thin_ref[side])
                up_spread = nn(nn(pick, rows).astype(BF16), broad_ref[side])
                placed = spread if placed is None else placed + spread
                up_placed = up_spread if up_placed is None else up_placed + up_spread
            for j in range(count):
                row = placed[8 * j : 8 * j + 8]
                vec = vec + jnp.where(rel_ref[...] == j, row, 0.0)
                plain = plain + jnp.where(abs_ref[...] == j, row, 0.0)
            chosen = jnp.where(up_ref[...] == index, up_placed, 0.0)
            wide = wide + jnp.sum(chosen, axis=0, keepdims=True)
        vec_ref[...] = vec
        for side in range(2):
            low_half = first if side == 0 else jnp.logical_not(first)
            part = jnp.where(low_half, plain[:, :cols], plain[:, cols:])
            head_ref[side : side + 1, :cols] = part[2:3]
            head_ref[side : side + 1, cols : 2 * cols] = jnp.zeros((1, cols), F32)
            head_ref[side : side + 1, 2 * cols :] = part[3:4]
            middle = hidden // 2
            side_ref[side : side + 1, :] = jnp.where(low_half, wide[:, :middle], wide[:, middle:])

    outs = (
        shaped((8, width), F32),
        shaped((2, 3 * cols), F32),
        shaped((2, hidden // 2), F32),
        shaped((width, LANES), BF16),
    )
    return call(
        kernel,
        outs,
        (core[None], thin, broad, rel, absolute, up_rel, *pieces),
        in_specs=[pl.BlockSpec(memory_space=pltpu.SMEM)] + [WHOLE] * 5 + [ANY] * 8,
        scratch=[pltpu.VMEM((2, width, LANES), BF16), pltpu.SemaphoreType.DMA((2, 4))],
    )


def pack_grads(
    core, thin, broad, rel, absolute, up_rel, sums, up_sums, head_sums, proj_grad,
):
    width, hidden = thin.shape[2], broad.shape[2]
    count = width // SMALL

    def kernel(
        core_ref, thin_ref, broad_ref, rel_ref, abs_ref, up_ref, sums_ref, ups_ref, heads_ref,
        pg_ref, own_ref, other_ref,
    ):
        first = core_ref[0] == 0
        fold = lambda v: jnp.sum(v, axis=0, keepdims=True)

        def ordered(own, other):
            low, high = jnp.where(first, own, other), jnp.where(first, other, own)
            return jnp.concatenate([low, high], axis=1)

        def heads(half, kind):
            return fold(heads_ref[half, kind])

        rows = [
            fold(sums_ref[0:8]),
            fold(sums_ref[24:32]),
            ordered(heads(0, 0), heads(1, 0)),
            ordered(heads(0, 1), heads(1, 1)),
            fold(sums_ref[16:24]),
            fold(sums_ref[8:16]),
            fold(sums_ref[40:48]),
            fold(sums_ref[32:40]),
        ]
        grads = jnp.concatenate(rows, axis=0)
        row = lax.broadcasted_iota(jnp.int32, (8, width), 0)
        block = jnp.where((row == 2) | (row == 3), abs_ref[...], rel_ref[...])
        spread = [jnp.where(block == j, grads, 0.0) for j in range(count)]
        spread = jnp.concatenate(spread, axis=0)
        high = spread.astype(BF16)
        rest = (spread - high.astype(F32)).astype(BF16)
        up = ordered(fold(ups_ref[0:8]), fold(ups_ref[8:16]))
        index = lax.broadcasted_iota(jnp.int32, (count, hidden), 0)
        up = jnp.where(up_ref[...] == index, up, 0.0)
        up_high = up.astype(BF16)
        up_rest = (up - up_high.astype(F32)).astype(BF16)
        flat = lax.broadcasted_iota(jnp.int32, (count * 8, count), 0)
        put = flat == 8 * lax.broadcasted_iota(jnp.int32, (count * 8, count), 1)
        put = put.astype(F32).astype(BF16)
        tops = pg_ref[...].reshape(count, SMALL, LANES)
        for side, out_ref in enumerate((own_ref, other_ref)):
            low_half = first if side == 0 else jnp.logical_not(first)
            top = jnp.where(low_half, tops[:, : SMALL // 2], tops[:, SMALL // 2 :])
            thin_part = nt(high, thin_ref[side]) + nt(rest, thin_ref[side])
            up_part = nt(up_high, broad_ref[side]) + nt(up_rest, broad_ref[side])
            vec = (thin_part + nn(put, up_part.astype(BF16))).reshape(count, 8, LANES)
            blank = jnp.zeros((count, SMALL // 2 - 8, LANES), F32)
            made = jnp.concatenate([top, vec, blank], axis=1).reshape(width, LANES).astype(BF16)
            quarter = width // 4
            for place in range(4):
                source = OTHER[place] if side == 1 else place
                out_ref[place * quarter : (place + 1) * quarter, :] = made[
                    source * quarter : (source + 1) * quarter
                ]

    out = shaped((width, LANES), BF16)
    return call(
        kernel,
        (out, out),
        (
            core[None], thin, broad, rel, absolute, up_rel, sums, up_sums, head_sums, proj_grad,
        ),
        in_specs=[pl.BlockSpec(memory_space=pltpu.SMEM)] + [WHOLE] * 9,
    )


def finish(kept, came, a_wide, cols, chunk, up_chunk, emb_shape):
    rows = kept.shape[0]
    b_wide = cols - a_wide
    beside = 3 * a_wide
    second = beside + cols

    def kernel(kept_ref, *refs):
        qkv_ref, out_ref, emb_ref, gain_ref, bias_ref, up_ref, sum_ref = refs[len(came) :]
        total = kept_ref[...]
        for ref in refs[: len(came)]:
            total = total + ref[...].astype(F32)
        sum_ref[...] = total
        for part in range(3):
            qkv_ref[part, :, :a_wide] = sum_ref[:, part * a_wide : (part + 1) * a_wide]
            start = second + part * b_wide
            qkv_ref[part, :, a_wide:] = sum_ref[:, start : start + b_wide]
        out_ref[...] = sum_ref[:, beside:second]
        first = second + 3 * b_wide
        half = SMALL // 2
        emb_ref[...] = sum_ref[0:half, first:]
        gain_ref[...] = sum_ref[half : half + 2, first : first + chunk]
        bias_ref[...] = sum_ref[half + 2 : half + 8, first : first + chunk]
        up_ref[...] = sum_ref[half : half + 1, first + UP : first + UP + up_chunk]

    outs = (
        shaped((3, rows, cols), F32),
        shaped((rows, cols), F32),
        shaped(emb_shape, F32),
        shaped((2, chunk), F32),
        shaped((6, chunk), F32),
        shaped((1, up_chunk), F32),
    )
    return call(kernel, outs, (kept, *came), scratch=[pltpu.VMEM(kept.shape, F32)])


def pack_plain(qkv_w, out_w, emb_w, gains, biases, up_bias):
    rows = out_w.shape[0]
    vector = jnp.concatenate([gains.reshape(-1), biases.reshape(-1), up_bias])
    pad_to = -(-vector.size // LANES) * LANES
    padded = jnp.pad(vector, (0, pad_to - vector.size))
    flat = jnp.concatenate([emb_w.reshape(-1), *three_parts(padded)])
    extra = -(-flat.size // (rows * LANES)) * LANES
    flat = jnp.pad(flat, (0, rows * extra - flat.size)).reshape(rows, extra)
    one = jnp.concatenate([qkv_w[0], qkv_w[1], qkv_w[2], out_w, flat], axis=1)
    sizes = (rows, extra, emb_w.size, gains.shape[1], up_bias.size, pad_to)
    return one, sizes


def unpack_plain(core, sides, pieces, blocks, sizes):
    rows, extra, emb_size, chunk, up_chunk, pad_to = sizes
    size = blocks.shape[0]
    width = size * rows
    cols = width // 2
    ff_local = size * up_chunk
    pieces = [part[:, 4 * cols :] for part in pieces]
    own = jnp.concatenate(pieces[:4])
    other = jnp.concatenate([pieces[4 + place] for place in OTHER])
    small = [part.reshape(size, rows * extra) for part in (own, other)]
    small = jnp.where(core == 0, jnp.stack(small, 1), jnp.stack(small[::-1], 1))
    proj = small[:, :, :emb_size].reshape(width, -1)
    thirds = small[:, :, emb_size : emb_size + 3 * pad_to].astype(F32)
    thirds = thirds.reshape(size, 2, 3, pad_to)
    vectors = thirds[:, :, 0] + (thirds[:, :, 1] + thirds[:, :, 2])
    plain = vectors[jnp.argsort(blocks)].reshape(size * 2, pad_to)
    vectors = vectors.reshape(size * 2, pad_to)
    vec = jnp.moveaxis(vectors[:, : 8 * chunk].reshape(-1, 8, chunk), 1, 0).reshape(8, width)
    query_bias = plain[:, 2 * chunk : 3 * chunk].reshape(-1)
    value_bias = plain[:, 3 * chunk : 4 * chunk].reshape(-1)
    up_bias = plain[:, 8 * chunk : 8 * chunk + up_chunk].reshape(-1)
    head_bias, side_bias = [], []
    for side in sides:
        query_part = lax.dynamic_slice_in_dim(query_bias, side * cols, cols)
        value_part = lax.dynamic_slice_in_dim(value_bias, side * cols, cols)
        head_bias.append(jnp.concatenate([query_part, jnp.zeros_like(query_part), value_part]))
        side_bias.append(lax.dynamic_slice_in_dim(up_bias, side * ff_local, ff_local))
    return vec, jnp.stack(head_bias), jnp.stack(side_bias), proj


def pack_grads_plain(
    core, blocks, sizes, sums, up_sums, head_sums, proj_grad
):
    rows, extra, emb_size, chunk, up_chunk, pad_to = sizes
    size = blocks.shape[0]

    def fold(value):
        return jnp.sum(value.reshape(-1, 8, value.shape[-1]), axis=1)

    def absolute(own, other):
        return jnp.where(
            core == 0, jnp.concatenate([own, other]), jnp.concatenate([other, own])
        )

    def relative(value):
        return value.reshape(size, 2, -1)[blocks]

    gain_one, shift_one, out_bias, gain_two, shift_two, ffn_bias = (
        row.reshape(size, 2, chunk) for row in fold(sums)
    )
    own, other = jnp.sum(head_sums, axis=2)
    small = jnp.concatenate(
        [
            proj_grad.reshape(size, 2, emb_size),
            gain_one,
            gain_two,
            relative(absolute(own[0], other[0])),
            relative(absolute(own[1], other[1])),
            out_bias,
            shift_one,
            ffn_bias,
            shift_two,
            relative(absolute(*fold(up_sums))),
        ],
        axis=2,
    ).astype(BF16)
    small = jnp.pad(small, ((0, 0), (0, 0), (0, rows * extra - small.shape[2])))
    small = jnp.where(core == 0, small, small[:, ::-1])
    own, other = jnp.moveaxis(small, 1, 0).reshape(2, size * rows, extra)
    first, second, third, fourth = jnp.split(other, 4)
    return own, jnp.concatenate([first, third, second, fourth])


def body(
    tokens,
    lengths,
    key_mask,
    order,
    query_key_value_weight,
    output_projection_weight,
    up_projection_weight,
    down_projection_weight,
    embedding_projection_weight,
    gains,
    biases,
    up_bias_vector,
    cotangent,
):
    size = lax.axis_size("dp")
    core = lax.axis_index("tensor")
    ways = Exchange(size)
    depth = ways.depth
    half_len = tokens.shape[1]
    full_len = key_mask.shape[1]
    width = tokens.shape[2]
    cols = output_projection_weight.shape[0]
    rows = output_projection_weight.shape[1]
    ff_local = up_projection_weight.shape[1]
    chunk = gains.shape[1]
    emb_size = embedding_projection_weight.size
    sides = (core, 1 - core)

    fast = rows == SMALL and emb_size == SMALL // 2 * LANES and up_bias_vector.size <= LANES - UP
    small_args = (
        query_key_value_weight,
        output_projection_weight.T,
        embedding_projection_weight,
        gains,
        biases,
        up_bias_vector,
    )
    if fast:
        one = pack(*small_args)
    else:
        one, small_sizes = pack_plain(*small_args)

    wide = 4 * cols
    seconds, lasts = depth - 2, depth - 1
    for step in range(depth - 4):
        one = join(one, ways.flip(one, step))
    tokens, order, lengths, key_mask = after((tokens, order, lengths, key_mask), one)
    mine = order[0, core]
    theirs = order[0, 1 - core]
    my_half = lax.dynamic_index_in_dim(tokens, mine, 0, keepdims=False)
    their_half = lax.dynamic_index_in_dim(tokens, theirs, 0, keepdims=False)
    blocks = ways.blocks()
    one_came = ways.flip_three([one] * 3)
    if fast:
        thin, broad = spreads(sides, width, 2 * ff_local, chunk, up_bias_vector.size)
        places_of = jnp.argsort(blocks)
        rel = (jnp.arange(width, dtype=jnp.int32) // rows)[None]
        absolute = jnp.repeat(places_of, rows)[None].astype(jnp.int32)
        up_rel = jnp.repeat(places_of, 2 * up_bias_vector.size)[None].astype(jnp.int32)
        *one_came, thin, broad, rel, absolute, up_rel = together(
            *one_came, thin, broad, rel, absolute, up_rel
        )
        tables = (core, thin, broad, rel, absolute, up_rel)

    def in_order(own, other):
        return jnp.where(
            core == 0, jnp.concatenate([own, other]), jnp.concatenate([other, own])
        )

    def half_of(value, which):
        return lax.dynamic_slice_in_dim(value, which * half_len, half_len)

    seq_len = lengths[mine]
    marks = lax.dynamic_index_in_dim(key_mask, mine, 0, keepdims=False)
    places = jnp.arange(full_len, dtype=jnp.int32)
    key_ok = (places < seq_len) & ((marks == 1) | (places == 0))
    mask = jnp.where(key_ok, 0.0, -1e30).astype(F32)[None, :]
    where = (blocks[:, None] * rows + jnp.arange(rows, dtype=jnp.int32)[None]).reshape(-1)
    perm = (jnp.arange(width, dtype=jnp.int32)[:, None] == where[None]).astype(BF16)
    two, three = after((up_projection_weight, down_projection_weight.T), order)
    for step in range(depth - 4):
        two = join(two, ways.flip(two, step))
        three = join(three, ways.flip(three, step))
    one = join(one, *one_came)
    here = in_order(my_half, swap_cores(after(their_half, one)))
    two_came = ways.flip_three([after(two, one)] * 3)
    one_b, one_c, here, mask, perm, *two_came = together(
        ways.flip(one, seconds), ways.flip(one, lasts), here, mask, perm, *two_came
    )
    two = join(two, *two_came)
    one_other = together(swap_cores(one), swap_cores(one_b), swap_cores(one_c))
    three_came = ways.flip_three([after(three, two, *one_other)] * 3)
    one_d, two_b, *three_came = together(
        ways.flip(one_b, lasts), ways.flip(two, seconds), *three_came
    )
    three = join(three, *three_came)
    two_both = join(two, two_b)
    one_pieces = (one, one_b, one_c, one_d, *one_other, swap_cores(one_d))
    two_more, three_b = ways.flip(two_both, lasts), ways.flip(three, seconds)
    one_pieces = together(*one_pieces, two_both, three)[:8]
    if fast:
        vec, head_bias, side_bias, proj = unpack(core, one_pieces, *tables[1:], cols)
    else:
        vec, head_bias, side_bias, proj = unpack_plain(
            core, sides, one_pieces, blocks, small_sizes
        )
    side_bias = (side_bias[0:1], side_bias[1:2])

    qkv, lse, att, res_one, first, first_low, first_low_t, here_t, weights = attention_forward(
        here, perm, head_bias, mask, vec, one_pieces, cols
    )
    two_more, three_b = after((two_more, three_b), first_low)
    three_both = join(three, three_b)
    three_more = ways.flip(three_both, lasts)
    two_other = [swap_cores(part) for part in (two_both, two_more)]

    def quarters(both, more):
        return ((both, 0), (both, 1), (more, 0), (more, 1))

    two_own = (two_both, two_more)
    hid_own, slope_own = up_forward(
        after(first_low, three_both, two_more), quarters(*two_own), side_bias[0], False
    )
    two_other = after(two_other, hid_own)
    three_both_other = swap_cores(three_both)
    cot_mine = lax.dynamic_index_in_dim(cotangent, core, 0, keepdims=False)
    cot_other = lax.dynamic_index_in_dim(cotangent, 1 - core, 0, keepdims=False)
    cot = in_order(cot_mine, after(swap_cores(after(cot_other, first_low)), hid_own))
    hid_other, slope_other = up_forward(after(first_low, cot), quarters(*two_other), side_bias[1], True)
    three_more, three_both_other = after((three_more, three_both_other), hid_other)
    three_more_other = swap_cores(three_more)
    three_own = (three_both, three_more)
    three_other = (three_both_other, three_more_other)
    emb, g_ffn, g_ffn_t, g_res_two, proj_grad, sums_two = down_both(
        seq_len[None],
        (hid_own, hid_other),
        (three_both, three_more, three_both_other, three_more_other),
        first,
        vec,
        proj,
        cot,
    )

    def low(*values):
        return added(*values).astype(BF16)

    def spread(value):
        kept, sent = halves(value)
        return kept, sent.astype(BF16)

    def quarter_out(value):
        kept, *sent = jnp.split(value, 4)
        return kept, [part.astype(BF16) for part in sent]

    dk_other, ds_other = down_grad(g_ffn_t, hid_other, True)
    ds_came, dk_came = swap_cores(ds_other), swap_cores(dk_other)
    dk, ds = down_grad(g_ffn_t, after(hid_own, ds_other), False)
    ds_came = after(ds_came, ds)
    d_high = low(halves(ds)[1], halves(ds_came)[1])
    d_low = low(halves(ds)[0], halves(ds_came)[0])
    d_came_high = ways.flip(d_high, lasts)
    uk_other, us_other, up_bias_other, part = up_grad(
        after(g_ffn, d_high, d_low),
        first_low_t,
        slope_other,
        three_other,
        two_other,
        g_res_two,
        True,
        (),
    )
    us_came, uk_came = swap_cores(us_other), swap_cores(uk_other)
    d_came_high, dk_came, d_low = after((d_came_high, dk_came, d_low), us_other)
    d_came_low = ways.flip(d_low, lasts)
    uk, us, up_bias, g_first = up_grad(
        after(g_ffn, us_other, d_came_high),
        first_low_t,
        slope_own,
        three_own,
        two_own,
        part,
        False,
        (up_bias_other,),
    )
    d_came_low, us_came, uk_came = after((d_came_low, us_came, uk_came), us)
    u_sent = low(us, us_came)
    u_came = ways.flip(u_sent, lasts)
    d_sent = low(halves(dk)[1], halves(dk_came)[1], d_came_high)
    d_held = added(halves(dk)[0], halves(dk_came)[0], d_came_low)
    d_came = ways.flip(d_sent, seconds)
    g_res_one, g_branch_t, g_att, sums = norm_back(
        after(g_first, u_sent, d_sent), res_one, vec, weights, sums_two, cols
    )
    pairs = list(range(cols // LANES))
    split = (len(pairs) + 1) // 2
    g_a, bias_a = attention_back(pairs[:split], g_att, att, qkv, lse, mask)
    beside = (g_branch_t, att)
    ak_other, as_other = project_other(here_t, g_a, beside)
    as_came, ak_came = swap_cores(as_other), swap_cores(ak_other)
    g_b, head_sums = attention_back(
        pairs[split:], after(g_att, as_other), att, qkv, lse, mask, (bias_a,)
    )
    as_came, ak_came = after((as_came, ak_came), g_b)
    a_keep, a_send = project_own(here_t, g_a, beside, (), ak_came, as_came)
    u_came = after(u_came, a_send)
    a_came = ways.flip(a_send, lasts)
    u_sent = low(halves(uk)[1], halves(uk_came)[1], halves(u_came)[1])
    u_held = added(halves(uk)[0], halves(uk_came)[0], halves(u_came)[0])
    u_came = ways.flip(u_sent, seconds)
    bk_other, bs_other = project_other(here_t, after(g_b, a_send, u_sent), ())
    bs_came, bk_came = swap_cores(bs_other), swap_cores(bk_other)
    d_came = after(d_came, bs_other)
    d_held, d_sent = quarter_out(d_held + d_came.astype(F32))
    d_came = ways.flip_three(d_sent)
    if fast:
        small_own, small_other = pack_grads(
            *tables, after(sums, bs_other, *d_sent), up_bias, head_sums, proj_grad
        )
    else:
        small_own, small_other = pack_grads_plain(
            core, blocks, small_sizes, sums, up_bias, head_sums, proj_grad
        )
    small_came = swap_cores(small_other)
    bs_came, bk_came = after((bs_came, bk_came), small_other)
    b_keep, b_send = project_own(here_t, g_b, (), (small_own, small_came), bk_came, bs_came)
    u_came, a_came = after((u_came, a_came), b_send)
    b_came = ways.flip(b_send, lasts)
    a_sent = low(halves(a_keep)[1], halves(a_came)[1])
    a_held = added(halves(a_keep)[0], halves(a_came)[0])
    a_came = ways.flip(a_sent, seconds)
    u_held, u_sent = quarter_out(after(u_held, a_sent) + u_came.astype(F32))
    u_came = ways.flip_three(u_sent)
    b_came = after(b_came, *u_sent)
    b_sent = low(halves(b_keep)[1], halves(b_came)[1])
    b_held = added(halves(b_keep)[0], halves(b_came)[0])
    b_came = ways.flip(b_sent, seconds)
    g_here = token_back(
        (after(g_a, b_send, a_sent, b_sent, *u_sent, *d_came), g_b), g_res_one, perm, weights, cols
    )
    a_came, b_came, u_came, emb = after((a_came, b_came, u_came, emb), g_here)
    held = jnp.concatenate([a_held + a_came.astype(F32), b_held + b_came.astype(F32)], axis=1)
    held, sent = quarter_out(held)
    came = ways.flip_three(sent)
    d_came, u_came, u_held = after((d_came, u_came, u_held), *sent)
    d_held, u_held = added(d_held, *d_came), added(u_held, *u_came)
    for step in range(depth - 5, -1, -1):
        held, sent = spread(added(held, *came))
        came = [ways.flip(sent, step)]
        d_held, sent = spread(d_held)
        d_held = d_held + ways.flip(sent, step).astype(F32)
        u_held, sent = spread(u_held)
        u_held = u_held + ways.flip(sent, step).astype(F32)
    down_shard, up_shard = d_held, u_held
    a_wide, b_wide = split * LANES, (len(pairs) - split) * LANES
    if fast:
        qkv_shard, out_shard, emb_shard, gain_shard, bias_shard, up_bias_shard = finish(
            held, came, a_wide, cols, chunk, up_bias_vector.size, embedding_projection_weight.shape
        )
        out_shard, up_bias_shard = out_shard.T, up_bias_shard[0]
    else:
        shard = added(held, *came)
        a_shard, b_shard = shard[:, : 3 * a_wide + cols], shard[:, 3 * a_wide + cols :]
        qkv_shard = jnp.stack(
            [
                jnp.concatenate(
                    [
                        a_shard[:, i * a_wide : (i + 1) * a_wide],
                        b_shard[:, i * b_wide : (i + 1) * b_wide],
                    ],
                    axis=1,
                )
                for i in range(3)
            ]
        )
        out_shard = a_shard[:, 3 * a_wide :].T
        tail = b_shard[:, 3 * b_wide :].reshape(-1)
        emb_shard = tail[:emb_size].reshape(embedding_projection_weight.shape)
        tail = tail[emb_size:]
        gain_shard = tail[: 2 * chunk].reshape(2, chunk)
        bias_shard = tail[2 * chunk : 8 * chunk].reshape(6, chunk)
        up_bias_shard = tail[8 * chunk : 8 * chunk + up_bias_vector.size]

    def give_back(value, places_of):
        own = half_of(value, core)
        other = swap_cores(half_of(value, 1 - core))
        blank = jnp.zeros((2,) + own.shape, value.dtype)
        blank = lax.dynamic_update_slice(blank, own[None], (places_of[0], 0, 0))
        return lax.dynamic_update_slice(blank, other[None], (places_of[1], 0, 0))

    embeddings = give_back(emb, (core, 1 - core))
    grad_tokens = give_back(g_here, (mine, theirs))
    return (
        embeddings,
        grad_tokens,
        qkv_shard,
        out_shard,
        up_shard,
        down_shard.T,
        emb_shard,
        gain_shard,
        bias_shard,
        up_bias_shard,
    )


def solution(mesh):
    return jax.shard_map(
        body,
        mesh=mesh,
        in_specs=(
            P("dp", "tensor", None),
            P("dp"),
            P("dp", None),
            P("dp", None),
            P(None, "dp", "tensor"),
            P("tensor", "dp"),
            P("dp", "tensor"),
            P("tensor", "dp"),
            P(("dp", "tensor"), None),
            P(None, ("dp", "tensor")),
            P(None, ("dp", "tensor")),
            P(("dp", "tensor")),
            P("dp", "tensor", None),
        ),
        out_specs=(
            P("dp", "tensor", None),
            P("dp", "tensor", None),
            P(None, "dp", "tensor"),
            P("tensor", "dp"),
            P("dp", "tensor"),
            P("tensor", "dp"),
            P(("dp", "tensor"), None),
            P(None, ("dp", "tensor")),
            P(None, ("dp", "tensor")),
            P(("dp", "tensor")),
        ),
        check_vma=False,
    )
```

```python
import functools

import jax
import jax.numpy as jnp
import numpy as np
from jax import lax
from jax.experimental import pallas as pl
from jax.experimental.pallas import tpu as pltpu
from jax.sharding import PartitionSpec as P

HD = 64
LANES = 128
STRIP = 256
F32 = jnp.float32
BF16 = jnp.bfloat16
VMEM_LIMIT = 15 * 1024 * 1024


def nn(left, right):
    return lax.dot_general(left, right, (((1,), (0,)), ((), ())), preferred_element_type=F32)


def nt(left, right):
    return lax.dot_general(left, right, (((1,), (1,)), ((), ())), preferred_element_type=F32)


def swap_cores(value):
    return lax.ppermute(value, "tensor", [(0, 1), (1, 0)])


def after(value, *others):
    return lax.optimization_barrier((value, others))[0]


def together(*values):
    return lax.optimization_barrier(values)


def strips(count, size, step):
    def run(i, carry):
        step(pl.ds(pl.multiple_of(i * size, size), size))
        return carry

    lax.fori_loop(0, count // size, run, 0)


def columns_of(width, step):
    block = 256 if width % 256 == 0 else width

    def run(i, carry):
        step(pl.ds(pl.multiple_of(i * block, block), block))
        return carry

    lax.fori_loop(0, width // block, run, 0)


def call(
    body, outs, args, grid=None, in_specs=None, out_specs=None, scratch=(), flops=0, grant=VMEM_LIMIT
):
    whole = pl.BlockSpec(memory_space=pltpu.VMEM)
    return pl.pallas_call(
        body,
        out_shape=outs,
        grid=grid or (),
        in_specs=in_specs or [whole] * len(args),
        out_specs=out_specs or jax.tree.map(lambda _: whole, outs),
        scratch_shapes=scratch,
        compiler_params=pltpu.CompilerParams(vmem_limit_bytes=grant),
        cost_estimate=pl.CostEstimate(flops=flops, bytes_accessed=1 << 20, transcendentals=0),
    )(*args)


def shaped(shape, dtype):
    return jax.ShapeDtypeStruct(shape, dtype)


ANY = pl.BlockSpec(memory_space=pl.ANY)
WHOLE = pl.BlockSpec(memory_space=pltpu.VMEM)


OTHER = (0, 2, 1, 3)


def load_weights(pieces, target, sems, first=0, last=None, at=(0,) * 8):
    quarter = target.shape[1] // 4
    columns = slice(first, last)
    copies = []
    for side in range(2):
        for place in range(4):
            source = place if side == 0 else 4 + OTHER[place]
            rows = pl.ds(at[source] * quarter, quarter)
            copies.append(
                pltpu.make_async_copy(
                    pieces[source].at[rows, columns],
                    target.at[side, pl.ds(place * quarter, quarter)],
                    sems.at[side, place],
                )
            )
    for copy in copies:
        copy.start()
    return copies


def attention_kernel(
    x_ref, perm_ref, bias_ref, mask_ref, vec_ref, *refs
):
    pieces, refs = refs[:8], refs[8:]
    qkv_ref, lse_ref, att_ref, res_ref, first_ref, low_ref, lowt_ref, xt_ref, w_ref = refs[:9]
    col_ref, rel_ref, sems = refs[9:]
    cols = qkv_ref.shape[2] // 3
    tokens = x_ref.shape[0]
    copies = load_weights(pieces, w_ref, sems, 0, 4 * cols)

    def reorder(span):
        rel_ref[:, span] = nn(x_ref[...], perm_ref[:, span]).astype(BF16)

    columns_of(x_ref.shape[1], reorder)
    xt_ref[...] = rel_ref[...].T
    col_ref[...] = jnp.broadcast_to(mask_ref[...], (LANES, tokens)).T
    for copy in copies:
        copy.wait()

    def project(i, carry):
        half, part = i // 3, i % 3
        span = pl.ds(pl.multiple_of(part * cols, cols), cols)
        made = nn(rel_ref[...], w_ref[half, :, span]) + bias_ref[pl.ds(half, 1), span]
        qkv_ref[half, :, span] = made.astype(BF16)
        return carry

    lax.fori_loop(0, 6, project, 0)
    lane = lax.broadcasted_iota(jnp.int32, (tokens, LANES), 1) < HD
    pairs = cols // LANES


    def pair(step, carry):
        half, i = step // pairs, step % pairs
        off = pl.multiple_of(i * LANES, LANES)
        query = qkv_ref[half, :, pl.ds(off, LANES)] * BF16(HD ** (-0.5))
        key = qkv_ref[half, :, pl.ds(pl.multiple_of(cols + off, LANES), LANES)]
        value = qkv_ref[half, :, pl.ds(pl.multiple_of(2 * cols + off, LANES), LANES)]
        value_t = value.T
        outs = []
        for head in range(2):
            kept = jnp.where(lane == (head == 0), key, jnp.zeros_like(key))
            scores = nt(kept, query)
            scores = scores + jnp.concatenate([col_ref[...]] * (tokens // LANES), axis=1)
            top = jnp.max(scores, axis=0, keepdims=True)
            shifted = jnp.exp(scores - top)
            total = jnp.sum(shifted, axis=0, keepdims=True)
            out = nn(value_t[head * HD : (head + 1) * HD], shifted.astype(BF16))
            outs.append(out / total)
            lse_ref[half, pl.ds(i * 2 + head, 1), :] = top + jnp.log(total)
        both = jnp.concatenate(outs, axis=0).T
        att_ref[half, :, pl.ds(off, LANES)] = both.astype(BF16)
        return carry

    lax.fori_loop(0, 2 * pairs, pair, 0)
    out = slice(3 * cols, 4 * cols)

    def branch(span):
        made = nt(att_ref[0], w_ref[0, span, out]) + nt(att_ref[1], w_ref[1, span, out])
        res_ref[:, span] = made

    columns_of(x_ref.shape[1], branch)

    def norm(rows):
        value = res_ref[rows, :] + vec_ref[4:5, :] + rel_ref[rows, :].astype(F32)
        res_ref[rows, :] = value
        average = jnp.mean(value, axis=-1, keepdims=True)
        centred = value - average
        inverse = lax.rsqrt(jnp.mean(centred * centred, axis=-1, keepdims=True) + 1e-12)
        first = centred * inverse * vec_ref[0:1, :] + vec_ref[5:6, :]
        first_ref[rows, :] = first
        low_ref[rows, :] = first.astype(BF16)

    strips(tokens, STRIP, norm)
    lowt_ref[...] = low_ref[...].T


def attention_forward(x, perm, head_bias, mask, vec, pieces, cols):
    tokens, width = x.shape
    heads = cols // HD
    outs = (
        shaped((2, tokens, 3 * cols), BF16),
        shaped((2, heads, tokens), F32),
        shaped((2, tokens, cols), BF16),
        shaped((tokens, width), F32),
        shaped((tokens, width), F32),
        shaped((tokens, width), BF16),
        shaped((width, tokens), BF16),
        shaped((width, tokens), BF16),
        shaped((2, width, 4 * cols), BF16),
    )
    return call(
        attention_kernel,
        outs,
        (x, perm, head_bias, mask, vec, *pieces),
        in_specs=[WHOLE] * 5 + [ANY] * 8,
        scratch=[
            pltpu.VMEM((tokens, LANES), F32),
            pltpu.VMEM((tokens, width), BF16),
            pltpu.SemaphoreType.DMA((2, 4)),
        ],
        flops=8 * tokens * width * width,
    )


ERF = (0.254829592, -0.284496736, 1.421413741, -1.453152027, 1.061405429)


def gelu_pair(value):
    size = jnp.abs(value)
    bell = jnp.exp(-0.5 * value * value)
    t = 1.0 / (1.0 + (0.3275911 * 0.5**0.5) * size)
    poly = ERF[4]
    for term in ERF[3::-1]:
        poly = poly * t + term
    tail = 0.5 * poly * t * bell
    phi = jnp.where(value >= 0, 1.0 - tail, tail)
    return value * phi, phi + value * bell * 0.3989422804014327


def join_rows(refs, target, swapped):
    quarter = target.shape[0] // 4
    for place in range(4):
        source = OTHER[place] if swapped else place
        target[place * quarter : (place + 1) * quarter, :] = refs[source][...]


def split_rows(value, keep_ref, send_ref, swapped):
    quarter = value.shape[0] // 4
    for place in range(4):
        source = OTHER[place] if swapped else place
        ref = (keep_ref, send_ref)[place // 2]
        rows = slice((place % 2) * quarter, (place % 2 + 1) * quarter)
        ref[rows, :] = value[source * quarter : (source + 1) * quarter, :]


def column_block(hidden):
    return 512 if hidden % 512 == 0 else hidden


def up_forward(low, pieces, bias, swapped):
    tokens, width = low.shape
    pieces, at = zip(*pieces)
    hidden = pieces[0].shape[1]
    block = column_block(hidden)

    def kernel(low_ref, a_ref, b_ref, c_ref, d_ref, bias_ref, hid_ref, slope_ref, acc_ref, w_ref):
        join_rows((a_ref, b_ref, c_ref, d_ref), w_ref, swapped)
        acc_ref[...] = nn(low_ref[...], w_ref[...])

        def act(rows):
            active, slope = gelu_pair(acc_ref[rows, :] + bias_ref[...])
            hid_ref[rows, :] = active.astype(BF16)
            slope_ref[rows, :] = slope.astype(BF16)

        strips(tokens, STRIP, act)

    outs = (shaped((tokens, hidden), BF16), shaped((tokens, hidden), BF16))
    chunk = pl.BlockSpec((tokens, block), lambda i: (0, i))
    parts = [pl.BlockSpec((width // 4, block), lambda i, row=row: (row, i)) for row in at]
    return call(
        kernel,
        outs,
        (low, *pieces, bias),
        grid=(hidden // block,),
        in_specs=[
            pl.BlockSpec((tokens, width), lambda i: (0, 0)),
            *parts,
            pl.BlockSpec((1, block), lambda i: (0, i)),
        ],
        out_specs=(chunk, chunk),
        scratch=[pltpu.VMEM((tokens, block), F32), pltpu.VMEM((width, block), BF16)],
        flops=2 * tokens * width * hidden,
    )


def down_kernel(
    len_ref, h0_ref, h1_ref, first_ref, vec_ref, proj_ref, cot_ref, *refs
):
    both_ref, more_ref, both_other, more_other, *refs = refs
    emb_ref, low_ref, lowt_ref, res_ref, pgrad_ref, sums_ref = refs[:6]
    ffn_ref, norm_ref, sec_ref, gp_ref, gs_ref, inv_ref, prj_ref, w_ref = refs[6:]
    tokens = first_ref.shape[0]
    length = len_ref[0]
    quarter = w_ref.shape[0] // 4
    for place, ref, part in ((0, both_other, 0), (1, more_other, 0), (2, both_other, 1), (3, more_other, 1)):
        w_ref[place * quarter : (place + 1) * quarter] = ref[part * quarter : (part + 1) * quarter]
    for ref, first in ((both_ref, 0), (more_ref, 2 * quarter)):
        span = slice(first, first + 2 * quarter)
        ffn_ref[:, span] = nt(h0_ref[...], ref[...]) + nt(h1_ref[...], w_ref[span])

    def norm(rows):
        value = first_ref[rows, :] + ffn_ref[rows, :] + vec_ref[6:7, :]
        average = jnp.mean(value, axis=-1, keepdims=True)
        centred = value - average
        inverse = lax.rsqrt(jnp.mean(centred * centred, axis=-1, keepdims=True) + 1e-12)
        normed = centred * inverse
        norm_ref[rows, :] = normed
        inv_ref[rows, :] = jnp.broadcast_to(inverse, (STRIP, LANES))
        sec_ref[rows, :] = (normed * vec_ref[1:2, :] + vec_ref[7:8, :]).astype(BF16)

    strips(tokens, STRIP, norm)
    prj_ref[...] = nn(sec_ref[...], proj_ref[...])

    def embed(rows):
        projected = prj_ref[rows, :]
        valid = rows.start + lax.broadcasted_iota(jnp.int32, projected.shape, 0) < length
        valid = valid.astype(F32)
        scale = lax.rsqrt(jnp.sum(projected * projected, axis=-1, keepdims=True) + 1e-06)
        unit = projected * scale
        emb_ref[rows, :] = unit * valid
        cot = cot_ref[rows, :] * valid
        back = scale * (cot - unit * jnp.sum(unit * cot, axis=-1, keepdims=True))
        gp_ref[rows, :] = back.astype(BF16)

    strips(tokens, STRIP, embed)
    pgrad_ref[...] = nn(sec_ref[...].T, gp_ref[...])
    gs_ref[...] = nt(gp_ref[...], proj_ref[...])
    sums_ref[...] = jnp.zeros_like(sums_ref)

    def back(rows):
        grad = gs_ref[rows, :]
        normed = norm_ref[rows, :]
        scaled = grad * vec_ref[1:2, :]
        inside = (
            scaled
            - jnp.mean(scaled, axis=-1, keepdims=True)
            - normed * jnp.mean(scaled * normed, axis=-1, keepdims=True)
        )
        value = inside * inv_ref[rows, 0:1]
        low = value.astype(BF16)
        res_ref[rows, :] = value
        low_ref[rows, :] = low
        fold = lambda v: jnp.sum(v.reshape(STRIP // 8, 8, v.shape[1]), axis=0)
        sums_ref[0:8, :] += fold(grad * normed)
        sums_ref[8:16, :] += fold(grad)
        sums_ref[16:24, :] += fold(low.astype(F32))

    strips(tokens, STRIP, back)
    lowt_ref[...] = low_ref[...].T


def down_both(length, hidden, pieces, first, vec, proj, cot):
    tokens, width = first.shape
    embed = proj.shape[1]
    outs = (
        shaped((tokens, embed), F32),
        shaped((tokens, width), BF16),
        shaped((width, tokens), BF16),
        shaped((tokens, width), F32),
        shaped((width, embed), F32),
        shaped((24, width), F32),
    )
    args = (length, *hidden, first, vec, proj, cot, *pieces)
    return call(
        down_kernel,
        outs,
        args,
        in_specs=[pl.BlockSpec(memory_space=pltpu.SMEM)] + [WHOLE] * 10,
        scratch=[
            pltpu.VMEM((tokens, width), F32),
            pltpu.VMEM((tokens, width), F32),
            pltpu.VMEM((tokens, width), BF16),
            pltpu.VMEM((tokens, embed), BF16),
            pltpu.VMEM((tokens, width), F32),
            pltpu.VMEM((tokens, LANES), F32),
            pltpu.VMEM((tokens, embed), F32),
            pltpu.VMEM((width, hidden[0].shape[1]), BF16),
        ],
        flops=2 * tokens * width * hidden[0].shape[1] * 2,
    )


def down_grad(g_low_t, hid, swapped):
    width, tokens = g_low_t.shape
    hidden = hid.shape[1]
    block = column_block(hidden)

    def kernel(gt_ref, hid_ref, keep_ref, send_ref):
        split_rows(nn(gt_ref[...], hid_ref[...]).astype(BF16), keep_ref, send_ref, swapped)

    piece = pl.BlockSpec((width // 2, block), lambda i: (0, i))
    out = shaped((width // 2, hidden), BF16)
    return call(
        kernel,
        (out, out),
        (g_low_t, hid),
        grid=(hidden // block,),
        in_specs=[
            pl.BlockSpec((width, tokens), lambda i: (0, 0)),
            pl.BlockSpec((tokens, block), lambda i: (0, i)),
        ],
        out_specs=(piece, piece),
        flops=2 * tokens * width * hidden,
    )


def up_grad(g_low, low_t, slope, down, up, start, swapped, biases):
    tokens, width = g_low.shape
    hidden = slope.shape[1]
    block = column_block(hidden)
    quarter = width // 4
    count = 8 * (1 + len(biases))

    def kernel(g_ref, lowt_ref, slope_ref, start_ref, db_ref, dm_ref, ub_ref, um_ref, *refs):
        more, refs = refs[: len(biases)], refs[len(biases) :]
        keep_ref, send_ref, bias_ref, first_ref, gh_ref, gin_ref, wd_ref, wu_ref = refs
        first_ref[...] = start_ref[...]
        bias_ref[...] = jnp.zeros_like(bias_ref)
        for ref in more:
            bias_ref[8:16, :] = ref[...]

        def chunk(i, carry):
            here = pl.ds(pl.multiple_of(i * block, block), block)
            for target, both_ref, more_ref in ((wd_ref, db_ref, dm_ref), (wu_ref, ub_ref, um_ref)):
                for place in range(4):
                    source = OTHER[place] if swapped else place
                    ref = (both_ref, more_ref)[source // 2]
                    rows = slice((source % 2) * quarter, (source % 2 + 1) * quarter)
                    target[place * quarter : (place + 1) * quarter, :] = ref[rows, here]

            def matmul(span):
                gh_ref[:, span] = nn(g_ref[...], wd_ref[:, span])

            columns_of(block, matmul)

            def act(rows):
                grad = (gh_ref[rows, :] * slope_ref[rows, here].astype(F32)).astype(BF16)
                gin_ref[rows, :] = grad
                wide = grad.astype(F32)
                total = jnp.sum(wide.reshape(STRIP // 8, 8, wide.shape[1]), axis=0)
                bias_ref[0:8, here] += total

            strips(tokens, STRIP, act)
            made = nn(lowt_ref[...], gin_ref[...]).astype(BF16)
            split_rows(made, keep_ref.at[:, here], send_ref.at[:, here], swapped)

            def add(span):
                first_ref[:, span] += nt(gin_ref[...], wu_ref[span, :])

            columns_of(width, add)
            return carry

        lax.fori_loop(0, hidden // block, chunk, 0)

    out = shaped((width // 2, hidden), BF16)
    return call(
        kernel,
        (out, out, shaped((count, hidden), F32), shaped((tokens, width), F32)),
        (g_low, low_t, slope, start, *down, *up, *biases),
        scratch=[
            pltpu.VMEM((tokens, block), F32),
            pltpu.VMEM((tokens, block), BF16),
            pltpu.VMEM((width, block), BF16),
            pltpu.VMEM((width, block), BF16),
        ],
        flops=6 * tokens * width * hidden,
    )


def norm_back(g_first, res, vec, weights, sums_two, cols):
    tokens, width = g_first.shape

    def kernel(
        gf_ref, res_ref, vec_ref, w_ref, two_ref, gres_ref, turn_ref, gatt_ref, sums_ref, low_ref
    ):
        sums_ref[0:24, :] = jnp.zeros((24, width), F32)
        sums_ref[24:48, :] = two_ref[...]

        def back(rows):
            value = res_ref[rows, :]
            average = jnp.mean(value, axis=-1, keepdims=True)
            centred = value - average
            inverse = lax.rsqrt(jnp.mean(centred * centred, axis=-1, keepdims=True) + 1e-12)
            normed = centred * inverse
            grad = gf_ref[rows, :]
            scaled = grad * vec_ref[0:1, :]
            inside = (
                scaled
                - jnp.mean(scaled, axis=-1, keepdims=True)
                - normed * jnp.mean(scaled * normed, axis=-1, keepdims=True)
            )
            out = inside * inverse
            low = out.astype(BF16)
            gres_ref[rows, :] = out
            low_ref[rows, :] = low
            fold = lambda v: jnp.sum(v.reshape(STRIP // 8, 8, v.shape[1]), axis=0)
            sums_ref[0:8, :] += fold(grad * normed)
            sums_ref[8:16, :] += fold(grad)
            sums_ref[16:24, :] += fold(low.astype(F32))

        strips(tokens, STRIP, back)
        turn_ref[...] = low_ref[...].T
        for half in range(2):
            gatt_ref[half] = nn(low_ref[...], w_ref[half, :, 3 * cols :]).astype(BF16)

    outs = (
        shaped((tokens, width), F32),
        shaped((width, tokens), BF16),
        shaped((2, tokens, cols), BF16),
        shaped((48, width), F32),
    )
    return call(
        kernel,
        outs,
        (g_first, res, vec, weights, sums_two),
        scratch=[pltpu.VMEM((tokens, width), BF16)],
        flops=4 * tokens * width * cols,
    )


def attention_back(pairs, g_att, att, qkv, lse, mask, earlier=()):
    tokens, cols = att.shape[1:]
    wide = len(pairs) * LANES
    scale = HD ** (-0.5)

    before = sum(part.shape[3] for part in earlier)

    def kernel(gatt_ref, att_ref, qkv_ref, lse_ref, mask_ref, *refs):
        gqkv_ref, sums_ref, col_ref = refs[len(earlier) :]
        for ref in refs[: len(earlier)]:
            sums_ref[:, :, :, 0:before] = ref[...]
        col_ref[...] = jnp.broadcast_to(mask_ref[...], (LANES, tokens)).T
        lane = lax.broadcasted_iota(jnp.int32, (tokens, LANES), 1) < HD

        def pair(step, carry):
            half, place = step // len(pairs), step % len(pairs)
            i = pairs[0] + place
            off = pl.multiple_of(i * LANES, LANES)
            off_k = pl.multiple_of(cols + off, LANES)
            off_v = pl.multiple_of(2 * cols + off, LANES)
            query = qkv_ref[half, :, pl.ds(off, LANES)] * BF16(scale)
            key = qkv_ref[half, :, pl.ds(off_k, LANES)]
            value = qkv_ref[half, :, pl.ds(off_v, LANES)]
            grad = gatt_ref[half, :, pl.ds(off, LANES)]
            out = att_ref[half, :, pl.ds(off, LANES)]
            key_t = (key * BF16(scale)).T
            delta = (grad.astype(F32) * out.astype(F32)).T
            g_query, g_key, g_value = [], [], []
            for head in range(2):
                pick = lane == (head == 0)
                span = slice(head * HD, (head + 1) * HD)
                zero = jnp.zeros_like(key)
                scores = nt(jnp.where(pick, key, zero), query)
                scores = scores + jnp.concatenate([col_ref[...]] * (tokens // LANES), axis=1)
                probs = jnp.exp(scores - lse_ref[half, pl.ds(i * 2 + head, 1), :])
                g_probs = nt(jnp.where(pick, value, zero), grad)
                row_delta = jnp.sum(delta[span], axis=0, keepdims=True)
                g_scores = (probs * (g_probs - row_delta)).astype(BF16)
                g_value.append(nn(probs.astype(BF16), grad))
                g_key.append(nn(g_scores, query))
                g_query.append(nn(key_t[span], g_scores))
            g_q = jnp.concatenate(g_query, axis=0).T.astype(BF16)
            g_v = jnp.where(lane, *g_value).astype(BF16)
            to = pl.multiple_of(place * LANES, LANES)
            gqkv_ref[half, :, pl.ds(to, LANES)] = g_q
            to_k = pl.ds(pl.multiple_of(wide + to, LANES), LANES)
            gqkv_ref[half, :, to_k] = jnp.where(lane, *g_key).astype(BF16)
            gqkv_ref[half, :, pl.ds(pl.multiple_of(2 * wide + to, LANES), LANES)] = g_v
            for row, grads in ((0, g_q), (1, g_v)):
                total = jnp.sum(grads.astype(F32).reshape(-1, 8, LANES), axis=0)
                place_to = pl.ds(pl.multiple_of(before + to, LANES), LANES)
                sums_ref[half, row, :, place_to] = total
            return carry

        lax.fori_loop(0, 2 * len(pairs), pair, 0)

    return call(
        kernel,
        (shaped((2, tokens, 3 * wide), BF16), shaped((2, 2, 8, before + wide), F32)),
        (g_att, att, qkv, lse, mask, *earlier),
        scratch=[pltpu.VMEM((tokens, LANES), F32)],
        flops=20 * tokens * tokens * wide * 2,
    )


def project_other(x_t, g_qkv, beside):
    width, tokens = x_t.shape
    columns = g_qkv.shape[2]
    extra = beside[1].shape[2] if beside else 0

    def kernel(xt_ref, g_ref, *refs):
        keep_ref, send_ref = refs[len(beside) :]
        span = slice(0, columns)
        made = nn(xt_ref[...], g_ref[1]).astype(BF16)
        split_rows(made, keep_ref.at[:, span], send_ref.at[:, span], True)
        if beside:
            span = slice(columns, columns + extra)
            made = nn(refs[0][...], refs[1][1]).astype(BF16)
            split_rows(made, keep_ref.at[:, span], send_ref.at[:, span], True)

    out = shaped((width // 2, columns + extra), BF16)
    return call(
        kernel,
        (out, out),
        (x_t, g_qkv, *beside),
        flops=2 * tokens * width * (columns + extra),
    )


def project_own(x_t, g_qkv, beside, small, keep_came, send_came):
    width, tokens = x_t.shape
    columns = g_qkv.shape[2]
    extra = beside[1].shape[2] if beside else 0
    tail = small[0].shape[1] if small else 0
    middle = width // 2
    count = len(beside) + len(small)

    def kernel(xt_ref, g_ref, kc_ref, sc_ref, *refs):
        keep_ref, send_ref = refs[count:]
        for out, came, first in ((keep_ref, kc_ref, 0), (send_ref, sc_ref, middle)):
            rows = slice(first, first + middle)
            span = slice(0, columns)
            made = nn(xt_ref[rows, :], g_ref[0])
            out[:, span] = (made + came[:, span].astype(F32)).astype(BF16)
            if beside:
                span = slice(columns, columns + extra)
                made = nn(refs[0][rows, :], refs[1][0])
                out[:, span] = (made + came[:, span].astype(F32)).astype(BF16)
            if small:
                total = refs[count - 2][rows, :].astype(F32) + refs[count - 1][rows, :].astype(F32)
                out[:, columns + extra :] = total.astype(BF16)

    out = shaped((middle, columns + extra + tail), BF16)
    return call(
        kernel,
        (out, out),
        (x_t, g_qkv, keep_came, send_came, *beside, *small),
        flops=2 * tokens * width * (columns + extra),
    )


def token_back(g_parts, start, perm, weights, cols):
    tokens, width = start.shape
    widths = [part.shape[2] // 3 for part in g_parts]

    def kernel(a_ref, b_ref, start_ref, perm_ref, w_ref, out_ref, g_ref, high_ref, rest_ref):
        for half in range(2):
            for kind in range(3):
                to = kind * cols
                for ref, wide in zip((a_ref, b_ref), widths):
                    taken = ref[half, :, kind * wide : (kind + 1) * wide]
                    g_ref[half, :, to : to + wide] = taken
                    to += wide
        used = slice(0, 3 * cols)

        def matmul(span):
            made = nt(g_ref[0], w_ref[0, span, used]) + nt(g_ref[1], w_ref[1, span, used])
            made = start_ref[:, span] + made
            high = made.astype(BF16)
            high_ref[:, span] = high
            rest_ref[:, span] = (made - high.astype(F32)).astype(BF16)

        columns_of(width, matmul)

        def reorder(span):
            turn = perm_ref[span, :]
            out_ref[:, span] = nt(high_ref[...], turn) + nt(rest_ref[...], turn)

        columns_of(width, reorder)

    return call(
        kernel,
        shaped((tokens, width), F32),
        (*g_parts, start, perm, weights),
        scratch=[
            pltpu.VMEM((2, tokens, 3 * cols), BF16),
            pltpu.VMEM((tokens, width), BF16),
            pltpu.VMEM((tokens, width), BF16),
        ],
        flops=16 * tokens * width * cols,
    )


class Exchange:
    def __init__(self, size):
        self.size = size
        self.depth = size.bit_length() - 1
        self.rank = lax.axis_index("dp")
        self.core = lax.axis_index("tensor")
        outer = list(range(self.depth - 1, 1, -1))
        self.bits = (outer + [1, 0], outer + [0, 1])

    def flip(self, value, *steps):
        pairs = []
        for i in range(self.size):
            for core in range(2):
                to = i
                for step in steps:
                    to ^= 1 << self.bits[core][step]
                pairs.append((i * 2 + core, to * 2 + core))
        return lax.ppermute(value, ("dp", "tensor"), pairs)

    def last_outer(self):
        low, high = self.depth - 4, self.depth - 3
        return (low,), (high,), (low, high)

    def flip_three(self, values):
        return [self.flip(value, *steps) for value, steps in zip(values, self.last_outer())]

    def blocks(self):
        tables = []
        for bits in self.bits:
            tables.append(
                [
                    sum(((j >> step) & 1) << bit for step, bit in enumerate(bits))
                    for j in range(self.size)
                ]
            )
        table = np.array(tables, np.int32)
        return jnp.where(self.core == 0, table[0], table[1]) ^ self.rank


def join(*parts):
    return jnp.concatenate(parts, axis=0)


def added(*values):
    total = values[0].astype(F32)
    for value in values[1:]:
        total = total + value.astype(F32)
    return total


def halves(value):
    middle = value.shape[0] // 2
    return value[:middle], value[middle:]


def three_parts(value):
    high = lax.reduce_precision(value, 8, 7)
    rest = value - high
    middle = lax.reduce_precision(rest, 8, 7)
    return (high.astype(BF16), middle.astype(BF16), (rest - middle).astype(BF16))


SMALL = 48
UP = 32


def pack(qkv_w, out_w, emb_w, gains, biases, up_bias):
    rows, cols = out_w.shape
    chunk = gains.shape[1]
    args = (qkv_w, out_w, emb_w, gains, biases, up_bias[None])

    def kernel(*refs):
        one_ref, refs, vec_ref, sems = refs[6], (*refs[:6], *refs[7:13]), refs[13], refs[14]
        copies = []
        for place in range(6):
            copies.append(pltpu.make_async_copy(refs[place], refs[6 + place], sems.at[place]))
        for copy in copies:
            copy.start()
        for copy in copies:
            copy.wait()
        q_ref, o_ref, e_ref, g_ref, b_ref, u_ref = refs[6:]
        for part in range(3):
            one_ref[:, part * cols : (part + 1) * cols] = q_ref[part]
        one_ref[:, 3 * cols : 4 * cols] = o_ref[...]
        vec_ref[...] = jnp.zeros_like(vec_ref)
        vec_ref[0:2, 0:chunk] = g_ref[...]
        vec_ref[2:8, 0:chunk] = b_ref[...]
        vec_ref[0:1, UP : UP + u_ref.shape[1]] = u_ref[...]
        value = vec_ref[...]
        high = value.astype(BF16).astype(F32)
        middle = (value - high).astype(BF16).astype(F32)
        block = [e_ref[...].astype(F32), high, middle, value - high - middle]
        one_ref[:, 4 * cols :] = jnp.concatenate(block, axis=0).astype(BF16)

    return call(
        kernel,
        shaped((rows, 4 * cols + LANES), BF16),
        args,
        in_specs=[pl.BlockSpec(memory_space=pltpu.HBM)] * 6,
        scratch=[pltpu.VMEM(arg.shape, arg.dtype) for arg in args]
        + [pltpu.VMEM((8, LANES), F32), pltpu.SemaphoreType.DMA((6,))],
        grant=60 * 1024 * 1024,
    )


def spreads(sides, width, hidden, chunk, up_chunk):
    lane = jnp.arange(LANES, dtype=jnp.int32)[:, None]
    column = jnp.arange(width, dtype=jnp.int32)[None]
    up_column = jnp.arange(hidden, dtype=jnp.int32)[None]
    thin, broad = [], []
    for side in sides:
        thin.append((lane < chunk) & (column % (2 * chunk) == side * chunk + lane))
        broad.append((lane >= UP) & (up_column % (2 * up_chunk) == side * up_chunk + lane - UP))
    return jnp.stack(thin).astype(BF16), jnp.stack(broad).astype(BF16)


def unpack(core, pieces, thin, broad, rel, absolute, up_rel, cols):
    width, hidden = thin.shape[2], broad.shape[2]
    count = width // SMALL

    def kernel(core_ref, thin_ref, broad_ref, rel_ref, abs_ref, up_ref, *refs):
        vec_ref, head_ref, side_ref, proj_ref, e_ref, sems = refs[8:]
        copies = load_weights(refs[:8], e_ref, sems, 4 * cols, 4 * cols + LANES)
        for copy in copies:
            copy.wait()
        first = core_ref[0] == 0
        blocks = [e_ref[side].astype(F32).reshape(count, SMALL, LANES) for side in range(2)]
        tops = [block[:, : SMALL // 2] for block in blocks]
        halves = [jnp.where(first, tops[0], tops[1]), jnp.where(first, tops[1], tops[0])]
        proj_ref[...] = jnp.concatenate(halves, axis=1).reshape(width, LANES).astype(BF16)
        flat = lax.broadcasted_iota(jnp.int32, (count, count * 8), 1)
        pick = flat == 8 * lax.broadcasted_iota(jnp.int32, (count, count * 8), 0)
        pick = pick.astype(F32).astype(BF16)
        vec = jnp.zeros((8, width), F32)
        plain = jnp.zeros((8, width), F32)
        wide = jnp.zeros((1, hidden), F32)
        index = lax.broadcasted_iota(jnp.int32, (count, hidden), 0)
        for side in range(2):
            placed, up_placed = None, None
            for part in (2, 1, 0):
                start = SMALL // 2 + 8 * part
                rows = blocks[side][:, start : start + 8].reshape(count * 8, LANES).astype(BF16)
                spread = nn(rows, thin_ref[side])
                up_spread = nn(nn(pick, rows).astype(BF16), broad_ref[side])
                placed = spread if placed is None else placed + spread
                up_placed = up_spread if up_placed is None else up_placed + up_spread
            for j in range(count):
                row = placed[8 * j : 8 * j + 8]
                vec = vec + jnp.where(rel_ref[...] == j, row, 0.0)
                plain = plain + jnp.where(abs_ref[...] == j, row, 0.0)
            chosen = jnp.where(up_ref[...] == index, up_placed, 0.0)
            wide = wide + jnp.sum(chosen, axis=0, keepdims=True)
        vec_ref[...] = vec
        for side in range(2):
            low_half = first if side == 0 else jnp.logical_not(first)
            part = jnp.where(low_half, plain[:, :cols], plain[:, cols:])
            head_ref[side : side + 1, :cols] = part[2:3]
            head_ref[side : side + 1, cols : 2 * cols] = jnp.zeros((1, cols), F32)
            head_ref[side : side + 1, 2 * cols :] = part[3:4]
            middle = hidden // 2
            side_ref[side : side + 1, :] = jnp.where(low_half, wide[:, :middle], wide[:, middle:])

    outs = (
        shaped((8, width), F32),
        shaped((2, 3 * cols), F32),
        shaped((2, hidden // 2), F32),
        shaped((width, LANES), BF16),
    )
    return call(
        kernel,
        outs,
        (core[None], thin, broad, rel, absolute, up_rel, *pieces),
        in_specs=[pl.BlockSpec(memory_space=pltpu.SMEM)] + [WHOLE] * 5 + [ANY] * 8,
        scratch=[pltpu.VMEM((2, width, LANES), BF16), pltpu.SemaphoreType.DMA((2, 4))],
    )


def pack_grads(
    core, thin, broad, rel, absolute, up_rel, sums, up_sums, head_sums, proj_grad,
):
    width, hidden = thin.shape[2], broad.shape[2]
    count = width // SMALL

    def kernel(
        core_ref, thin_ref, broad_ref, rel_ref, abs_ref, up_ref, sums_ref, ups_ref, heads_ref,
        pg_ref, own_ref, other_ref,
    ):
        first = core_ref[0] == 0
        fold = lambda v: jnp.sum(v, axis=0, keepdims=True)

        def ordered(own, other):
            low, high = jnp.where(first, own, other), jnp.where(first, other, own)
            return jnp.concatenate([low, high], axis=1)

        def heads(half, kind):
            return fold(heads_ref[half, kind])

        rows = [
            fold(sums_ref[0:8]),
            fold(sums_ref[24:32]),
            ordered(heads(0, 0), heads(1, 0)),
            ordered(heads(0, 1), heads(1, 1)),
            fold(sums_ref[16:24]),
            fold(sums_ref[8:16]),
            fold(sums_ref[40:48]),
            fold(sums_ref[32:40]),
        ]
        grads = jnp.concatenate(rows, axis=0)
        row = lax.broadcasted_iota(jnp.int32, (8, width), 0)
        block = jnp.where((row == 2) | (row == 3), abs_ref[...], rel_ref[...])
        spread = [jnp.where(block == j, grads, 0.0) for j in range(count)]
        spread = jnp.concatenate(spread, axis=0)
        high = spread.astype(BF16)
        rest = (spread - high.astype(F32)).astype(BF16)
        up = ordered(fold(ups_ref[0:8]), fold(ups_ref[8:16]))
        index = lax.broadcasted_iota(jnp.int32, (count, hidden), 0)
        up = jnp.where(up_ref[...] == index, up, 0.0)
        up_high = up.astype(BF16)
        up_rest = (up - up_high.astype(F32)).astype(BF16)
        flat = lax.broadcasted_iota(jnp.int32, (count * 8, count), 0)
        put = flat == 8 * lax.broadcasted_iota(jnp.int32, (count * 8, count), 1)
        put = put.astype(F32).astype(BF16)
        tops = pg_ref[...].reshape(count, SMALL, LANES)
        for side, out_ref in enumerate((own_ref, other_ref)):
            low_half = first if side == 0 else jnp.logical_not(first)
            top = jnp.where(low_half, tops[:, : SMALL // 2], tops[:, SMALL // 2 :])
            thin_part = nt(high, thin_ref[side]) + nt(rest, thin_ref[side])
            up_part = nt(up_high, broad_ref[side]) + nt(up_rest, broad_ref[side])
            vec = (thin_part + nn(put, up_part.astype(BF16))).reshape(count, 8, LANES)
            blank = jnp.zeros((count, SMALL // 2 - 8, LANES), F32)
            made = jnp.concatenate([top, vec, blank], axis=1).reshape(width, LANES).astype(BF16)
            quarter = width // 4
            for place in range(4):
                source = OTHER[place] if side == 1 else place
                out_ref[place * quarter : (place + 1) * quarter, :] = made[
                    source * quarter : (source + 1) * quarter
                ]

    out = shaped((width, LANES), BF16)
    return call(
        kernel,
        (out, out),
        (
            core[None], thin, broad, rel, absolute, up_rel, sums, up_sums, head_sums, proj_grad,
        ),
        in_specs=[pl.BlockSpec(memory_space=pltpu.SMEM)] + [WHOLE] * 9,
    )


def finish(kept, came, a_wide, cols, chunk, up_chunk, emb_shape):
    rows = kept.shape[0]
    b_wide = cols - a_wide
    beside = 3 * a_wide
    second = beside + cols

    def kernel(kept_ref, *refs):
        qkv_ref, out_ref, emb_ref, gain_ref, bias_ref, up_ref, sum_ref = refs[len(came) :]
        total = kept_ref[...]
        for ref in refs[: len(came)]:
            total = total + ref[...].astype(F32)
        sum_ref[...] = total
        for part in range(3):
            qkv_ref[part, :, :a_wide] = sum_ref[:, part * a_wide : (part + 1) * a_wide]
            start = second + part * b_wide
            qkv_ref[part, :, a_wide:] = sum_ref[:, start : start + b_wide]
        out_ref[...] = sum_ref[:, beside:second]
        first = second + 3 * b_wide
        half = SMALL // 2
        emb_ref[...] = sum_ref[0:half, first:]
        gain_ref[...] = sum_ref[half : half + 2, first : first + chunk]
        bias_ref[...] = sum_ref[half + 2 : half + 8, first : first + chunk]
        up_ref[...] = sum_ref[half : half + 1, first + UP : first + UP + up_chunk]

    outs = (
        shaped((3, rows, cols), F32),
        shaped((rows, cols), F32),
        shaped(emb_shape, F32),
        shaped((2, chunk), F32),
        shaped((6, chunk), F32),
        shaped((1, up_chunk), F32),
    )
    return call(kernel, outs, (kept, *came), scratch=[pltpu.VMEM(kept.shape, F32)])


def pack_plain(qkv_w, out_w, emb_w, gains, biases, up_bias):
    rows = out_w.shape[0]
    vector = jnp.concatenate([gains.reshape(-1), biases.reshape(-1), up_bias])
    pad_to = -(-vector.size // LANES) * LANES
    padded = jnp.pad(vector, (0, pad_to - vector.size))
    flat = jnp.concatenate([emb_w.reshape(-1), *three_parts(padded)])
    extra = -(-flat.size // (rows * LANES)) * LANES
    flat = jnp.pad(flat, (0, rows * extra - flat.size)).reshape(rows, extra)
    one = jnp.concatenate([qkv_w[0], qkv_w[1], qkv_w[2], out_w, flat], axis=1)
    sizes = (rows, extra, emb_w.size, gains.shape[1], up_bias.size, pad_to)
    return one, sizes


def unpack_plain(core, sides, pieces, blocks, sizes):
    rows, extra, emb_size, chunk, up_chunk, pad_to = sizes
    size = blocks.shape[0]
    width = size * rows
    cols = width // 2
    ff_local = size * up_chunk
    pieces = [part[:, 4 * cols :] for part in pieces]
    own = jnp.concatenate(pieces[:4])
    other = jnp.concatenate([pieces[4 + place] for place in OTHER])
    small = [part.reshape(size, rows * extra) for part in (own, other)]
    small = jnp.where(core == 0, jnp.stack(small, 1), jnp.stack(small[::-1], 1))
    proj = small[:, :, :emb_size].reshape(width, -1)
    thirds = small[:, :, emb_size : emb_size + 3 * pad_to].astype(F32)
    thirds = thirds.reshape(size, 2, 3, pad_to)
    vectors = thirds[:, :, 0] + (thirds[:, :, 1] + thirds[:, :, 2])
    plain = vectors[jnp.argsort(blocks)].reshape(size * 2, pad_to)
    vectors = vectors.reshape(size * 2, pad_to)
    vec = jnp.moveaxis(vectors[:, : 8 * chunk].reshape(-1, 8, chunk), 1, 0).reshape(8, width)
    query_bias = plain[:, 2 * chunk : 3 * chunk].reshape(-1)
    value_bias = plain[:, 3 * chunk : 4 * chunk].reshape(-1)
    up_bias = plain[:, 8 * chunk : 8 * chunk + up_chunk].reshape(-1)
    head_bias, side_bias = [], []
    for side in sides:
        query_part = lax.dynamic_slice_in_dim(query_bias, side * cols, cols)
        value_part = lax.dynamic_slice_in_dim(value_bias, side * cols, cols)
        head_bias.append(jnp.concatenate([query_part, jnp.zeros_like(query_part), value_part]))
        side_bias.append(lax.dynamic_slice_in_dim(up_bias, side * ff_local, ff_local))
    return vec, jnp.stack(head_bias), jnp.stack(side_bias), proj


def pack_grads_plain(
    core, blocks, sizes, sums, up_sums, head_sums, proj_grad
):
    rows, extra, emb_size, chunk, up_chunk, pad_to = sizes
    size = blocks.shape[0]

    def fold(value):
        return jnp.sum(value.reshape(-1, 8, value.shape[-1]), axis=1)

    def absolute(own, other):
        return jnp.where(
            core == 0, jnp.concatenate([own, other]), jnp.concatenate([other, own])
        )

    def relative(value):
        return value.reshape(size, 2, -1)[blocks]

    gain_one, shift_one, out_bias, gain_two, shift_two, ffn_bias = (
        row.reshape(size, 2, chunk) for row in fold(sums)
    )
    own, other = jnp.sum(head_sums, axis=2)
    small = jnp.concatenate(
        [
            proj_grad.reshape(size, 2, emb_size),
            gain_one,
            gain_two,
            relative(absolute(own[0], other[0])),
            relative(absolute(own[1], other[1])),
            out_bias,
            shift_one,
            ffn_bias,
            shift_two,
            relative(absolute(*fold(up_sums))),
        ],
        axis=2,
    ).astype(BF16)
    small = jnp.pad(small, ((0, 0), (0, 0), (0, rows * extra - small.shape[2])))
    small = jnp.where(core == 0, small, small[:, ::-1])
    own, other = jnp.moveaxis(small, 1, 0).reshape(2, size * rows, extra)
    first, second, third, fourth = jnp.split(other, 4)
    return own, jnp.concatenate([first, third, second, fourth])


def body(
    tokens,
    lengths,
    key_mask,
    order,
    query_key_value_weight,
    output_projection_weight,
    up_projection_weight,
    down_projection_weight,
    embedding_projection_weight,
    gains,
    biases,
    up_bias_vector,
    cotangent,
):
    size = lax.axis_size("dp")
    core = lax.axis_index("tensor")
    ways = Exchange(size)
    depth = ways.depth
    half_len = tokens.shape[1]
    full_len = key_mask.shape[1]
    width = tokens.shape[2]
    cols = output_projection_weight.shape[0]
    rows = output_projection_weight.shape[1]
    ff_local = up_projection_weight.shape[1]
    chunk = gains.shape[1]
    emb_size = embedding_projection_weight.size
    sides = (core, 1 - core)

    fast = rows == SMALL and emb_size == SMALL // 2 * LANES and up_bias_vector.size <= LANES - UP
    small_args = (
        query_key_value_weight,
        output_projection_weight.T,
        embedding_projection_weight,
        gains,
        biases,
        up_bias_vector,
    )
    if fast:
        one = pack(*small_args)
    else:
        one, small_sizes = pack_plain(*small_args)

    wide = 4 * cols
    seconds, lasts = depth - 2, depth - 1
    for step in range(depth - 4):
        one = join(one, ways.flip(one, step))
    tokens, order, lengths, key_mask = after((tokens, order, lengths, key_mask), one)
    mine = order[0, core]
    theirs = order[0, 1 - core]
    my_half = lax.dynamic_index_in_dim(tokens, mine, 0, keepdims=False)
    their_half = lax.dynamic_index_in_dim(tokens, theirs, 0, keepdims=False)
    blocks = ways.blocks()
    one_came = ways.flip_three([one] * 3)
    if fast:
        thin, broad = spreads(sides, width, 2 * ff_local, chunk, up_bias_vector.size)
        places_of = jnp.argsort(blocks)
        rel = (jnp.arange(width, dtype=jnp.int32) // rows)[None]
        absolute = jnp.repeat(places_of, rows)[None].astype(jnp.int32)
        up_rel = jnp.repeat(places_of, 2 * up_bias_vector.size)[None].astype(jnp.int32)
        *one_came, thin, broad, rel, absolute, up_rel = together(
            *one_came, thin, broad, rel, absolute, up_rel
        )
        tables = (core, thin, broad, rel, absolute, up_rel)

    def in_order(own, other):
        return jnp.where(
            core == 0, jnp.concatenate([own, other]), jnp.concatenate([other, own])
        )

    def half_of(value, which):
        return lax.dynamic_slice_in_dim(value, which * half_len, half_len)

    seq_len = lengths[mine]
    marks = lax.dynamic_index_in_dim(key_mask, mine, 0, keepdims=False)
    places = jnp.arange(full_len, dtype=jnp.int32)
    key_ok = (places < seq_len) & ((marks == 1) | (places == 0))
    mask = jnp.where(key_ok, 0.0, -1e30).astype(F32)[None, :]
    where = (blocks[:, None] * rows + jnp.arange(rows, dtype=jnp.int32)[None]).reshape(-1)
    perm = (jnp.arange(width, dtype=jnp.int32)[:, None] == where[None]).astype(BF16)
    two, three = after((up_projection_weight, down_projection_weight.T), order)
    for step in range(depth - 4):
        two = join(two, ways.flip(two, step))
        three = join(three, ways.flip(three, step))
    one = join(one, *one_came)
    here = in_order(my_half, swap_cores(after(their_half, one)))
    two_came = ways.flip_three([after(two, one)] * 3)
    one_b, one_c, here, mask, perm, *two_came = together(
        ways.flip(one, seconds), ways.flip(one, lasts), here, mask, perm, *two_came
    )
    two = join(two, *two_came)
    one_other = together(swap_cores(one), swap_cores(one_b), swap_cores(one_c))
    three_came = ways.flip_three([after(three, two, *one_other)] * 3)
    one_d, two_b, *three_came = together(
        ways.flip(one_b, lasts), ways.flip(two, seconds), *three_came
    )
    three = join(three, *three_came)
    two_both = join(two, two_b)
    one_pieces = (one, one_b, one_c, one_d, *one_other, swap_cores(one_d))
    two_more, three_b = ways.flip(two_both, lasts), ways.flip(three, seconds)
    one_pieces = together(*one_pieces, two_both, three)[:8]
    if fast:
        vec, head_bias, side_bias, proj = unpack(core, one_pieces, *tables[1:], cols)
    else:
        vec, head_bias, side_bias, proj = unpack_plain(
            core, sides, one_pieces, blocks, small_sizes
        )
    side_bias = (side_bias[0:1], side_bias[1:2])

    qkv, lse, att, res_one, first, first_low, first_low_t, here_t, weights = attention_forward(
        here, perm, head_bias, mask, vec, one_pieces, cols
    )
    two_more, three_b = after((two_more, three_b), first_low)
    three_both = join(three, three_b)
    three_more = ways.flip(three_both, lasts)
    two_other = [swap_cores(part) for part in (two_both, two_more)]

    def quarters(both, more):
        return ((both, 0), (both, 1), (more, 0), (more, 1))

    two_own = (two_both, two_more)
    hid_own, slope_own = up_forward(
        after(first_low, three_both, two_more), quarters(*two_own), side_bias[0], False
    )
    two_other = after(two_other, hid_own)
    three_both_other = swap_cores(three_both)
    cot_mine = lax.dynamic_index_in_dim(cotangent, core, 0, keepdims=False)
    cot_other = lax.dynamic_index_in_dim(cotangent, 1 - core, 0, keepdims=False)
    cot = in_order(cot_mine, after(swap_cores(after(cot_other, first_low)), hid_own))
    hid_other, slope_other = up_forward(after(first_low, cot), quarters(*two_other), side_bias[1], True)
    three_more, three_both_other = after((three_more, three_both_other), hid_other)
    three_more_other = swap_cores(three_more)
    three_own = (three_both, three_more)
    three_other = (three_both_other, three_more_other)
    emb, g_ffn, g_ffn_t, g_res_two, proj_grad, sums_two = down_both(
        seq_len[None],
        (hid_own, hid_other),
        (three_both, three_more, three_both_other, three_more_other),
        first,
        vec,
        proj,
        cot,
    )

    def low(*values):
        return added(*values).astype(BF16)

    def spread(value):
        kept, sent = halves(value)
        return kept, sent.astype(BF16)

    def quarter_out(value):
        kept, *sent = jnp.split(value, 4)
        return kept, [part.astype(BF16) for part in sent]

    dk_other, ds_other = down_grad(g_ffn_t, hid_other, True)
    ds_came, dk_came = swap_cores(ds_other), swap_cores(dk_other)
    dk, ds = down_grad(g_ffn_t, after(hid_own, ds_other), False)
    ds_came = after(ds_came, ds)
    d_high = low(halves(ds)[1], halves(ds_came)[1])
    d_low = low(halves(ds)[0], halves(ds_came)[0])
    d_came_high = ways.flip(d_high, lasts)
    uk_other, us_other, up_bias_other, part = up_grad(
        after(g_ffn, d_high, d_low),
        first_low_t,
        slope_other,
        three_other,
        two_other,
        g_res_two,
        True,
        (),
    )
    us_came, uk_came = swap_cores(us_other), swap_cores(uk_other)
    d_came_high, dk_came, d_low = after((d_came_high, dk_came, d_low), us_other)
    d_came_low = ways.flip(d_low, lasts)
    uk, us, up_bias, g_first = up_grad(
        after(g_ffn, us_other, d_came_high),
        first_low_t,
        slope_own,
        three_own,
        two_own,
        part,
        False,
        (up_bias_other,),
    )
    d_came_low, us_came, uk_came = after((d_came_low, us_came, uk_came), us)
    u_sent = low(us, us_came)
    u_came = ways.flip(u_sent, lasts)
    d_sent = low(halves(dk)[1], halves(dk_came)[1], d_came_high)
    d_held = added(halves(dk)[0], halves(dk_came)[0], d_came_low)
    d_came = ways.flip(d_sent, seconds)
    g_res_one, g_branch_t, g_att, sums = norm_back(
        after(g_first, u_sent, d_sent), res_one, vec, weights, sums_two, cols
    )
    pairs = list(range(cols // LANES))
    split = (len(pairs) + 1) // 2
    g_a, bias_a = attention_back(pairs[:split], g_att, att, qkv, lse, mask)
    beside = (g_branch_t, att)
    ak_other, as_other = project_other(here_t, g_a, beside)
    as_came, ak_came = swap_cores(as_other), swap_cores(ak_other)
    g_b, head_sums = attention_back(
        pairs[split:], after(g_att, as_other), att, qkv, lse, mask, (bias_a,)
    )
    as_came, ak_came = after((as_came, ak_came), g_b)
    a_keep, a_send = project_own(here_t, g_a, beside, (), ak_came, as_came)
    u_came = after(u_came, a_send)
    a_came = ways.flip(a_send, lasts)
    u_sent = low(halves(uk)[1], halves(uk_came)[1], halves(u_came)[1])
    u_held = added(halves(uk)[0], halves(uk_came)[0], halves(u_came)[0])
    u_came = ways.flip(u_sent, seconds)
    bk_other, bs_other = project_other(here_t, after(g_b, a_send, u_sent), ())
    bs_came, bk_came = swap_cores(bs_other), swap_cores(bk_other)
    d_came = after(d_came, bs_other)
    d_held, d_sent = quarter_out(d_held + d_came.astype(F32))
    d_came = ways.flip_three(d_sent)
    if fast:
        small_own, small_other = pack_grads(
            *tables, after(sums, bs_other, *d_sent), up_bias, head_sums, proj_grad
        )
    else:
        small_own, small_other = pack_grads_plain(
            core, blocks, small_sizes, sums, up_bias, head_sums, proj_grad
        )
    small_came = swap_cores(small_other)
    bs_came, bk_came = after((bs_came, bk_came), small_other)
    b_keep, b_send = project_own(here_t, g_b, (), (small_own, small_came), bk_came, bs_came)
    u_came, a_came = after((u_came, a_came), b_send)
    b_came = ways.flip(b_send, lasts)
    a_sent = low(halves(a_keep)[1], halves(a_came)[1])
    a_held = added(halves(a_keep)[0], halves(a_came)[0])
    a_came = ways.flip(a_sent, seconds)
    u_held, u_sent = quarter_out(after(u_held, a_sent) + u_came.astype(F32))
    u_came = ways.flip_three(u_sent)
    b_came = after(b_came, *u_sent)
    b_sent = low(halves(b_keep)[1], halves(b_came)[1])
    b_held = added(halves(b_keep)[0], halves(b_came)[0])
    b_came = ways.flip(b_sent, seconds)
    g_here = token_back(
        (after(g_a, b_send, a_sent, b_sent, *u_sent, *d_came), g_b), g_res_one, perm, weights, cols
    )
    a_came, b_came, u_came, emb = after((a_came, b_came, u_came, emb), g_here)
    held = jnp.concatenate([a_held + a_came.astype(F32), b_held + b_came.astype(F32)], axis=1)
    held, sent = quarter_out(held)
    came = ways.flip_three(sent)
    d_came, u_came, u_held = after((d_came, u_came, u_held), *sent)
    d_held, u_held = added(d_held, *d_came), added(u_held, *u_came)
    for step in range(depth - 5, -1, -1):
        held, sent = spread(added(held, *came))
        came = [ways.flip(sent, step)]
        d_held, sent = spread(d_held)
        d_held = d_held + ways.flip(sent, step).astype(F32)
        u_held, sent = spread(u_held)
        u_held = u_held + ways.flip(sent, step).astype(F32)
    down_shard, up_shard = d_held, u_held
    a_wide, b_wide = split * LANES, (len(pairs) - split) * LANES
    if fast:
        qkv_shard, out_shard, emb_shard, gain_shard, bias_shard, up_bias_shard = finish(
            held, came, a_wide, cols, chunk, up_bias_vector.size, embedding_projection_weight.shape
        )
        out_shard, up_bias_shard = out_shard.T, up_bias_shard[0]
    else:
        shard = added(held, *came)
        a_shard, b_shard = shard[:, : 3 * a_wide + cols], shard[:, 3 * a_wide + cols :]
        qkv_shard = jnp.stack(
            [
                jnp.concatenate(
                    [
                        a_shard[:, i * a_wide : (i + 1) * a_wide],
                        b_shard[:, i * b_wide : (i + 1) * b_wide],
                    ],
                    axis=1,
                )
                for i in range(3)
            ]
        )
        out_shard = a_shard[:, 3 * a_wide :].T
        tail = b_shard[:, 3 * b_wide :].reshape(-1)
        emb_shard = tail[:emb_size].reshape(embedding_projection_weight.shape)
        tail = tail[emb_size:]
        gain_shard = tail[: 2 * chunk].reshape(2, chunk)
        bias_shard = tail[2 * chunk : 8 * chunk].reshape(6, chunk)
        up_bias_shard = tail[8 * chunk : 8 * chunk + up_bias_vector.size]

    def give_back(value, places_of):
        own = half_of(value, core)
        other = swap_cores(half_of(value, 1 - core))
        blank = jnp.zeros((2,) + own.shape, value.dtype)
        blank = lax.dynamic_update_slice(blank, own[None], (places_of[0], 0, 0))
        return lax.dynamic_update_slice(blank, other[None], (places_of[1], 0, 0))

    embeddings = give_back(emb, (core, 1 - core))
    grad_tokens = give_back(g_here, (mine, theirs))
    return (
        embeddings,
        grad_tokens,
        qkv_shard,
        out_shard,
        up_shard,
        down_shard.T,
        emb_shard,
        gain_shard,
        bias_shard,
        up_bias_shard,
    )


def solution(mesh):
    return jax.shard_map(
        body,
        mesh=mesh,
        in_specs=(
            P("dp", "tensor", None),
            P("dp"),
            P("dp", None),
            P("dp", None),
            P(None, "dp", "tensor"),
            P("tensor", "dp"),
            P("dp", "tensor"),
            P("tensor", "dp"),
            P(("dp", "tensor"), None),
            P(None, ("dp", "tensor")),
            P(None, ("dp", "tensor")),
            P(("dp", "tensor")),
            P("dp", "tensor", None),
        ),
        out_specs=(
            P("dp", "tensor", None),
            P("dp", "tensor", None),
            P(None, "dp", "tensor"),
            P("tensor", "dp"),
            P("dp", "tensor"),
            P("tensor", "dp"),
            P(("dp", "tensor"), None),
            P(None, ("dp", "tensor")),
            P(None, ("dp", "tensor")),
            P(("dp", "tensor")),
        ),
        check_vma=False,
    )
```
